256 devices in a mesh: elem: 8 (over z), tm: 32 (over y, x, core).
Axes of the slice: x: 4, y: 4, z: 8, core: 2. Of those that a mesh axis runs over, the one named last changes fastest.
Arguments:
- samples: bfloat16 [24576, 2048], P('tm', 'elem'), may hold values from -160 to 160
- taps_weight: bfloat16 [16, 2048, 512], P(None, 'elem'), may hold values from -0.046875 to 0.046875
- retain: float32 [24576], P('tm')
Outputs:
- whitened: float32 [512, 24576], P('elem', 'tm')
The draws below stay inside these ranges and needn't reach their ends.
All inputs are finite; a program needn't handle non-finite values.
Results may differ from the reference program's by a relative error of at most 0.0003.
Values may be sent and summed in bfloat16 or wider, within the bound.
No kernel may reach another device: no remote copies, remote signals or barrier semaphores. Data moves between devices by JAX's collectives and lax.ppermute only.
A program may use at most 192 MiB of HBM per device.

```python
import jax
import jax.numpy as jnp
from jax import lax

ELEMENTS = 2048
BEAMS = 512
TAPS = 16
TM_DEV = 768
SAMPLES = 24576
N_TM = 32


def draw_samples(key, part):
    keys = jax.random.split(jax.random.fold_in(key, 11), 6)
    power_matrix = jnp.arange(SAMPLES, dtype=jnp.int32)[:, None]
    envelope = jnp.exp(jnp.log(3.0) * power_matrix.astype(jnp.float32) / SAMPLES)
    noise = jnp.clip(jax.random.normal(keys[0], (SAMPLES, ELEMENTS), jnp.float32), -5.0, 5.0)
    element_gain = jnp.exp(jax.random.uniform(keys[1], (1, ELEMENTS), jnp.float32, jnp.log(0.5), jnp.log(2.0)))
    sources = jnp.clip(jax.random.normal(keys[2], (SAMPLES, 4), jnp.float32), -5.0, 5.0)
    steering = jnp.clip(jax.random.normal(keys[3], (4, ELEMENTS), jnp.float32), -3.0, 3.0)
    onsets = jax.random.randint(keys[4], (4,), 0, SAMPLES)
    spans = jax.random.randint(keys[5], (4,), SAMPLES // 8, SAMPLES // 2)
    active = jnp.logical_and(power_matrix >= onsets[None, :], power_matrix < onsets[None, :] + spans[None, :]).astype(jnp.float32)
    result = noise * element_gain * envelope
    for emitter_number in range(4):
        result = result + (2.0 * active[:, emitter_number] * sources[:, emitter_number])[:, None] * steering[emitter_number][None, :]
    return result.astype(jnp.bfloat16)


def draw_retain(key, part):
    keys = jax.random.split(jax.random.fold_in(key, 23), 2)
    spread = jax.random.uniform(keys[0], (SAMPLES,), jnp.float32, 0.2, 1.8)
    retained_readings = jnp.exp(-spread / SAMPLES)
    receiver_locations = jax.random.randint(keys[1], (3,), 0, SAMPLES)
    power_matrix = jnp.arange(SAMPLES, dtype=jnp.int32)
    pulse_clusters = jnp.sum((power_matrix[:, None] == receiver_locations[None, :]).astype(jnp.int32), axis=1) > 0
    return jnp.where(pulse_clusters, 0.7, retained_readings).astype(jnp.float32)


def strengthened(drawn, key, source, target, shards_of, factor):
    def block_of(axis_at):
        return (jnp.arange(drawn.shape[axis_at]) // (drawn.shape[axis_at] // shards_of)).reshape((-1,) + (1,) * (drawn.ndim - 1 - axis_at))

    near = jax.random.permutation(key, shards_of)[block_of(target)]
    far = (block_of(target) + shards_of // 2) % shards_of
    return jnp.where((block_of(source) == near) | (block_of(source) == far), factor * drawn, drawn)


def block_levels(rng, shape, pieces, least, high):
    def one(position, shards_of):
        heights = jax.random.uniform(jax.random.fold_in(jax.random.fold_in(rng, 6), position), (shards_of,), jnp.float32, least / len(pieces), high / len(pieces))
        return jnp.repeat(jnp.exp(heights), shape[position] // shards_of).reshape((-1,) + (1,) * (len(shape) - position - 1))

    factor_of = one(*pieces[0])
    for cut in pieces[1:]:
        factor_of = factor_of * one(*cut)
    return factor_of


def gaussian_with(key, extent, scale, most, pieces, heavy, kind=jnp.bfloat16):
    values = scale * jax.random.normal(key, extent, jnp.float32)
    if pieces:
        values = values * block_levels(key, extent, pieces, -0.22, 0.18)
    return jnp.clip(strengthened(values, jax.random.fold_in(key, 3), *heavy), -most, most).astype(kind)


def setup_inputs(seed: int = 0) -> dict:
    seeds = jax.random.split(jax.random.key(seed), 4)
    samples = draw_samples(jax.random.fold_in(seeds[3], 71), 0)
    taps_weight = gaussian_with(seeds[1], (TAPS, ELEMENTS, BEAMS), (TAPS * ELEMENTS) ** -0.5, 0.046875, ((1, 8),), (1, 2, 8, 2.0))
    retain = draw_retain(jax.random.fold_in(seeds[3], 71), 0)
    return {"samples": samples, "taps_weight": taps_weight, "retain": retain}


loading_level = 0.1

def reference(samples, taps_weight, retain):
    filters = taps_weight.astype(jnp.float32).reshape(TAPS * ELEMENTS, BEAMS)
    padded = jnp.concatenate([jnp.zeros((TAPS - 1, ELEMENTS), jnp.float32), samples.astype(jnp.float32)], 0)
    unit_matrix = jnp.eye(BEAMS, dtype=jnp.float32)

    def advance(carry, block_index):
        gram_sum, count_sum = carry
        first_row = block_index * TM_DEV
        window_rows = lax.dynamic_slice_in_dim(padded, first_row, TM_DEV + TAPS - 1, 0)
        windowed = jnp.concatenate([window_rows[TAPS - 1 - filter_tap_index:TAPS - 1 - filter_tap_index + TM_DEV] for filter_tap_index in range(TAPS)], 1)
        beam_rows = jnp.dot(windowed, filters, precision=lax.Precision.HIGHEST)
        log_retain = jnp.log(lax.dynamic_slice_in_dim(retain, first_row, TM_DEV, 0))
        log_total = jnp.sum(log_retain)
        row_weight = jnp.exp(log_total - jnp.cumsum(log_retain))
        factor = jnp.exp(log_total)
        gram_block = jnp.dot((beam_rows * row_weight[:, None]).T, beam_rows, precision=lax.Precision.HIGHEST)
        gram_sum = factor * gram_sum + gram_block
        count_sum = factor * count_sum + jnp.sum(row_weight)
        covariance_estimate = gram_sum / count_sum + loading_level * unit_matrix
        lower_factor = jnp.linalg.cholesky(covariance_estimate)
        inverse_lower = jax.scipy.linalg.solve_triangular(lower_factor, unit_matrix, lower=True)
        whitened_block = lax.dot_general(inverse_lower, beam_rows, (((1,), (1,)), ((), ())), precision=lax.Precision.HIGHEST)
        return ((gram_sum, count_sum), whitened_block)
    initial = (jnp.zeros((BEAMS, BEAMS), jnp.float32), jnp.zeros((), jnp.float32))
    final_state, blocks = lax.scan(advance, initial, jnp.arange(N_TM, dtype=jnp.int32))
    return jnp.transpose(blocks, (1, 0, 2)).reshape(BEAMS, SAMPLES)
```

```python
import jax
import jax.numpy as jnp
from jax import lax
from jax.experimental import pallas as pl
from jax.experimental.pallas import tpu as pltpu
from jax.sharding import PartitionSpec as P

loading_level = 0.1
HI = lax.Precision.HIGHEST
TILE = 128
VMEM = pl.BlockSpec(memory_space=pltpu.VMEM)
SMEM = pl.BlockSpec(memory_space=pltpu.SMEM)


def shifted(array, axis, by):
    size = lax.axis_size(axis)
    pairs = [(i, i + by) for i in range(size) if 0 <= i + by < size]
    return lax.ppermute(array, axis, pairs)


def fir_body(halo_ref, x_ref, w_ref, o_ref, ext_ref):
    taps, width, beams = w_ref.shape
    rows = x_ref.shape[0]
    lead = halo_ref.shape[0]
    ext_ref[:lead, :] = halo_ref[...].astype(jnp.float32)
    ext_ref[lead:, :] = x_ref[...].astype(jnp.float32)
    step = 256
    for m in range(0, rows, step):
        window = jnp.concatenate(
            [
                ext_ref[lead - k + m : lead - k + m + step, :].astype(jnp.bfloat16)
                for k in range(taps)
            ],
            1,
        )
        o_ref[m : m + step, :] = jnp.dot(
            window, w_ref[...].reshape(taps * width, beams), preferred_element_type=jnp.float32
        )


def fir(halo, samples, taps_weight):
    rows, width = samples.shape
    taps, _, beams = taps_weight.shape
    return pl.pallas_call(
        fir_body,
        out_shape=jax.ShapeDtypeStruct((rows, beams), jnp.float32),
        in_specs=[VMEM] * 3,
        out_specs=VMEM,
        scratch_shapes=[pltpu.VMEM((rows + halo.shape[0], width), jnp.float32)],
        compiler_params=pltpu.CompilerParams(vmem_limit_bytes=40 << 20),
        cost_estimate=pl.CostEstimate(
            flops=2 * rows * taps * width * beams, bytes_accessed=6 << 20, transcendentals=0
        ),
        name="fir",
    )(halo, samples, taps_weight)


def gram_body(b_ref, weight_ref, o_ref):
    beams = b_ref.shape[1]
    weighted = b_ref[...] * weight_ref[...]
    at = 0
    for r in range(0, beams, TILE):
        part = lax.dot_general(
            weighted[:, r : r + TILE],
            b_ref[:, r:],
            (((0,), (0,)), ((), ())),
            precision=HI,
            preferred_element_type=jnp.float32,
        )
        for c in range(0, beams - r, TILE):
            o_ref[at : at + TILE, :] = part[:, c : c + TILE]
            at += TILE


def packed_gram(beam_rows, weight):
    beams = beam_rows.shape[1]
    n = beams // TILE
    return pl.pallas_call(
        gram_body,
        out_shape=jax.ShapeDtypeStruct((n * (n + 1) // 2 * TILE, TILE), jnp.float32),
        in_specs=[VMEM] * 2,
        out_specs=VMEM,
        name="packed_gram",
    )(beam_rows, weight)


def share_body(stats_ref, p_ref, o_ref):
    groups, rows, _ = p_ref.shape
    ways = o_ref.shape[0]
    total = p_ref[0]
    for g in range(1, groups):
        total = total + p_ref[g]
    tiles = rows // ways
    for s in range(tiles):
        o_ref[:, s * TILE : (s + 1) * TILE] = total[s * ways : (s + 1) * ways, :]
    lane = lax.broadcasted_iota(jnp.int32, (ways, TILE), 1)
    o_ref[:, tiles * TILE :] = jnp.where(lane == 0, stats_ref[0], stats_ref[1])


def spread_share(parts, log_total, mass, ways):
    groups, rows, _ = parts.shape
    return pl.pallas_call(
        share_body,
        out_shape=jax.ShapeDtypeStruct((ways, (rows // ways + 1) * TILE), jnp.float32),
        in_specs=[SMEM, VMEM],
        out_specs=VMEM,
        name="spread_share",
    )(jnp.stack([log_total, mass]), parts)


def decay_body(r_ref, o_ref):
    n, wide = r_ref.shape
    stats = r_ref[:, wide - TILE :]
    logs = stats[:, 0:1]
    row = lax.broadcasted_iota(jnp.int32, (n, n), 0)
    col = lax.broadcasted_iota(jnp.int32, (n, n), 1)
    upto = jnp.where(col <= row, 1.0, 0.0)
    later = jnp.where(row > col, jnp.broadcast_to(logs, (n, n)), 0.0)
    span = jnp.dot(upto, later, precision=HI, preferred_element_type=jnp.float32)
    factor = jnp.where(col <= row, jnp.exp(jnp.where(col <= row, span, 0.0)), 0.0)
    count = jnp.dot(factor, stats, precision=HI, preferred_element_type=jnp.float32)[:, 1:2]
    gram = jnp.dot(
        factor, r_ref[:, : wide - TILE], precision=HI, preferred_element_type=jnp.float32
    )
    o_ref[...] = gram / count


def decayed(received):
    n, wide = received.shape
    return pl.pallas_call(
        decay_body,
        out_shape=jax.ShapeDtypeStruct((n, wide - TILE), jnp.float32),
        in_specs=[VMEM],
        out_specs=VMEM,
        name="decayed_sums",
    )(received)


def spread_row(x, r):
    return jnp.broadcast_to(x[r : r + 1, :], x.shape)


def spread_lane(x, at):
    return jnp.broadcast_to(x[:, at : at + 1], x.shape)


def factor_tile(rows):
    lane = lax.broadcasted_iota(jnp.int32, (8, TILE), 1)
    sub = lax.broadcasted_iota(jnp.int32, (8, TILE), 0)
    rows, out = (list(rows), [])
    for k in range(len(rows)):
        base = 8 * k
        cols = [spread_lane(rows[k], base + c) for c in range(8)]
        inside = (lane >= base) & (lane < base + 8)
        g = jnp.where(inside, jnp.where(lane - base == sub, 1.0, 0.0), rows[k])
        w = g
        pivots = jnp.ones((8, TILE), jnp.float32)
        inverses = pivots
        for c in range(8):
            pivot = spread_row(cols[c], c)
            inverse = 1.0 / pivot
            scaled = cols[c] * inverse
            other = jnp.where(sub == c, 0.0, scaled)
            below = jnp.where(sub > c, scaled, 0.0)
            for s in range(c + 1, 8):
                cols[s] = cols[s] - other * spread_row(cols[s], c)
            g = g - other * spread_row(g, c)
            w = w - below * spread_row(w, c)
            pivots = jnp.where(sub == c, pivot, pivots)
            inverses = jnp.where(sub == c, inverse, inverses)
        z = g * inverses
        out.append(jnp.where(lane < base + 8, w * lax.rsqrt(pivots), 0.0))
        if k + 1 < len(rows):
            z_rows = [spread_row(z, c) for c in range(8)]
            for i in range(k + 1, len(rows)):
                m = [spread_lane(rows[i], base + c) * z_rows[c] for c in range(8)]
                total = ((m[0] + m[1]) + (m[2] + m[3])) + ((m[4] + m[5]) + (m[6] + m[7]))
                rows[i] = jnp.where(inside, 0.0, rows[i]) - total
    return out


def factor_body(group_ref, p_ref, o_ref, s_ref, d_ref, l_ref):
    groups, ways, wide = p_ref.shape
    n = s_ref.shape[0]
    count = n // TILE
    blocks = [(r, c) for r in range(count) for c in range(r, count)]
    for g in range(groups):
        for s in range(wide // TILE):
            first = (g * (wide // TILE) + s) * ways
            r, c = blocks[first // TILE]
            top = r * TILE + first % TILE
            piece = p_ref[g, :, s * TILE : (s + 1) * TILE]
            if r == c:
                row = lax.broadcasted_iota(jnp.int32, piece.shape, 0) + first % TILE
                lane = lax.broadcasted_iota(jnp.int32, piece.shape, 1)
                piece = piece + jnp.where(row == lane, loading_level, 0.0)
            s_ref[top : top + ways, c * TILE : (c + 1) * TILE] = piece
    for r in range(count):
        for c in range(r):
            s_ref[r * TILE : (r + 1) * TILE, c * TILE : (c + 1) * TILE] = jnp.zeros(
                (TILE, TILE), jnp.float32
            )
    tile_of = lax.broadcasted_iota(jnp.int32, (TILE, n), 1) // TILE

    @pl.loop(0, count)
    def _(k):
        first = pl.multiple_of(k * TILE, TILE)
        d_ref[...] = s_ref[pl.ds(first, TILE), pl.ds(first, TILE)]
        rows = factor_tile([d_ref[i : i + 8, :] for i in range(0, TILE, 8)])
        for i in range(TILE // 8):
            d_ref[8 * i : 8 * i + 8, :] = rows[i]
        x = d_ref[...]
        y = jnp.dot(x, s_ref[pl.ds(first, TILE), :], precision=HI, preferred_element_type=jnp.float32)
        y = jnp.where(tile_of == k, jnp.concatenate([x] * count, 1), y)
        l_ref[pl.ds(first, TILE), :] = jnp.where(tile_of <= k, y, 0.0)
        for i in range(1, count):

            @pl.when(i > k)
            def _():
                change = lax.dot_general(
                    y[:, i * TILE : (i + 1) * TILE],
                    y,
                    (((0,), (0,)), ((), ())),
                    precision=HI,
                    preferred_element_type=jnp.float32,
                )
                old = s_ref[i * TILE : (i + 1) * TILE, :]
                s_ref[i * TILE : (i + 1) * TILE, :] = jnp.where(tile_of == k, 0.0, old) - change

    mine = o_ref.shape[0]
    o_ref[...] = l_ref[pl.ds(pl.multiple_of(group_ref[0] * mine, mine), mine), :]


def inverse_factor_rows(packed, group, groups):
    ways, wide = packed.shape[1:]
    tiles = packed.size // (TILE * TILE)
    count = next(c for c in range(1, tiles + 1) if c * (c + 1) // 2 == tiles)
    n = count * TILE
    return pl.pallas_call(
        factor_body,
        out_shape=jax.ShapeDtypeStruct((n // groups, n), jnp.float32),
        in_specs=[SMEM, VMEM],
        out_specs=VMEM,
        scratch_shapes=[
            pltpu.VMEM((n, n), jnp.float32),
            pltpu.VMEM((TILE, TILE), jnp.float32),
            pltpu.VMEM((n, n), jnp.float32),
        ],
        compiler_params=pltpu.CompilerParams(vmem_limit_bytes=32 << 20),
        cost_estimate=pl.CostEstimate(flops=12 * n**3, bytes_accessed=1 << 20, transcendentals=n),
        name="inverse_factor",
    )(group.reshape(1).astype(jnp.int32), packed)


def local(samples, taps_weight, retain):
    row_count = samples.shape[0]
    groups, blocks = (lax.axis_size("elem"), lax.axis_size("tm"))
    group = lax.axis_index("elem")
    share = row_count // groups
    with jax.named_scope("halo"):
        halo = shifted(samples[row_count - 16 :], "tm", 1)
    beams_part = fir(halo, samples, taps_weight)
    log_retain = jnp.log(retain)
    log_total = jnp.sum(log_retain)
    row_weight = jnp.exp(log_total - jnp.cumsum(log_retain))
    mass = jnp.sum(row_weight)
    my_weight = lax.dynamic_slice_in_dim(row_weight, group * share, share)[:, None]
    with jax.named_scope("beams_sum"):
        my_beams = lax.psum_scatter(beams_part, "elem", scatter_dimension=0, tiled=True)
    packed = packed_gram(my_beams, my_weight)
    with jax.named_scope("gram_sum"):
        parts = lax.all_to_all(
            packed.reshape(groups, packed.shape[0] // groups, TILE), "elem", 0, 0
        )
    with jax.named_scope("beams_gather"):
        my_beams, _ = lax.optimization_barrier((my_beams, parts[0, :8]))
        beam_rows = lax.all_gather(my_beams, "elem", tiled=True)
    spread = spread_share(parts, log_total, mass, blocks)
    with jax.named_scope("blocks_out"):
        received = lax.all_to_all(spread, "tm", 0, 0, tiled=True)
    estimate = decayed(received)
    with jax.named_scope("blocks_back"):
        returned = lax.all_to_all(estimate, "tm", 0, 0, tiled=True)
    with jax.named_scope("gram_gather"):
        packed_estimate = lax.all_gather(returned, "elem")
    inverse_rows = inverse_factor_rows(packed_estimate, group, groups)
    return lax.dot_general(
        inverse_rows, beam_rows, (((1,), (1,)), ((), ())), precision=HI
    )


def solution(mesh):
    placed = (P("tm", "elem"), P(None, "elem", None), P("tm"))
    return jax.shard_map(
        local, mesh=mesh, in_specs=placed, out_specs=P("elem", "tm"), check_vma=False
    )
```

```python
import jax
import jax.numpy as jnp
from jax import lax
from jax.experimental import pallas as pl
from jax.experimental.pallas import tpu as pltpu
from jax.sharding import PartitionSpec as P

loading_level = 0.1
HI = lax.Precision.HIGHEST
TILE = 128
VMEM = pl.BlockSpec(memory_space=pltpu.VMEM)
SMEM = pl.BlockSpec(memory_space=pltpu.SMEM)


def shifted(array, axis, by):
    size = lax.axis_size(axis)
    pairs = [(i, i + by) for i in range(size) if 0 <= i + by < size]
    return lax.ppermute(array, axis, pairs)


LEAD = 16
SPLIT = 4


def fir_body(offsets, weights, group_ref, halo_ref, x_hbm, w_hbm, retain_ref, *refs):
    outs, (xb_ref, xe_ref, part_ref, wv_ref, x_sem, w_sem) = (refs[:-6], refs[-6:])
    taps, width, beams = w_hbm.shape
    rows = x_hbm.shape[0]
    groups = 8
    share = rows // groups
    each = taps // SPLIT
    copy_x = pltpu.make_async_copy(x_hbm, xb_ref, x_sem)
    copy_x.start()
    copies = []
    for q in range(SPLIT):
        span = pl.ds(q * each, each)
        copies.append(pltpu.make_async_copy(w_hbm.at[span], wv_ref.at[span], w_sem.at[q]))
        copies[-1].start()
    group = group_ref[0]
    if weights:
        weights_of(group, groups, retain_ref, outs[-2], outs[-1])
        outs = outs[:-2]
    xe_ref[:LEAD, :] = halo_ref[...].astype(jnp.float32)
    copy_x.wait()
    xe_ref[LEAD:, :] = xb_ref[...].astype(jnp.float32)
    tall = share + LEAD
    for i, by in enumerate(offsets):
        chunk = lax.rem(group + (by + groups), groups)
        part_ref[i * tall : (i + 1) * tall, :] = xe_ref[
            pl.ds(pl.multiple_of(chunk * share, 8), tall), :
        ]
    total = None
    for q in range(SPLIT):
        copies[q].wait()
        window = jnp.concatenate(
            [
                jnp.concatenate(
                    [
                        part_ref[i * tall + LEAD - k : (i + 1) * tall - k, :]
                        for i in range(len(offsets))
                    ],
                    0,
                ).astype(jnp.bfloat16)
                for k in range(q * each, (q + 1) * each)
            ],
            1,
        )
        product = jnp.dot(
            window,
            wv_ref[q * each : (q + 1) * each].reshape(each * width, beams),
            preferred_element_type=jnp.float32,
        )
        at = 0
        for o_ref in outs:
            tall_o = o_ref.shape[0]
            piece = product[at : at + tall_o]
            o_ref[...] = piece if q == 0 else o_ref[...] + piece
            at += tall_o


def weights_of(group, groups, retain_ref, weight_ref, stats_ref):
    rows = retain_ref.shape[1]
    share = rows // groups
    logs = jnp.log(retain_ref[...])
    lane = lax.broadcasted_iota(jnp.int32, (share, rows), 1)
    row = lax.broadcasted_iota(jnp.int32, (share, rows), 0)
    spread = jnp.broadcast_to(logs, (share, rows))

    def weight_at(first):
        later = jnp.where(lane > row + first, spread, 0.0)
        return jnp.exp(jnp.sum(later, axis=1, keepdims=True))

    mass = jnp.zeros((1, 1), jnp.float32)
    for g in range(groups):
        mass = mass + jnp.sum(weight_at(g * share), axis=0, keepdims=True)
    weight_ref[...] = jnp.broadcast_to(weight_at(group * share), weight_ref.shape)
    log_total = jnp.sum(logs, axis=1, keepdims=True)
    at = lax.broadcasted_iota(jnp.int32, stats_ref.shape, 1)
    stats_ref[...] = jnp.where(
        at == 0,
        jnp.broadcast_to(log_total, stats_ref.shape),
        jnp.broadcast_to(mass, stats_ref.shape),
    )


def fir(offsets, heights, weights, group, halo, samples, taps_weight, retain):
    rows, width = samples.shape
    taps, _, beams = taps_weight.shape
    share = rows // 8
    tall = share + LEAD
    shapes = [jax.ShapeDtypeStruct((h, beams), jnp.float32) for h in heights]
    if weights:
        shapes.append(jax.ShapeDtypeStruct((share, TILE), jnp.float32))
        shapes.append(jax.ShapeDtypeStruct((1, TILE), jnp.float32))
    any_space = pl.BlockSpec(memory_space=pltpu.HBM)
    return pl.pallas_call(
        lambda *refs: fir_body(offsets, weights, *refs),
        out_shape=shapes,
        in_specs=[SMEM, VMEM, any_space, any_space, VMEM],
        out_specs=[VMEM] * len(shapes),
        scratch_shapes=[
            pltpu.VMEM((rows, width), samples.dtype),
            pltpu.VMEM((rows + LEAD, width), jnp.float32),
            pltpu.VMEM((tall * len(offsets), width), jnp.float32),
            pltpu.VMEM(taps_weight.shape, taps_weight.dtype),
            pltpu.SemaphoreType.DMA,
            pltpu.SemaphoreType.DMA((SPLIT,)),
        ],
        compiler_params=pltpu.CompilerParams(vmem_limit_bytes=60 << 20),
        cost_estimate=pl.CostEstimate(
            flops=2 * share * len(offsets) * taps * width * beams,
            bytes_accessed=6 << 20,
            transcendentals=0,
        ),
        name="fir_rest" if weights else "fir_sent",
    )(group, halo, samples, taps_weight, retain)


def ring(array, by):
    size = lax.axis_size("elem")
    return lax.ppermute(array, "elem", [(i, (i + by) % size) for i in range(size)])


def relay_body(keep_ref, down_ref, up_ref, far_down_ref, far_up_ref, low_ref, high_ref):
    share = low_ref.shape[0]
    half = share // 2
    low = keep_ref[share : 2 * share, :] + down_ref[share:, :]
    low_ref[:half, :] = low[:half] + far_down_ref[...]
    low_ref[half:, :] = low[half:]
    high = keep_ref[2 * share :, :] + up_ref[share:, :]
    high_ref[:half, :] = high[:half]
    high_ref[half:, :] = high[half:] + far_up_ref[...]


def relay_sums(keep, down, up, far_down, far_up):
    shape = jax.ShapeDtypeStruct((keep.shape[0] // 3, keep.shape[1]), jnp.float32)
    return pl.pallas_call(
        relay_body,
        out_shape=(shape, shape),
        in_specs=[VMEM] * 5,
        out_specs=(VMEM, VMEM),
        compiler_params=pltpu.CompilerParams(vmem_limit_bytes=5 << 20),
        name="relay_sums",
    )(keep, down, up, far_down, far_up)


def gram_body(keep_ref, down_ref, up_ref, low_ref, high_ref, weight_ref, b_ref, o_ref):
    share, beams = b_ref.shape
    b_ref[...] = (
        (keep_ref[:share, :] + down_ref[:share, :])
        + (up_ref[:share, :] + low_ref[...])
        + high_ref[...]
    )
    weighted = b_ref[...] * jnp.concatenate([weight_ref[...]] * (beams // TILE), 1)
    at = 0
    for r in range(0, beams, TILE):
        part = lax.dot_general(
            weighted[:, r : r + TILE],
            b_ref[:, r:],
            (((0,), (0,)), ((), ())),
            precision=HI,
            preferred_element_type=jnp.float32,
        )
        for c in range(0, beams - r, TILE):
            o_ref[at : at + TILE, :] = part[:, c : c + TILE]
            at += TILE


def packed_gram(keep, down, up, low, high, weight):
    share, beams = low.shape
    n = beams // TILE
    return pl.pallas_call(
        gram_body,
        out_shape=(
            jax.ShapeDtypeStruct((share, beams), jnp.float32),
            jax.ShapeDtypeStruct((n * (n + 1) // 2 * TILE, TILE), jnp.float32),
        ),
        in_specs=[VMEM] * 6,
        out_specs=(VMEM, VMEM),
        compiler_params=pltpu.CompilerParams(vmem_limit_bytes=6 << 20),
        name="packed_gram",
    )(keep, down, up, low, high, weight)


def share_body(stats_ref, p_ref, o_ref):
    groups, rows, _ = p_ref.shape
    ways = o_ref.shape[0]
    total = p_ref[0]
    for g in range(1, groups):
        total = total + p_ref[g]
    tiles = rows // ways
    for s in range(tiles):
        o_ref[:, s, :] = total[s * ways : (s + 1) * ways, :]
    o_ref[:, tiles, :] = jnp.broadcast_to(stats_ref[...], (ways, TILE))


def spread_share(parts, stats, ways):
    groups, rows, _ = parts.shape
    return pl.pallas_call(
        share_body,
        out_shape=jax.ShapeDtypeStruct((ways, rows // ways + 1, TILE), jnp.float32),
        in_specs=[VMEM, VMEM],
        out_specs=VMEM,
        compiler_params=pltpu.CompilerParams(vmem_limit_bytes=4 << 20),
        name="spread_share",
    )(stats, parts)


def decay_body(r_ref, o_ref):
    n, tiles, _ = r_ref.shape
    tiles -= 1
    stats = r_ref[:, tiles, :]
    logs = stats[:, 0:1]
    row = lax.broadcasted_iota(jnp.int32, (n, n), 0)
    col = lax.broadcasted_iota(jnp.int32, (n, n), 1)
    upto = jnp.where(col <= row, 1.0, 0.0)
    later = jnp.where(row > col, jnp.broadcast_to(logs, (n, n)), 0.0)
    span = jnp.dot(upto, later, precision=HI, preferred_element_type=jnp.float32)
    factor = jnp.where(col <= row, jnp.exp(jnp.where(col <= row, span, 0.0)), 0.0)
    count = jnp.dot(factor, stats, precision=HI, preferred_element_type=jnp.float32)[:, 1:2]
    gram = jnp.dot(
        factor,
        jnp.concatenate([r_ref[:, s, :] for s in range(tiles)], 1),
        precision=HI,
        preferred_element_type=jnp.float32,
    )
    gram = gram / count
    for s in range(tiles):
        o_ref[:, s, :] = gram[:, s * TILE : (s + 1) * TILE]


def decayed(received):
    n, tiles, _ = received.shape
    return pl.pallas_call(
        decay_body,
        out_shape=jax.ShapeDtypeStruct((n, tiles - 1, TILE), jnp.float32),
        in_specs=[VMEM],
        out_specs=VMEM,
        compiler_params=pltpu.CompilerParams(vmem_limit_bytes=4 << 20),
        name="decayed_sums",
    )(received)


def replicate_body(r_ref, o_ref):
    ways, tiles, _ = r_ref.shape
    for s in range(tiles):
        piece = r_ref[:, s, :]
        for g in range(o_ref.shape[0]):
            o_ref[g, s * ways : (s + 1) * ways, :] = piece


def replicated(returned, groups):
    ways, tiles, _ = returned.shape
    return pl.pallas_call(
        replicate_body,
        out_shape=jax.ShapeDtypeStruct((groups, ways * tiles, TILE), jnp.float32),
        in_specs=[VMEM],
        out_specs=VMEM,
        compiler_params=pltpu.CompilerParams(vmem_limit_bytes=4 << 20),
        name="replicated",
    )(returned)


def spread_row(x, r):
    return jnp.broadcast_to(x[r : r + 1, :], x.shape)


def spread_lane(x, at):
    return jnp.broadcast_to(x[:, at : at + 1], x.shape)


def factor_tile(rows):
    lane = lax.broadcasted_iota(jnp.int32, (8, TILE), 1)
    sub = lax.broadcasted_iota(jnp.int32, (8, TILE), 0)
    rows, out = (list(rows), [])
    for k in range(len(rows)):
        base = 8 * k
        cols = [spread_lane(rows[k], base + c) for c in range(8)]
        inside = (lane >= base) & (lane < base + 8)
        g = jnp.where(inside, jnp.where(lane - base == sub, 1.0, 0.0), rows[k])
        w = g
        pivots = jnp.ones((8, TILE), jnp.float32)
        inverses = pivots
        for c in range(8):
            pivot = spread_row(cols[c], c)
            inverse = 1.0 / pivot
            scaled = cols[c] * inverse
            other = jnp.where(sub == c, 0.0, scaled)
            below = jnp.where(sub > c, scaled, 0.0)
            for s in range(c + 1, 8):
                cols[s] = cols[s] - other * spread_row(cols[s], c)
            g = g - other * spread_row(g, c)
            w = w - below * spread_row(w, c)
            pivots = jnp.where(sub == c, pivot, pivots)
            inverses = jnp.where(sub == c, inverse, inverses)
        z = g * inverses
        out.append(jnp.where(lane < base + 8, w * lax.rsqrt(pivots), 0.0))
        if k + 1 < len(rows):
            z_rows = [spread_row(z, c) for c in range(8)]
            for i in range(k + 1, len(rows)):
                m = [spread_lane(rows[i], base + c) * z_rows[c] for c in range(8)]
                total = ((m[0] + m[1]) + (m[2] + m[3])) + ((m[4] + m[5]) + (m[6] + m[7]))
                rows[i] = jnp.where(inside, 0.0, rows[i]) - total
    return out


def factor_body(p_ref, b_ref, o_ref, s_ref, d_ref, l_ref):
    groups, high, _ = p_ref.shape
    ways = 32
    tiles = high // ways
    n = s_ref.shape[0]
    count = n // TILE
    blocks = [(r, c) for r in range(count) for c in range(r, count)]
    for g in range(groups):
        for s in range(tiles):
            first = (g * tiles + s) * ways
            r, c = blocks[first // TILE]
            top = r * TILE + first % TILE
            piece = p_ref[g, s * ways : (s + 1) * ways, :]
            if r == c:
                row = lax.broadcasted_iota(jnp.int32, piece.shape, 0) + first % TILE
                lane = lax.broadcasted_iota(jnp.int32, piece.shape, 1)
                piece = piece + jnp.where(row == lane, loading_level, 0.0)
            s_ref[top : top + ways, c * TILE : (c + 1) * TILE] = piece
    for r in range(count):
        for c in range(r):
            s_ref[r * TILE : (r + 1) * TILE, c * TILE : (c + 1) * TILE] = jnp.zeros(
                (TILE, TILE), jnp.float32
            )
    tile_of = lax.broadcasted_iota(jnp.int32, (TILE, n), 1) // TILE

    @pl.loop(0, count)
    def _(k):
        first = pl.multiple_of(k * TILE, TILE)
        d_ref[...] = s_ref[pl.ds(first, TILE), pl.ds(first, TILE)]
        rows = factor_tile([d_ref[i : i + 8, :] for i in range(0, TILE, 8)])
        for i in range(TILE // 8):
            d_ref[8 * i : 8 * i + 8, :] = rows[i]
        x = d_ref[...]
        y = jnp.dot(x, s_ref[pl.ds(first, TILE), :], precision=HI, preferred_element_type=jnp.float32)
        y = jnp.where(tile_of == k, jnp.concatenate([x] * count, 1), y)
        l_ref[pl.ds(first, TILE), :] = jnp.where(tile_of <= k, y, 0.0)
        for i in range(1, count):

            @pl.when(i > k)
            def _():
                change = lax.dot_general(
                    y[:, i * TILE : (i + 1) * TILE],
                    y,
                    (((0,), (0,)), ((), ())),
                    precision=HI,
                    preferred_element_type=jnp.float32,
                )
                old = s_ref[i * TILE : (i + 1) * TILE, :]
                s_ref[i * TILE : (i + 1) * TILE, :] = jnp.where(tile_of == k, 0.0, old) - change

    o_ref[...] = lax.dot_general(
        l_ref[...],
        b_ref[...],
        (((1,), (1,)), ((), ())),
        precision=HI,
        preferred_element_type=jnp.float32,
    )


def whitened_share(packed, my_beams):
    share, n = my_beams.shape
    return pl.pallas_call(
        factor_body,
        out_shape=jax.ShapeDtypeStruct((n, share), jnp.float32),
        in_specs=[VMEM, VMEM],
        out_specs=VMEM,
        scratch_shapes=[
            pltpu.VMEM((n, n), jnp.float32),
            pltpu.VMEM((TILE, TILE), jnp.float32),
            pltpu.VMEM((n, n), jnp.float32),
        ],
        compiler_params=pltpu.CompilerParams(vmem_limit_bytes=8 << 20),
        cost_estimate=pl.CostEstimate(flops=12 * n**3, bytes_accessed=1 << 20, transcendentals=n),
        name="whitened_share",
    )(packed, my_beams)


def join_body(r_ref, o_ref):
    share = r_ref.shape[2]
    for g in range(r_ref.shape[0]):
        o_ref[:, g * share : (g + 1) * share] = r_ref[g]


def joined(received):
    groups, mine, share = received.shape
    return pl.pallas_call(
        join_body,
        out_shape=jax.ShapeDtypeStruct((mine, groups * share), jnp.float32),
        in_specs=[VMEM],
        out_specs=VMEM,
        compiler_params=pltpu.CompilerParams(vmem_limit_bytes=3 << 20),
        name="joined",
    )(received)


def local(samples, taps_weight, retain):
    row_count = samples.shape[0]
    groups, blocks = (lax.axis_size("elem"), lax.axis_size("tm"))
    group = lax.axis_index("elem").reshape(1).astype(jnp.int32)
    share = row_count // groups
    half = share // 2
    with jax.named_scope("halo"):
        halo = shifted(samples[row_count - LEAD :], "tm", 1)
    args = (group, halo, samples, taps_weight, retain.reshape(1, row_count))
    down, up, far_down, far_up = fir(
        (-1, -3, 1, 3, 4), (2 * share, 2 * share, half, half), False, *args
    )
    with jax.named_scope("beams_near"):
        down, up = (ring(down, -1), ring(up, 1))
        far_down, far_up = (ring(far_down, -2), ring(far_up, 2))
    keep, weight, stats = fir((0, -2, 2), (3 * share,), True, *args)
    low, high = relay_sums(keep, down, up, far_down, far_up)
    with jax.named_scope("beams_far"):
        low, high = (ring(low, -2), ring(high, 2))
    my_beams, packed = packed_gram(keep, down, up, low, high, weight)
    with jax.named_scope("gram_sum"):
        parts = lax.all_to_all(
            packed.reshape(groups, packed.shape[0] // groups, TILE), "elem", 0, 0
        )
    spread = spread_share(parts, stats, blocks)
    with jax.named_scope("blocks_out"):
        received = lax.all_to_all(spread, "tm", 0, 0, tiled=True)
    estimate = decayed(received)
    with jax.named_scope("blocks_back"):
        returned = lax.all_to_all(estimate, "tm", 0, 0, tiled=True)
    with jax.named_scope("gram_gather"):
        packed_estimate = lax.all_to_all(replicated(returned, groups), "elem", 0, 0)
    mine = whitened_share(packed_estimate, my_beams)
    with jax.named_scope("whitened_out"):
        pieces = lax.all_to_all(mine.reshape(groups, mine.shape[0] // groups, share), "elem", 0, 0)
    return joined(pieces)


def solution(mesh):
    placed = (P("tm", "elem"), P(None, "elem", None), P("tm"))
    return jax.shard_map(
        local, mesh=mesh, in_specs=placed, out_specs=P("elem", "tm"), check_vma=False
    )
```

```python
import jax
import jax.numpy as jnp
from jax import lax
from jax.experimental import pallas as pl
from jax.experimental.pallas import tpu as pltpu
from jax.sharding import PartitionSpec as P

loading_level = 0.1
HI = lax.Precision.HIGHEST
TILE = 128
VMEM = pl.BlockSpec(memory_space=pltpu.VMEM)
SMEM = pl.BlockSpec(memory_space=pltpu.SMEM)


def shifted(array, axis, by):
    size = lax.axis_size(axis)
    pairs = [(i, i + by) for i in range(size) if 0 <= i + by < size]
    return lax.ppermute(array, axis, pairs)


LEAD = 16
SPLIT = 4


def fir_body(offsets, weights, group_ref, halo_ref, x_hbm, w_hbm, *refs):
    if weights:
        retain_ref, refs = (refs[0], refs[1:])
    held = 2 if weights else 6
    outs, (xe_ref, part_ref, *own) = (refs[:-held], refs[-held:])
    taps, width, beams = w_hbm.shape
    rows = x_hbm.shape[0]
    groups = 8
    share = rows // groups
    each = taps // SPLIT
    copies = []
    if weights:
        xb_ref, wv_ref = (x_hbm, w_hbm)
    else:
        xb_ref, wv_ref, x_sem, w_sem = own
        copy_x = pltpu.make_async_copy(x_hbm, xb_ref, x_sem)
        copy_x.start()
        for q in range(SPLIT):
            span = pl.ds(q * each, each)
            copies.append(pltpu.make_async_copy(w_hbm.at[span], wv_ref.at[span], w_sem.at[q]))
            copies[-1].start()
    group = group_ref[0]
    if weights:
        weights_of(group, groups, retain_ref, outs[-2], outs[-1])
        outs = outs[:-2]
    xe_ref[:LEAD, :] = halo_ref[...].astype(jnp.float32)
    if not weights:
        copy_x.wait()
    xe_ref[LEAD:, :] = xb_ref[...].astype(jnp.float32)
    tall = share + LEAD
    for i, by in enumerate(offsets):
        chunk = lax.rem(group + (by + groups), groups)
        part_ref[i * tall : (i + 1) * tall, :] = xe_ref[
            pl.ds(pl.multiple_of(chunk * share, 8), tall), :
        ]
    total = None
    for q in range(SPLIT):
        if not weights:
            copies[q].wait()
        window = jnp.concatenate(
            [
                jnp.concatenate(
                    [
                        part_ref[i * tall + LEAD - k : (i + 1) * tall - k, :]
                        for i in range(len(offsets))
                    ],
                    0,
                ).astype(jnp.bfloat16)
                for k in range(q * each, (q + 1) * each)
            ],
            1,
        )
        product = jnp.dot(
            window,
            wv_ref[q * each : (q + 1) * each].reshape(each * width, beams),
            preferred_element_type=jnp.float32,
        )
        at = 0
        for o_ref in outs:
            tall_o = o_ref.shape[0]
            piece = product[at : at + tall_o]
            o_ref[...] = piece if q == 0 else o_ref[...] + piece
            at += tall_o


def weights_of(group, groups, retain_ref, weight_ref, stats_ref):
    rows = retain_ref.shape[0]
    share = rows // groups
    logs = jnp.log(retain_ref[...].reshape(1, rows))
    lane = lax.broadcasted_iota(jnp.int32, (share, rows), 1)
    row = lax.broadcasted_iota(jnp.int32, (share, rows), 0)
    spread = jnp.broadcast_to(logs, (share, rows))

    def weight_at(first):
        later = jnp.where(lane > row + first, spread, 0.0)
        return jnp.exp(jnp.sum(later, axis=1, keepdims=True))

    mass = jnp.zeros((1, 1), jnp.float32)
    for g in range(groups):
        mass = mass + jnp.sum(weight_at(g * share), axis=0, keepdims=True)
    weight_ref[...] = jnp.broadcast_to(weight_at(group * share), weight_ref.shape)
    log_total = jnp.sum(logs, axis=1, keepdims=True)
    at = lax.broadcasted_iota(jnp.int32, stats_ref.shape, 1)
    stats_ref[...] = jnp.where(
        at == 0,
        jnp.broadcast_to(log_total, stats_ref.shape),
        jnp.broadcast_to(mass, stats_ref.shape),
    )


def fir(offsets, heights, weights, group, halo, samples, taps_weight, retain):
    rows, width = samples.shape
    taps, _, beams = taps_weight.shape
    share = rows // 8
    tall = share + LEAD
    shapes = [jax.ShapeDtypeStruct((h, beams), jnp.float32) for h in heights]
    if weights:
        shapes.append(jax.ShapeDtypeStruct((share, TILE), jnp.float32))
        shapes.append(jax.ShapeDtypeStruct((1, TILE), jnp.float32))
    large = VMEM if weights else pl.BlockSpec(memory_space=pltpu.HBM)
    scratch = [
        pltpu.VMEM((rows + LEAD, width), jnp.float32),
        pltpu.VMEM((tall * len(offsets), width), jnp.float32),
    ]
    if not weights:
        scratch += [
            pltpu.VMEM((rows, width), samples.dtype),
            pltpu.VMEM(taps_weight.shape, taps_weight.dtype),
            pltpu.SemaphoreType.DMA,
            pltpu.SemaphoreType.DMA((SPLIT,)),
        ]
    return pl.pallas_call(
        lambda *refs: fir_body(offsets, weights, *refs),
        out_shape=shapes,
        in_specs=[SMEM, VMEM, large, large] + [VMEM] * weights,
        out_specs=[VMEM] * len(shapes),
        scratch_shapes=scratch,
        compiler_params=pltpu.CompilerParams(vmem_limit_bytes=(16 if weights else 60) << 20),
        cost_estimate=pl.CostEstimate(
            flops=2 * share * len(offsets) * taps * width * beams,
            bytes_accessed=6 << 20,
            transcendentals=0,
        ),
        name="fir_rest" if weights else "fir_sent",
    )(group, halo, samples, taps_weight, *([retain] if weights else []))


def ring(array, by):
    size = lax.axis_size("elem")
    return lax.ppermute(array, "elem", [(i, (i + by) % size) for i in range(size)])


def relay_body(keep_ref, down_ref, up_ref, far_down_ref, far_up_ref, low_ref, high_ref):
    share = low_ref.shape[0]
    half = share // 2
    low = keep_ref[share : 2 * share, :] + down_ref[share:, :]
    low_ref[:half, :] = low[:half] + far_down_ref[...]
    low_ref[half:, :] = low[half:]
    high = keep_ref[2 * share :, :] + up_ref[share:, :]
    high_ref[:half, :] = high[:half]
    high_ref[half:, :] = high[half:] + far_up_ref[...]


def relay_sums(keep, down, up, far_down, far_up):
    shape = jax.ShapeDtypeStruct((keep.shape[0] // 3, keep.shape[1]), jnp.float32)
    return pl.pallas_call(
        relay_body,
        out_shape=(shape, shape),
        in_specs=[VMEM] * 5,
        out_specs=(VMEM, VMEM),
        compiler_params=pltpu.CompilerParams(vmem_limit_bytes=5 << 20),
        name="relay_sums",
    )(keep, down, up, far_down, far_up)


def gram_body(keep_ref, down_ref, up_ref, low_ref, high_ref, weight_ref, b_ref, o_ref):
    share, beams = b_ref.shape
    b_ref[...] = (
        (keep_ref[:share, :] + down_ref[:share, :])
        + (up_ref[:share, :] + low_ref[...])
        + high_ref[...]
    )
    weighted = b_ref[...] * jnp.concatenate([weight_ref[...]] * (beams // TILE), 1)
    at = 0
    for r in range(0, beams, TILE):
        part = lax.dot_general(
            weighted[:, r : r + TILE],
            b_ref[:, r:],
            (((0,), (0,)), ((), ())),
            precision=HI,
            preferred_element_type=jnp.float32,
        )
        for c in range(0, beams - r, TILE):
            o_ref[at : at + TILE, :] = part[:, c : c + TILE]
            at += TILE


def packed_gram(keep, down, up, low, high, weight):
    share, beams = low.shape
    n = beams // TILE
    return pl.pallas_call(
        gram_body,
        out_shape=(
            jax.ShapeDtypeStruct((share, beams), jnp.float32),
            jax.ShapeDtypeStruct((n * (n + 1) // 2 * TILE, TILE), jnp.float32),
        ),
        in_specs=[VMEM] * 6,
        out_specs=(VMEM, VMEM),
        compiler_params=pltpu.CompilerParams(vmem_limit_bytes=6 << 20),
        name="packed_gram",
    )(keep, down, up, low, high, weight)


def share_body(stats_ref, p_ref, o_ref):
    groups, rows, _ = p_ref.shape
    ways = o_ref.shape[0]
    total = p_ref[0]
    for g in range(1, groups):
        total = total + p_ref[g]
    tiles = rows // ways
    for s in range(tiles):
        o_ref[:, s, :] = total[s * ways : (s + 1) * ways, :]
    o_ref[:, tiles, :] = jnp.broadcast_to(stats_ref[...], (ways, TILE))


def spread_share(parts, stats, ways):
    groups, rows, _ = parts.shape
    return pl.pallas_call(
        share_body,
        out_shape=jax.ShapeDtypeStruct((ways, rows // ways + 1, TILE), jnp.float32),
        in_specs=[VMEM, VMEM],
        out_specs=VMEM,
        compiler_params=pltpu.CompilerParams(vmem_limit_bytes=4 << 20),
        name="spread_share",
    )(stats, parts)


def decay_body(r_ref, o_ref):
    n, tiles, _ = r_ref.shape
    tiles -= 1
    stats = r_ref[:, tiles, :]
    logs = stats[:, 0:1]
    row = lax.broadcasted_iota(jnp.int32, (n, n), 0)
    col = lax.broadcasted_iota(jnp.int32, (n, n), 1)
    upto = jnp.where(col <= row, 1.0, 0.0)
    later = jnp.where(row > col, jnp.broadcast_to(logs, (n, n)), 0.0)
    span = jnp.dot(upto, later, precision=HI, preferred_element_type=jnp.float32)
    factor = jnp.where(col <= row, jnp.exp(jnp.where(col <= row, span, 0.0)), 0.0)
    count = jnp.dot(factor, stats, precision=HI, preferred_element_type=jnp.float32)[:, 1:2]
    gram = jnp.dot(
        factor,
        jnp.concatenate([r_ref[:, s, :] for s in range(tiles)], 1),
        precision=HI,
        preferred_element_type=jnp.float32,
    )
    gram = gram / count
    for s in range(tiles):
        o_ref[:, s, :] = gram[:, s * TILE : (s + 1) * TILE]


def decayed(received):
    n, tiles, _ = received.shape
    return pl.pallas_call(
        decay_body,
        out_shape=jax.ShapeDtypeStruct((n, tiles - 1, TILE), jnp.float32),
        in_specs=[VMEM],
        out_specs=VMEM,
        compiler_params=pltpu.CompilerParams(vmem_limit_bytes=4 << 20),
        name="decayed_sums",
    )(received)


def replicate_body(r_ref, o_ref):
    ways, tiles, _ = r_ref.shape
    for s in range(tiles):
        piece = r_ref[:, s, :]
        for g in range(o_ref.shape[0]):
            o_ref[g, s * ways : (s + 1) * ways, :] = piece


def replicated(returned, groups):
    ways, tiles, _ = returned.shape
    return pl.pallas_call(
        replicate_body,
        out_shape=jax.ShapeDtypeStruct((groups, ways * tiles, TILE), jnp.float32),
        in_specs=[VMEM],
        out_specs=VMEM,
        compiler_params=pltpu.CompilerParams(vmem_limit_bytes=4 << 20),
        name="replicated",
    )(returned)


def spread_row(x, r):
    return jnp.broadcast_to(x[r : r + 1, :], x.shape)


def spread_lane(x, at):
    return jnp.broadcast_to(x[:, at : at + 1], x.shape)


def factor_tile(rows):
    lane = lax.broadcasted_iota(jnp.int32, (8, TILE), 1)
    sub = lax.broadcasted_iota(jnp.int32, (8, TILE), 0)
    rows, out, n = (list(rows), [], len(rows))
    cols = [spread_lane(rows[0], c) for c in range(8)]
    for k in range(n):
        base = 8 * k
        last = k + 1 == n
        after = [] if last else [spread_lane(rows[k], base + 8 + c) for c in range(8)]
        inside = (lane >= base) & (lane < base + 8)
        g = jnp.where(inside, jnp.where(lane - base == sub, 1.0, 0.0), rows[k])
        w = g
        pivots = jnp.ones((8, TILE), jnp.float32)
        inverses = pivots
        for c in range(8):
            pivot = spread_row(cols[c], c)
            inverse = 1.0 / pivot
            other = jnp.where(sub == c, 0.0, cols[c])
            below = jnp.where(sub > c, cols[c], 0.0)
            for s in range(c + 1, 8):
                cols[s] = cols[s] - (other * spread_row(cols[s], c)) * inverse
            scaled = other * inverse
            g = g - scaled * spread_row(g, c)
            w = w - (below * inverse) * spread_row(w, c)
            after = [v - scaled * spread_row(v, c) for v in after]
            pivots = jnp.where(sub == c, pivot, pivots)
            inverses = jnp.where(sub == c, inverse, inverses)
        z = g * inverses
        out.append(jnp.where(lane < base + 8, w * lax.rsqrt(pivots), 0.0))
        if last:
            break
        z_rows = [spread_row(z, c) for c in range(8)]
        for i in range(k + 1, n):
            factors = [spread_lane(rows[i], base + c) for c in range(8)]
            if i == k + 1:
                new = []
                for s in range(8):
                    v = after[s] * inverses
                    m = [factors[c] * spread_row(v, c) for c in range(8)]
                    new.append(spread_lane(rows[i], base + 8 + s) - sum_of(m))
                cols = new
            m = [factors[c] * z_rows[c] for c in range(8)]
            rows[i] = jnp.where(inside, 0.0, rows[i]) - sum_of(m)
    return out


def sum_of(m):
    return ((m[0] + m[1]) + (m[2] + m[3])) + ((m[4] + m[5]) + (m[6] + m[7]))


def factor_body(p_ref, b_ref, o_ref, s_ref, d_ref, l_ref):
    groups, high, _ = p_ref.shape
    ways = 32
    tiles = high // ways
    n = s_ref.shape[0]
    count = n // TILE
    blocks = [(r, c) for r in range(count) for c in range(r, count)]
    for g in range(groups):
        for s in range(tiles):
            first = (g * tiles + s) * ways
            r, c = blocks[first // TILE]
            top = r * TILE + first % TILE
            piece = p_ref[g, s * ways : (s + 1) * ways, :]
            if r == c:
                row = lax.broadcasted_iota(jnp.int32, piece.shape, 0) + first % TILE
                lane = lax.broadcasted_iota(jnp.int32, piece.shape, 1)
                piece = piece + jnp.where(row == lane, loading_level, 0.0)
            s_ref[top : top + ways, c * TILE : (c + 1) * TILE] = piece
    for r in range(count):
        for c in range(r):
            s_ref[r * TILE : (r + 1) * TILE, c * TILE : (c + 1) * TILE] = jnp.zeros(
                (TILE, TILE), jnp.float32
            )
    tile_of = lax.broadcasted_iota(jnp.int32, (TILE, n), 1) // TILE

    @pl.loop(0, count)
    def _(k):
        first = pl.multiple_of(k * TILE, TILE)
        d_ref[...] = s_ref[pl.ds(first, TILE), pl.ds(first, TILE)]
        rows = factor_tile([d_ref[i : i + 8, :] for i in range(0, TILE, 8)])
        for i in range(TILE // 8):
            d_ref[8 * i : 8 * i + 8, :] = rows[i]
        x = d_ref[...]
        y = jnp.dot(x, s_ref[pl.ds(first, TILE), :], precision=HI, preferred_element_type=jnp.float32)
        y = jnp.where(tile_of == k, jnp.concatenate([x] * count, 1), y)
        l_ref[pl.ds(first, TILE), :] = jnp.where(tile_of <= k, y, 0.0)
        for i in range(1, count):

            @pl.when(i > k)
            def _():
                change = lax.dot_general(
                    y[:, i * TILE : (i + 1) * TILE],
                    y,
                    (((0,), (0,)), ((), ())),
                    precision=HI,
                    preferred_element_type=jnp.float32,
                )
                old = s_ref[i * TILE : (i + 1) * TILE, :]
                s_ref[i * TILE : (i + 1) * TILE, :] = jnp.where(tile_of == k, 0.0, old) - change

    o_ref[...] = lax.dot_general(
        l_ref[...],
        b_ref[...],
        (((1,), (1,)), ((), ())),
        precision=HI,
        preferred_element_type=jnp.float32,
    )


def whitened_share(packed, my_beams):
    share, n = my_beams.shape
    return pl.pallas_call(
        factor_body,
        out_shape=jax.ShapeDtypeStruct((n, share), jnp.float32),
        in_specs=[VMEM, VMEM],
        out_specs=VMEM,
        scratch_shapes=[
            pltpu.VMEM((n, n), jnp.float32),
            pltpu.VMEM((TILE, TILE), jnp.float32),
            pltpu.VMEM((n, n), jnp.float32),
        ],
        compiler_params=pltpu.CompilerParams(vmem_limit_bytes=8 << 20),
        cost_estimate=pl.CostEstimate(flops=12 * n**3, bytes_accessed=1 << 20, transcendentals=n),
        name="whitened_share",
    )(packed, my_beams)


def join_body(r_ref, o_ref):
    share = r_ref.shape[2]
    for g in range(r_ref.shape[0]):
        o_ref[:, g * share : (g + 1) * share] = r_ref[g]


def joined(received):
    groups, mine, share = received.shape
    return pl.pallas_call(
        join_body,
        out_shape=jax.ShapeDtypeStruct((mine, groups * share), jnp.float32),
        in_specs=[VMEM],
        out_specs=VMEM,
        compiler_params=pltpu.CompilerParams(vmem_limit_bytes=3 << 20),
        name="joined",
    )(received)


def local(samples, taps_weight, retain):
    row_count = samples.shape[0]
    groups, blocks = (lax.axis_size("elem"), lax.axis_size("tm"))
    group = lax.axis_index("elem").reshape(1).astype(jnp.int32)
    share = row_count // groups
    half = share // 2
    with jax.named_scope("halo"):
        halo = shifted(samples[row_count - LEAD :], "tm", 1)
    args = (group, halo, samples, taps_weight, retain)
    down, up, far_down, far_up = fir(
        (-1, -3, 1, 3, 4), (2 * share, 2 * share, half, half), False, *args
    )
    with jax.named_scope("beams_near"):
        down, up = (ring(down, -1), ring(up, 1))
        far_down, far_up = (ring(far_down, -2), ring(far_up, 2))
    keep, weight, stats = fir((0, -2, 2), (3 * share,), True, *args)
    low, high = relay_sums(keep, down, up, far_down, far_up)
    with jax.named_scope("beams_far"):
        low, high = (ring(low, -2), ring(high, 2))
    my_beams, packed = packed_gram(keep, down, up, low, high, weight)
    with jax.named_scope("gram_sum"):
        parts = lax.all_to_all(
            packed.reshape(groups, packed.shape[0] // groups, TILE), "elem", 0, 0
        )
    spread = spread_share(parts, stats, blocks)
    with jax.named_scope("blocks_out"):
        received = lax.all_to_all(spread, "tm", 0, 0, tiled=True)
    estimate = decayed(received)
    with jax.named_scope("blocks_back"):
        returned = lax.all_to_all(estimate, "tm", 0, 0, tiled=True)
    with jax.named_scope("gram_gather"):
        packed_estimate = lax.all_to_all(replicated(returned, groups), "elem", 0, 0)
    mine = whitened_share(packed_estimate, my_beams)
    with jax.named_scope("whitened_out"):
        pieces = lax.all_to_all(mine.reshape(groups, mine.shape[0] // groups, share), "elem", 0, 0)
    return joined(pieces)


def solution(mesh):
    placed = (P("tm", "elem"), P(None, "elem", None), P("tm"))
    return jax.shard_map(
        local, mesh=mesh, in_specs=placed, out_specs=P("elem", "tm"), check_vma=False
    )
```

```python
import jax
import jax.numpy as jnp
from jax import lax
from jax.experimental import pallas as pl
from jax.experimental.pallas import tpu as pltpu
from jax.sharding import PartitionSpec as P

loading_level = 0.1
HI = lax.Precision.HIGHEST
TILE = 128
VMEM = pl.BlockSpec(memory_space=pltpu.VMEM)
SMEM = pl.BlockSpec(memory_space=pltpu.SMEM)


def shifted(array, axis, by):
    size = lax.axis_size(axis)
    pairs = [(i, i + by) for i in range(size) if 0 <= i + by < size]
    return lax.ppermute(array, axis, pairs)


LEAD = 16
SPLIT = 4


def fir_body(offsets, weights, group_ref, halo_ref, x_hbm, w_hbm, *refs):
    if weights:
        retain_ref, refs = (refs[0], refs[1:])
    held = 2 if weights else 6
    outs, (xe_ref, part_ref, *own) = (refs[:-held], refs[-held:])
    taps, width, beams = w_hbm.shape
    rows = x_hbm.shape[0]
    groups = 8
    share = rows // groups
    each = taps // SPLIT
    copies = []
    if weights:
        xb_ref, wv_ref = (x_hbm, w_hbm)
    else:
        xb_ref, wv_ref, x_sem, w_sem = own
        copy_x = pltpu.make_async_copy(x_hbm, xb_ref, x_sem)
        copy_x.start()
        for q in range(SPLIT):
            span = pl.ds(q * each, each)
            copies.append(pltpu.make_async_copy(w_hbm.at[span], wv_ref.at[span], w_sem.at[q]))
            copies[-1].start()
    group = group_ref[0]
    if weights:
        weights_of(group, groups, retain_ref, outs[-2], outs[-1])
        outs = outs[:-2]
    xe_ref[:LEAD, :] = halo_ref[...].astype(jnp.float32)
    if not weights:
        copy_x.wait()
    xe_ref[LEAD:, :] = xb_ref[...].astype(jnp.float32)
    tall = share + LEAD
    for i, by in enumerate(offsets):
        chunk = lax.rem(group + (by + groups), groups)
        part_ref[i * tall : (i + 1) * tall, :] = xe_ref[
            pl.ds(pl.multiple_of(chunk * share, 8), tall), :
        ]
    total = None
    for q in range(SPLIT):
        if not weights:
            copies[q].wait()
        window = jnp.concatenate(
            [
                jnp.concatenate(
                    [
                        part_ref[i * tall + LEAD - k : (i + 1) * tall - k, :]
                        for i in range(len(offsets))
                    ],
                    0,
                ).astype(jnp.bfloat16)
                for k in range(q * each, (q + 1) * each)
            ],
            1,
        )
        product = jnp.dot(
            window,
            wv_ref[q * each : (q + 1) * each].reshape(each * width, beams),
            preferred_element_type=jnp.float32,
        )
        at = 0
        for o_ref in outs:
            tall_o = o_ref.shape[0]
            piece = product[at : at + tall_o]
            o_ref[...] = piece if q == 0 else o_ref[...] + piece
            at += tall_o


def weights_of(group, groups, retain_ref, weight_ref, stats_ref):
    rows = retain_ref.shape[0]
    share = rows // groups
    logs = jnp.log(retain_ref[...].reshape(1, rows))
    lane = lax.broadcasted_iota(jnp.int32, (share, rows), 1)
    row = lax.broadcasted_iota(jnp.int32, (share, rows), 0)
    spread = jnp.broadcast_to(logs, (share, rows))

    def weight_at(first):
        later = jnp.where(lane > row + first, spread, 0.0)
        return jnp.exp(jnp.sum(later, axis=1, keepdims=True))

    mass = jnp.zeros((1, 1), jnp.float32)
    for g in range(groups):
        mass = mass + jnp.sum(weight_at(g * share), axis=0, keepdims=True)
    weight_ref[...] = jnp.broadcast_to(weight_at(group * share), weight_ref.shape)
    log_total = jnp.sum(logs, axis=1, keepdims=True)
    at = lax.broadcasted_iota(jnp.int32, stats_ref.shape, 1)
    stats_ref[...] = jnp.where(
        at == 0,
        jnp.broadcast_to(log_total, stats_ref.shape),
        jnp.broadcast_to(mass, stats_ref.shape),
    )


def fir(offsets, heights, weights, group, halo, samples, taps_weight, retain):
    rows, width = samples.shape
    taps, _, beams = taps_weight.shape
    share = rows // 8
    tall = share + LEAD
    shapes = [jax.ShapeDtypeStruct((h, beams), jnp.float32) for h in heights]
    if weights:
        shapes.append(jax.ShapeDtypeStruct((share, TILE), jnp.float32))
        shapes.append(jax.ShapeDtypeStruct((1, TILE), jnp.float32))
    large = VMEM if weights else pl.BlockSpec(memory_space=pltpu.HBM)
    scratch = [
        pltpu.VMEM((rows + LEAD, width), jnp.float32),
        pltpu.VMEM((tall * len(offsets), width), jnp.float32),
    ]
    if not weights:
        scratch += [
            pltpu.VMEM((rows, width), samples.dtype),
            pltpu.VMEM(taps_weight.shape, taps_weight.dtype),
            pltpu.SemaphoreType.DMA,
            pltpu.SemaphoreType.DMA((SPLIT,)),
        ]
    return pl.pallas_call(
        lambda *refs: fir_body(offsets, weights, *refs),
        out_shape=shapes,
        in_specs=[SMEM, VMEM, large, large] + [VMEM] * weights,
        out_specs=[VMEM] * len(shapes),
        scratch_shapes=scratch,
        compiler_params=pltpu.CompilerParams(vmem_limit_bytes=(16 if weights else 60) << 20),
        cost_estimate=pl.CostEstimate(
            flops=2 * share * len(offsets) * taps * width * beams,
            bytes_accessed=6 << 20,
            transcendentals=0,
        ),
        name="fir_rest" if weights else "fir_sent",
    )(group, halo, samples, taps_weight, *([retain] if weights else []))


def ring(array, by):
    size = lax.axis_size("elem")
    return lax.ppermute(array, "elem", [(i, (i + by) % size) for i in range(size)])


def relay_body(keep_ref, down_ref, up_ref, far_down_ref, far_up_ref, low_ref, high_ref):
    share = low_ref.shape[0]
    half = share // 2
    low = keep_ref[share : 2 * share, :] + down_ref[share:, :]
    low_ref[:half, :] = low[:half] + far_down_ref[...]
    low_ref[half:, :] = low[half:]
    high = keep_ref[2 * share :, :] + up_ref[share:, :]
    high_ref[:half, :] = high[:half]
    high_ref[half:, :] = high[half:] + far_up_ref[...]


def relay_sums(keep, down, up, far_down, far_up):
    shape = jax.ShapeDtypeStruct((keep.shape[0] // 3, keep.shape[1]), jnp.float32)
    return pl.pallas_call(
        relay_body,
        out_shape=(shape, shape),
        in_specs=[VMEM] * 5,
        out_specs=(VMEM, VMEM),
        compiler_params=pltpu.CompilerParams(vmem_limit_bytes=5 << 20),
        name="relay_sums",
    )(keep, down, up, far_down, far_up)


def gram_body(keep_ref, down_ref, up_ref, low_ref, high_ref, weight_ref, b_ref, o_ref):
    share, beams = b_ref.shape
    b_ref[...] = (
        (keep_ref[:share, :] + down_ref[:share, :])
        + (up_ref[:share, :] + low_ref[...])
        + high_ref[...]
    )
    weighted = b_ref[...] * jnp.concatenate([weight_ref[...]] * (beams // TILE), 1)
    at = 0
    for r in range(0, beams, TILE):
        part = lax.dot_general(
            weighted[:, r : r + TILE],
            b_ref[:, r:],
            (((0,), (0,)), ((), ())),
            precision=HI,
            preferred_element_type=jnp.float32,
        )
        for c in range(0, beams - r, TILE):
            o_ref[at : at + TILE, :] = part[:, c : c + TILE]
            at += TILE


def packed_gram(keep, down, up, low, high, weight):
    share, beams = low.shape
    n = beams // TILE
    return pl.pallas_call(
        gram_body,
        out_shape=(
            jax.ShapeDtypeStruct((share, beams), jnp.float32),
            jax.ShapeDtypeStruct((n * (n + 1) // 2 * TILE, TILE), jnp.float32),
        ),
        in_specs=[VMEM] * 6,
        out_specs=(VMEM, VMEM),
        compiler_params=pltpu.CompilerParams(vmem_limit_bytes=6 << 20),
        name="packed_gram",
    )(keep, down, up, low, high, weight)


def share_body(stats_ref, p_ref, b_ref, o_ref, c_ref):
    c_ref[...] = b_ref[...]
    groups, rows, _ = p_ref.shape
    ways = o_ref.shape[0]
    total = p_ref[0]
    for g in range(1, groups):
        total = total + p_ref[g]
    tiles = rows // ways
    for s in range(tiles):
        o_ref[:, s, :] = total[s * ways : (s + 1) * ways, :]
    o_ref[:, tiles, :] = jnp.broadcast_to(stats_ref[...], (ways, TILE))


def spread_share(parts, stats, my_beams, ways):
    groups, rows, _ = parts.shape
    return pl.pallas_call(
        share_body,
        out_shape=(
            jax.ShapeDtypeStruct((ways, rows // ways + 1, TILE), jnp.float32),
            jax.ShapeDtypeStruct(my_beams.shape, jnp.float32),
        ),
        in_specs=[VMEM] * 3,
        out_specs=(VMEM, VMEM),
        compiler_params=pltpu.CompilerParams(vmem_limit_bytes=4 << 20),
        name="spread_share",
    )(stats, parts, my_beams)


def decay_body(r_ref, from_below, from_below2, from_above, from_above2, o_ref, low_ref, high_ref):
    share = from_below.shape[0]
    half = share // 2
    low_ref[:share, :] = from_above[...]
    low_ref[share:, :] = from_above2[:half, :]
    high_ref[:share, :] = from_below[...]
    high_ref[share:, :] = from_below2[half:, :]
    n, tiles, _ = r_ref.shape
    tiles -= 1
    stats = r_ref[:, tiles, :]
    logs = stats[:, 0:1]
    row = lax.broadcasted_iota(jnp.int32, (n, n), 0)
    col = lax.broadcasted_iota(jnp.int32, (n, n), 1)
    upto = jnp.where(col <= row, 1.0, 0.0)
    later = jnp.where(row > col, jnp.broadcast_to(logs, (n, n)), 0.0)
    span = jnp.dot(upto, later, precision=HI, preferred_element_type=jnp.float32)
    factor = jnp.where(col <= row, jnp.exp(jnp.where(col <= row, span, 0.0)), 0.0)
    count = jnp.dot(factor, stats, precision=HI, preferred_element_type=jnp.float32)[:, 1:2]
    gram = jnp.dot(
        factor,
        jnp.concatenate([r_ref[:, s, :] for s in range(tiles)], 1),
        precision=HI,
        preferred_element_type=jnp.float32,
    )
    gram = gram / count
    for s in range(tiles):
        o_ref[:, s, :] = gram[:, s * TILE : (s + 1) * TILE]


def decayed(received, *near):
    n, tiles, _ = received.shape
    share, beams = near[0].shape
    packed = jax.ShapeDtypeStruct((share + share // 2, beams), jnp.float32)
    return pl.pallas_call(
        decay_body,
        out_shape=(jax.ShapeDtypeStruct((n, tiles - 1, TILE), jnp.float32), packed, packed),
        in_specs=[VMEM] * 5,
        out_specs=(VMEM,) * 3,
        compiler_params=pltpu.CompilerParams(vmem_limit_bytes=5 << 20),
        name="decayed_sums",
    )(received, *near)


def replicate_body(r_ref, low_ref, high_ref, o_ref):
    ways, tiles, _ = r_ref.shape
    for s in range(tiles):
        piece = r_ref[:, s, :]
        for g in range(o_ref.shape[0]):
            o_ref[g, s * ways : (s + 1) * ways, :] = piece


def replicated(returned, groups, low, high):
    ways, tiles, _ = returned.shape
    return pl.pallas_call(
        replicate_body,
        out_shape=jax.ShapeDtypeStruct((groups, ways * tiles, TILE), jnp.float32),
        in_specs=[VMEM] * 3,
        out_specs=VMEM,
        compiler_params=pltpu.CompilerParams(vmem_limit_bytes=4 << 20),
        name="replicated",
    )(returned, low, high)


def spread_row(x, r):
    return jnp.broadcast_to(x[r : r + 1, :], x.shape)


def spread_lane(x, at):
    return jnp.broadcast_to(x[:, at : at + 1], x.shape)


def factor_tile(rows):
    lane = lax.broadcasted_iota(jnp.int32, (8, TILE), 1)
    sub = lax.broadcasted_iota(jnp.int32, (8, TILE), 0)
    rows, out, done, n = (list(rows), [], [], len(rows))
    cols = [spread_lane(rows[0], c) for c in range(8)]
    for k in range(n):
        base = 8 * k
        last = k + 1 == n
        after = [] if last else [spread_lane(rows[k], base + 8 + c) for c in range(8)]
        inside = (lane >= base) & (lane < base + 8)
        g = jnp.where(inside, jnp.where(lane - base == sub, 1.0, 0.0), rows[k])
        w = g
        pivots = jnp.ones((8, TILE), jnp.float32)
        inverses = pivots
        for c in range(8):
            pivot = spread_row(cols[c], c)
            inverse = 1.0 / pivot
            other = jnp.where(sub == c, 0.0, cols[c])
            below = jnp.where(sub > c, cols[c], 0.0)
            for s in range(c + 1, 8):
                cols[s] = cols[s] - (other * spread_row(cols[s], c)) * inverse
            scaled = other * inverse
            g = g - scaled * spread_row(g, c)
            w = w - (below * inverse) * spread_row(w, c)
            after = [v - scaled * spread_row(v, c) for v in after]
            pivots = jnp.where(sub == c, pivot, pivots)
            inverses = jnp.where(sub == c, inverse, inverses)
        z = g * inverses
        y = w * lax.rsqrt(pivots)
        out.append(jnp.where(lane < base + 8, y, 0.0))
        if last:
            break
        z_rows = [spread_row(z, c) for c in range(8)]
        panel = (k // 8 + 1) * 8
        far = k + 1 == panel
        done.append((y, jnp.where((lane < base + 8) | (lane >= 8 * panel), y, 0.0)))
        if far:
            block = jnp.concatenate([d[0] for d in done[-8:]], 0)
            right = jnp.concatenate([d[1] for d in done[-8:]], 0)
            rest = jnp.concatenate(rows[panel:], 0)
            change = lax.dot_general(
                block[:, 8 * panel :],
                right,
                (((0,), (0,)), ((), ())),
                precision=HI,
                preferred_element_type=jnp.float32,
            )
            cut = (lax.broadcasted_iota(jnp.int32, change.shape, 1) // 64) == k // 8
            rest = jnp.where(cut, 0.0, rest) - change
            for i in range(panel, n):
                rows[i] = rest[8 * (i - panel) : 8 * (i - panel) + 8, :]
            cols = [spread_lane(rows[k + 1], base + 8 + c) for c in range(8)]
        for i in range(k + 1, panel):
            factors = [spread_lane(rows[i], base + c) for c in range(8)]
            if i == k + 1:
                new = []
                for s in range(8):
                    v = after[s] * inverses
                    m = [factors[c] * spread_row(v, c) for c in range(8)]
                    new.append(spread_lane(rows[i], base + 8 + s) - sum_of(m))
                cols = new
            m = [factors[c] * z_rows[c] for c in range(8)]
            rows[i] = jnp.where(inside, 0.0, rows[i]) - sum_of(m)
    return out


def sum_of(m):
    return ((m[0] + m[1]) + (m[2] + m[3])) + ((m[4] + m[5]) + (m[6] + m[7]))


def factor_body(group_ref, p_ref, *refs):
    *beam_refs, o_ref, s_ref, d_ref, l_ref, b_ref = refs
    groups, high, _ = p_ref.shape
    ways = 32
    tiles = high // ways
    n = s_ref.shape[0]
    count = n // TILE
    blocks = [(r, c) for r in range(count) for c in range(r, count)]
    for g in range(groups):
        for s in range(tiles):
            first = (g * tiles + s) * ways
            r, c = blocks[first // TILE]
            top = r * TILE + first % TILE
            piece = p_ref[g, s * ways : (s + 1) * ways, :]
            if r == c:
                row = lax.broadcasted_iota(jnp.int32, piece.shape, 0) + first % TILE
                lane = lax.broadcasted_iota(jnp.int32, piece.shape, 1)
                piece = piece + jnp.where(row == lane, loading_level, 0.0)
            s_ref[top : top + ways, c * TILE : (c + 1) * TILE] = piece
    for r in range(count):
        for c in range(r):
            s_ref[r * TILE : (r + 1) * TILE, c * TILE : (c + 1) * TILE] = jnp.zeros(
                (TILE, TILE), jnp.float32
            )
    tile_of = lax.broadcasted_iota(jnp.int32, (TILE, n), 1) // TILE

    @pl.loop(0, count)
    def _(k):
        first = pl.multiple_of(k * TILE, TILE)
        d_ref[...] = s_ref[pl.ds(first, TILE), pl.ds(first, TILE)]
        rows = factor_tile([d_ref[i : i + 8, :] for i in range(0, TILE, 8)])
        for i in range(TILE // 8):
            d_ref[8 * i : 8 * i + 8, :] = rows[i]
        x = d_ref[...]
        y = jnp.dot(x, s_ref[pl.ds(first, TILE), :], precision=HI, preferred_element_type=jnp.float32)
        y = jnp.where(tile_of == k, jnp.concatenate([x] * count, 1), y)
        l_ref[pl.ds(first, TILE), :] = jnp.where(tile_of <= k, y, 0.0)
        for i in range(1, count):

            @pl.when(i > k)
            def _():
                change = lax.dot_general(
                    y[:, i * TILE : (i + 1) * TILE],
                    y,
                    (((0,), (0,)), ((), ())),
                    precision=HI,
                    preferred_element_type=jnp.float32,
                )
                old = s_ref[i * TILE : (i + 1) * TILE, :]
                s_ref[i * TILE : (i + 1) * TILE, :] = jnp.where(tile_of == k, 0.0, old) - change

    place_beams(group_ref[0], groups, beam_refs, b_ref)
    mine = o_ref.shape[0]
    o_ref[...] = lax.dot_general(
        l_ref[pl.ds(pl.multiple_of(group_ref[0] * mine, 8), mine), :],
        b_ref[...],
        (((1,), (1,)), ((), ())),
        precision=HI,
        preferred_element_type=jnp.float32,
    )


def place_beams(group, groups, beam_refs, b_ref):
    own, below, below2, above, above2, low, high = beam_refs
    share = own.shape[0]
    half = share // 2

    def put(by, at, values):
        owner = lax.rem(group + (by + groups), groups)
        first = pl.multiple_of(owner * share + at, 8)
        b_ref[pl.ds(first, values.shape[0]), :] = values

    put(0, 0, own[...])
    put(1, 0, above[...])
    put(2, 0, above2[...])
    put(3, 0, low[:share, :])
    put(4, 0, low[share:, :])
    put(4, half, high[share:, :])
    put(-3, 0, high[:share, :])
    put(-2, 0, below2[...])
    put(-1, 0, below[...])


def whitened_rows(group, packed, *beams):
    share, n = beams[0].shape
    groups = packed.shape[0]
    return pl.pallas_call(
        factor_body,
        out_shape=jax.ShapeDtypeStruct((n // groups, groups * share), jnp.float32),
        in_specs=[SMEM] + [VMEM] * 8,
        out_specs=VMEM,
        scratch_shapes=[
            pltpu.VMEM((n, n), jnp.float32),
            pltpu.VMEM((TILE, TILE), jnp.float32),
            pltpu.VMEM((n, n), jnp.float32),
            pltpu.VMEM((groups * share, n), jnp.float32),
        ],
        compiler_params=pltpu.CompilerParams(vmem_limit_bytes=14 << 20),
        cost_estimate=pl.CostEstimate(flops=12 * n**3, bytes_accessed=1 << 20, transcendentals=n),
        name="whitened_rows",
    )(group, packed, *beams)


def local(samples, taps_weight, retain):
    row_count = samples.shape[0]
    groups, blocks = (lax.axis_size("elem"), lax.axis_size("tm"))
    group = lax.axis_index("elem").reshape(1).astype(jnp.int32)
    share = row_count // groups
    half = share // 2
    with jax.named_scope("halo"):
        halo = shifted(samples[row_count - LEAD :], "tm", 1)
    args = (group, halo, samples, taps_weight, retain)
    down, up, far_down, far_up = fir(
        (-1, -3, 1, 3, 4), (2 * share, 2 * share, half, half), False, *args
    )
    with jax.named_scope("beams_near"):
        down, up = (ring(down, -1), ring(up, 1))
        far_down, far_up = (ring(far_down, -2), ring(far_up, 2))
    keep, weight, stats = fir((0, -2, 2), (3 * share,), True, *args)
    low, high = relay_sums(keep, down, up, far_down, far_up)
    with jax.named_scope("beams_far"):
        low, high = (ring(low, -2), ring(high, 2))
    my_beams, packed = packed_gram(keep, down, up, low, high, weight)
    with jax.named_scope("gram_sum"):
        parts = lax.all_to_all(
            packed.reshape(groups, packed.shape[0] // groups, TILE), "elem", 0, 0
        )
    spread, own = spread_share(parts, stats, my_beams, blocks)
    with jax.named_scope("beams_gather"):
        below, above = (ring(own, 1), ring(own, -1))
        below2, above2 = (ring(own, 2), ring(own, -2))
    with jax.named_scope("blocks_out"):
        received = lax.all_to_all(spread, "tm", 0, 0, tiled=True)
    estimate, low, high = decayed(received, below, below2, above, above2)
    with jax.named_scope("beams_gather"):
        low, high = (ring(low, -2), ring(high, 2))
    with jax.named_scope("blocks_back"):
        returned = lax.all_to_all(estimate, "tm", 0, 0, tiled=True)
    with jax.named_scope("gram_gather"):
        packed_estimate = lax.all_to_all(
            replicated(returned, groups, low, high), "elem", 0, 0
        )
    return whitened_rows(
        group, packed_estimate, own, below, below2, above, above2, low, high
    )


def solution(mesh):
    placed = (P("tm", "elem"), P(None, "elem", None), P("tm"))
    return jax.shard_map(
        local, mesh=mesh, in_specs=placed, out_specs=P("elem", "tm"), check_vma=False
    )
```

```python
import jax
import jax.numpy as jnp
from jax import lax
from jax.experimental import pallas as pl
from jax.experimental.pallas import tpu as pltpu
from jax.sharding import PartitionSpec as P

loading_level = 0.1
HI = lax.Precision.HIGHEST
TILE = 128
VMEM = pl.BlockSpec(memory_space=pltpu.VMEM)
SMEM = pl.BlockSpec(memory_space=pltpu.SMEM)


def shifted(array, axis, by):
    size = lax.axis_size(axis)
    pairs = [(i, i + by) for i in range(size) if 0 <= i + by < size]
    return lax.ppermute(array, axis, pairs)


LEAD = 16
SPLIT = 4


def fir_body(offsets, weights, group_ref, halo_ref, x_hbm, w_hbm, *refs):
    if weights:
        retain_ref, refs = (refs[0], refs[1:])
    held = 2 if weights else 6
    outs, (xe_ref, part_ref, *own) = (refs[:-held], refs[-held:])
    taps, width, beams = w_hbm.shape
    rows = x_hbm.shape[0]
    groups = 8
    share = rows // groups
    each = taps // SPLIT
    copies = []
    if weights:
        xb_ref, wv_ref = (x_hbm, w_hbm)
    else:
        xb_ref, wv_ref, x_sem, w_sem = own
        copy_x = pltpu.make_async_copy(x_hbm, xb_ref, x_sem)
        copy_x.start()
        for q in range(SPLIT):
            span = pl.ds(q * each, each)
            copies.append(pltpu.make_async_copy(w_hbm.at[span], wv_ref.at[span], w_sem.at[q]))
            copies[-1].start()
    group = group_ref[0]
    if weights:
        weights_of(group, groups, retain_ref, outs[-2], outs[-1])
        outs = outs[:-2]
    xe_ref[:LEAD, :] = halo_ref[...].astype(jnp.float32)
    if not weights:
        copy_x.wait()
    xe_ref[LEAD:, :] = xb_ref[...].astype(jnp.float32)
    tall = share + LEAD
    for i, by in enumerate(offsets):
        chunk = lax.rem(group + (by + groups), groups)
        part_ref[i * tall : (i + 1) * tall, :] = xe_ref[
            pl.ds(pl.multiple_of(chunk * share, 8), tall), :
        ]
    total = None
    for q in range(SPLIT):
        if not weights:
            copies[q].wait()
        window = jnp.concatenate(
            [
                jnp.concatenate(
                    [
                        part_ref[i * tall + LEAD - k : (i + 1) * tall - k, :]
                        for i in range(len(offsets))
                    ],
                    0,
                ).astype(jnp.bfloat16)
                for k in range(q * each, (q + 1) * each)
            ],
            1,
        )
        product = jnp.dot(
            window,
            wv_ref[q * each : (q + 1) * each].reshape(each * width, beams),
            preferred_element_type=jnp.float32,
        )
        at = 0
        for o_ref in outs:
            tall_o = o_ref.shape[0]
            piece = product[at : at + tall_o]
            o_ref[...] = piece if q == 0 else o_ref[...] + piece
            at += tall_o


def weights_of(group, groups, retain_ref, weight_ref, stats_ref):
    rows = retain_ref.shape[0]
    share = rows // groups
    logs = jnp.log(retain_ref[...].reshape(1, rows))
    lane = lax.broadcasted_iota(jnp.int32, (share, rows), 1)
    row = lax.broadcasted_iota(jnp.int32, (share, rows), 0)
    spread = jnp.broadcast_to(logs, (share, rows))

    def weight_at(first):
        later = jnp.where(lane > row + first, spread, 0.0)
        return jnp.exp(jnp.sum(later, axis=1, keepdims=True))

    mass = jnp.zeros((1, 1), jnp.float32)
    for g in range(groups):
        mass = mass + jnp.sum(weight_at(g * share), axis=0, keepdims=True)
    weight_ref[...] = jnp.broadcast_to(weight_at(group * share), weight_ref.shape)
    log_total = jnp.sum(logs, axis=1, keepdims=True)
    at = lax.broadcasted_iota(jnp.int32, stats_ref.shape, 1)
    stats_ref[...] = jnp.where(
        at == HALF,
        jnp.broadcast_to(log_total, stats_ref.shape),
        jnp.broadcast_to(mass, stats_ref.shape),
    )


def fir(offsets, heights, weights, group, halo, samples, taps_weight, retain):
    rows, width = samples.shape
    taps, _, beams = taps_weight.shape
    share = rows // 8
    tall = share + LEAD
    shapes = [jax.ShapeDtypeStruct((h, beams), jnp.float32) for h in heights]
    if weights:
        shapes.append(jax.ShapeDtypeStruct((share, TILE), jnp.float32))
        shapes.append(jax.ShapeDtypeStruct((1, TILE), jnp.float32))
    large = VMEM if weights else pl.BlockSpec(memory_space=pltpu.HBM)
    scratch = [
        pltpu.VMEM((rows + LEAD, width), jnp.float32),
        pltpu.VMEM((tall * len(offsets), width), jnp.float32),
    ]
    if not weights:
        scratch += [
            pltpu.VMEM((rows, width), samples.dtype),
            pltpu.VMEM(taps_weight.shape, taps_weight.dtype),
            pltpu.SemaphoreType.DMA,
            pltpu.SemaphoreType.DMA((SPLIT,)),
        ]
    return pl.pallas_call(
        lambda *refs: fir_body(offsets, weights, *refs),
        out_shape=shapes,
        in_specs=[SMEM, VMEM, large, large] + [VMEM] * weights,
        out_specs=[VMEM] * len(shapes),
        scratch_shapes=scratch,
        compiler_params=pltpu.CompilerParams(vmem_limit_bytes=(16 if weights else 60) << 20),
        cost_estimate=pl.CostEstimate(
            flops=2 * share * len(offsets) * taps * width * beams,
            bytes_accessed=6 << 20,
            transcendentals=0,
        ),
        name="fir_rest" if weights else "fir_sent",
    )(group, halo, samples, taps_weight, *([retain] if weights else []))


def ring(array, by):
    size = lax.axis_size("elem")
    return lax.ppermute(array, "elem", [(i, (i + by) % size) for i in range(size)])


def relay_body(keep_ref, down_ref, up_ref, far_down_ref, far_up_ref, low_ref, high_ref):
    share = low_ref.shape[0]
    half = share // 2
    low = keep_ref[share : 2 * share, :] + down_ref[share:, :]
    low_ref[:half, :] = low[:half] + far_down_ref[...]
    low_ref[half:, :] = low[half:]
    high = keep_ref[2 * share :, :] + up_ref[share:, :]
    high_ref[:half, :] = high[:half]
    high_ref[half:, :] = high[half:] + far_up_ref[...]


def relay_sums(keep, down, up, far_down, far_up):
    shape = jax.ShapeDtypeStruct((keep.shape[0] // 3, keep.shape[1]), jnp.float32)
    return pl.pallas_call(
        relay_body,
        out_shape=(shape, shape),
        in_specs=[VMEM] * 5,
        out_specs=(VMEM, VMEM),
        compiler_params=pltpu.CompilerParams(vmem_limit_bytes=5 << 20),
        name="relay_sums",
    )(keep, down, up, far_down, far_up)


def gram_body(keep_ref, down_ref, up_ref, low_ref, high_ref, weight_ref, b_ref, o_ref):
    share, beams = b_ref.shape
    b_ref[...] = (
        (keep_ref[:share, :] + down_ref[:share, :])
        + (up_ref[:share, :] + low_ref[...])
        + high_ref[...]
    )
    weighted = b_ref[...] * jnp.concatenate([weight_ref[...]] * (beams // TILE), 1)
    n = beams // TILE
    places = packing(n)
    lane = lax.broadcasted_iota(jnp.int32, (HALF, TILE), 1)
    corner = None
    for r in range(n):
        part = lax.dot_general(
            weighted[:, r * TILE : (r + 1) * TILE],
            b_ref[:, r * TILE :],
            (((0,), (0,)), ((), ())),
            precision=HI,
            preferred_element_type=jnp.float32,
        )
        for c in range(r + 1, n):
            at = places[r, c]
            o_ref[at : at + TILE, :] = part[:, (c - r) * TILE : (c - r + 1) * TILE]
        at, low = places[r, r]
        o_ref[at : at + HALF, :] = part[:HALF, :TILE]
        if r % 2 == 0:
            corner = pltpu.roll(part[HALF:, :TILE], HALF, 1)
        else:
            o_ref[low : low + HALF, :] = jnp.where(lane < HALF, corner, part[HALF:, :TILE])


HALF = TILE // 2


def packing(n):
    places, at = ({}, 0)
    for r in range(n):
        for c in range(r + 1, n):
            places[r, c] = at
            at += TILE
    for r in range(n):
        places[r, r] = (at + r * HALF, at + n * HALF + r // 2 * HALF)
    return places


def packed_rows(n):
    return (n * (n - 1) // 2) * TILE + n * HALF + n // 2 * HALF


def packed_gram(keep, down, up, low, high, weight):
    share, beams = low.shape
    n = beams // TILE
    return pl.pallas_call(
        gram_body,
        out_shape=(
            jax.ShapeDtypeStruct((share, beams), jnp.float32),
            jax.ShapeDtypeStruct((packed_rows(n), TILE), jnp.float32),
        ),
        in_specs=[VMEM] * 6,
        out_specs=(VMEM, VMEM),
        compiler_params=pltpu.CompilerParams(vmem_limit_bytes=6 << 20),
        name="packed_gram",
    )(keep, down, up, low, high, weight)


def share_body(stats_ref, p_ref, b_ref, o_ref, c_ref):
    c_ref[...] = b_ref[...]
    groups, rows, _ = p_ref.shape
    ways = o_ref.shape[0]
    total = p_ref[0]
    for g in range(1, groups):
        total = total + p_ref[g]
    tiles = rows // ways
    for s in range(tiles):
        o_ref[:, s, :] = total[s * ways : (s + 1) * ways, :]
    rest = total[tiles * ways :, :]
    lane = lax.broadcasted_iota(jnp.int32, (ways, TILE), 1)
    rest = jnp.concatenate([rest, pltpu.roll(rest, HALF, 1)], 0)
    o_ref[:, tiles, :] = jnp.where(lane < HALF, rest, stats_ref[...])


def spread_share(parts, stats, my_beams, ways):
    groups, rows, _ = parts.shape
    return pl.pallas_call(
        share_body,
        out_shape=(
            jax.ShapeDtypeStruct((ways, rows // ways + 1, TILE), jnp.float32),
            jax.ShapeDtypeStruct(my_beams.shape, jnp.float32),
        ),
        in_specs=[VMEM] * 3,
        out_specs=(VMEM, VMEM),
        compiler_params=pltpu.CompilerParams(vmem_limit_bytes=4 << 20),
        name="spread_share",
    )(stats, parts, my_beams)


def decay_body(r_ref, from_below, from_below2, from_above, from_above2, o_ref, low_ref, high_ref):
    share = from_below.shape[0]
    half = share // 2
    low_ref[:share, :] = from_above[...]
    low_ref[share:, :] = from_above2[:half, :]
    high_ref[:share, :] = from_below[...]
    high_ref[share:, :] = from_below2[half:, :]
    n, tiles, _ = r_ref.shape
    stats = r_ref[:, tiles - 1, :]
    logs = stats[:, HALF : HALF + 1]
    row = lax.broadcasted_iota(jnp.int32, (n, n), 0)
    col = lax.broadcasted_iota(jnp.int32, (n, n), 1)
    upto = jnp.where(col <= row, 1.0, 0.0)
    later = jnp.where(row > col, jnp.broadcast_to(logs, (n, n)), 0.0)
    span = jnp.dot(upto, later, precision=HI, preferred_element_type=jnp.float32)
    factor = jnp.where(col <= row, jnp.exp(jnp.where(col <= row, span, 0.0)), 0.0)
    count = jnp.dot(factor, stats, precision=HI, preferred_element_type=jnp.float32)[
        :, HALF + 1 : HALF + 2
    ]
    gram = jnp.dot(
        factor,
        jnp.concatenate([r_ref[:, s, :] for s in range(tiles)], 1),
        precision=HI,
        preferred_element_type=jnp.float32,
    )
    gram = gram / count
    for s in range(tiles):
        o_ref[:, s, :] = gram[:, s * TILE : (s + 1) * TILE]


def decayed(received, *near):
    n, tiles, _ = received.shape
    share, beams = near[0].shape
    packed = jax.ShapeDtypeStruct((share + share // 2, beams), jnp.float32)
    return pl.pallas_call(
        decay_body,
        out_shape=(jax.ShapeDtypeStruct((n, tiles, TILE), jnp.float32), packed, packed),
        in_specs=[VMEM] * 5,
        out_specs=(VMEM,) * 3,
        compiler_params=pltpu.CompilerParams(vmem_limit_bytes=5 << 20),
        name="decayed_sums",
    )(received, *near)


def replicate_body(r_ref, low_ref, high_ref, o_ref):
    ways, tiles, _ = r_ref.shape
    half = ways // 2
    tiles -= 1
    last = r_ref[:, tiles, :]
    lane = lax.broadcasted_iota(jnp.int32, (half, TILE), 1)
    last = jnp.where(lane < HALF, last[:half, :], pltpu.roll(last[half:, :], HALF, 1))
    for g in range(o_ref.shape[0]):
        for s in range(tiles):
            o_ref[g, s * ways : (s + 1) * ways, :] = r_ref[:, s, :]
        o_ref[g, tiles * ways :, :] = last


def replicated(returned, groups, low, high):
    ways, tiles, _ = returned.shape
    return pl.pallas_call(
        replicate_body,
        out_shape=jax.ShapeDtypeStruct((groups, ways * tiles - ways // 2, TILE), jnp.float32),
        in_specs=[VMEM] * 3,
        out_specs=VMEM,
        compiler_params=pltpu.CompilerParams(vmem_limit_bytes=4 << 20),
        name="replicated",
    )(returned, low, high)


def spread_row(x, r):
    return jnp.broadcast_to(x[r : r + 1, :], x.shape)


def spread_lane(x, at):
    return jnp.broadcast_to(x[:, at : at + 1], x.shape)


def factor_tile(rows):
    lane = lax.broadcasted_iota(jnp.int32, (8, TILE), 1)
    sub = lax.broadcasted_iota(jnp.int32, (8, TILE), 0)
    rows, out, done, n = (list(rows), [], [], len(rows))
    cols = [spread_lane(rows[0], c) for c in range(8)]
    for k in range(n):
        base = 8 * k
        last = k + 1 == n
        after = [] if last else [spread_lane(rows[k], base + 8 + c) for c in range(8)]
        inside = (lane >= base) & (lane < base + 8)
        g = jnp.where(inside, jnp.where(lane - base == sub, 1.0, 0.0), rows[k])
        w = g
        pivots = jnp.ones((8, TILE), jnp.float32)
        inverses = pivots
        for c in range(8):
            pivot = spread_row(cols[c], c)
            inverse = 1.0 / pivot
            other = jnp.where(sub == c, 0.0, cols[c])
            below = jnp.where(sub > c, cols[c], 0.0)
            for s in range(c + 1, 8):
                cols[s] = cols[s] - (other * spread_row(cols[s], c)) * inverse
            scaled = other * inverse
            g = g - scaled * spread_row(g, c)
            w = w - (below * inverse) * spread_row(w, c)
            after = [v - scaled * spread_row(v, c) for v in after]
            pivots = jnp.where(sub == c, pivot, pivots)
            inverses = jnp.where(sub == c, inverse, inverses)
        z = g * inverses
        y = w * lax.rsqrt(pivots)
        out.append(jnp.where(lane < base + 8, y, 0.0))
        if last:
            break
        z_rows = [spread_row(z, c) for c in range(8)]
        panel = (k // 8 + 1) * 8
        far = k + 1 == panel
        done.append((y, jnp.where((lane < base + 8) | (lane >= 8 * panel), y, 0.0)))
        if far:
            block = jnp.concatenate([d[0] for d in done[-8:]], 0)
            right = jnp.concatenate([d[1] for d in done[-8:]], 0)
            rest = jnp.concatenate(rows[panel:], 0)
            change = lax.dot_general(
                block[:, 8 * panel :],
                right,
                (((0,), (0,)), ((), ())),
                precision=HI,
                preferred_element_type=jnp.float32,
            )
            cut = (lax.broadcasted_iota(jnp.int32, change.shape, 1) // 64) == k // 8
            rest = jnp.where(cut, 0.0, rest) - change
            for i in range(panel, n):
                rows[i] = rest[8 * (i - panel) : 8 * (i - panel) + 8, :]
            cols = [spread_lane(rows[k + 1], base + 8 + c) for c in range(8)]
        for i in range(k + 1, panel):
            factors = [spread_lane(rows[i], base + c) for c in range(8)]
            if i == k + 1:
                new = []
                for s in range(8):
                    v = after[s] * inverses
                    m = [factors[c] * spread_row(v, c) for c in range(8)]
                    new.append(spread_lane(rows[i], base + 8 + s) - sum_of(m))
                cols = new
            m = [factors[c] * z_rows[c] for c in range(8)]
            rows[i] = jnp.where(inside, 0.0, rows[i]) - sum_of(m)
    return out


def sum_of(m):
    return ((m[0] + m[1]) + (m[2] + m[3])) + ((m[4] + m[5]) + (m[6] + m[7]))


def factor_body(group_ref, p_ref, *refs):
    *beam_refs, o_ref, s_ref, d_ref, l_ref, b_ref = refs
    groups, high, _ = p_ref.shape
    n = s_ref.shape[0]
    count = n // TILE
    unit = 16
    lane = lax.broadcasted_iota(jnp.int32, (unit, TILE), 1)
    row = lax.broadcasted_iota(jnp.int32, (unit, TILE), 0)

    def loaded(r, c, at, piece):
        if r == c:
            piece = piece + jnp.where(row + at == lane, loading_level, 0.0)
        s_ref[r * TILE + at : r * TILE + at + unit, c * TILE : (c + 1) * TILE] = piece

    def pieces(first, tall):
        for at in range(0, tall, unit):
            g, at_row = divmod(first + at, high)
            yield at, p_ref[g, at_row : at_row + unit, :]

    for (r, c), first in packing(count).items():
        if r != c:
            for at, piece in pieces(first, TILE):
                loaded(r, c, at, piece)
        else:
            for at, piece in pieces(first[0], HALF):
                loaded(r, r, at, piece)
            for at, piece in pieces(first[1], HALF):
                if r % 2 == 0:
                    piece = pltpu.roll(piece, HALF, 1)
                loaded(r, r, HALF + at, jnp.where(lane < HALF, 0.0, piece))
    for r in range(count):
        for c in range(r):
            s_ref[r * TILE : (r + 1) * TILE, c * TILE : (c + 1) * TILE] = jnp.zeros(
                (TILE, TILE), jnp.float32
            )
    tile_of = lax.broadcasted_iota(jnp.int32, (TILE, n), 1) // TILE

    @pl.loop(0, count)
    def _(k):
        first = pl.multiple_of(k * TILE, TILE)
        d_ref[...] = s_ref[pl.ds(first, TILE), pl.ds(first, TILE)]
        rows = factor_tile([d_ref[i : i + 8, :] for i in range(0, TILE, 8)])
        for i in range(TILE // 8):
            d_ref[8 * i : 8 * i + 8, :] = rows[i]
        x = d_ref[...]
        y = jnp.dot(x, s_ref[pl.ds(first, TILE), :], precision=HI, preferred_element_type=jnp.float32)
        y = jnp.where(tile_of == k, jnp.concatenate([x] * count, 1), y)
        l_ref[pl.ds(first, TILE), :] = jnp.where(tile_of <= k, y, 0.0)
        for i in range(1, count):

            @pl.when(i > k)
            def _():
                change = lax.dot_general(
                    y[:, i * TILE : (i + 1) * TILE],
                    y,
                    (((0,), (0,)), ((), ())),
                    precision=HI,
                    preferred_element_type=jnp.float32,
                )
                old = s_ref[i * TILE : (i + 1) * TILE, :]
                s_ref[i * TILE : (i + 1) * TILE, :] = jnp.where(tile_of == k, 0.0, old) - change

    place_beams(group_ref[0], groups, beam_refs, b_ref)
    mine = o_ref.shape[0]
    o_ref[...] = lax.dot_general(
        l_ref[pl.ds(pl.multiple_of(group_ref[0] * mine, 8), mine), :],
        b_ref[...],
        (((1,), (1,)), ((), ())),
        precision=HI,
        preferred_element_type=jnp.float32,
    )


def place_beams(group, groups, beam_refs, b_ref):
    own, below, below2, above, above2, low, high = beam_refs
    share = own.shape[0]
    half = share // 2

    def put(by, at, values):
        owner = lax.rem(group + (by + groups), groups)
        first = pl.multiple_of(owner * share + at, 8)
        b_ref[pl.ds(first, values.shape[0]), :] = values

    put(0, 0, own[...])
    put(1, 0, above[...])
    put(2, 0, above2[...])
    put(3, 0, low[:share, :])
    put(4, 0, low[share:, :])
    put(4, half, high[share:, :])
    put(-3, 0, high[:share, :])
    put(-2, 0, below2[...])
    put(-1, 0, below[...])


def whitened_rows(group, packed, *beams):
    share, n = beams[0].shape
    groups = packed.shape[0]
    return pl.pallas_call(
        factor_body,
        out_shape=jax.ShapeDtypeStruct((n // groups, groups * share), jnp.float32),
        in_specs=[SMEM] + [VMEM] * 8,
        out_specs=VMEM,
        scratch_shapes=[
            pltpu.VMEM((n, n), jnp.float32),
            pltpu.VMEM((TILE, TILE), jnp.float32),
            pltpu.VMEM((n, n), jnp.float32),
            pltpu.VMEM((groups * share, n), jnp.float32),
        ],
        compiler_params=pltpu.CompilerParams(vmem_limit_bytes=14 << 20),
        cost_estimate=pl.CostEstimate(flops=12 * n**3, bytes_accessed=1 << 20, transcendentals=n),
        name="whitened_rows",
    )(group, packed, *beams)


def local(samples, taps_weight, retain):
    row_count = samples.shape[0]
    groups, blocks = (lax.axis_size("elem"), lax.axis_size("tm"))
    group = lax.axis_index("elem").reshape(1).astype(jnp.int32)
    share = row_count // groups
    half = share // 2
    with jax.named_scope("halo"):
        halo = shifted(samples[row_count - LEAD :], "tm", 1)
    args = (group, halo, samples, taps_weight, retain)
    down, up, far_down, far_up = fir(
        (-1, -3, 1, 3, 4), (2 * share, 2 * share, half, half), False, *args
    )
    with jax.named_scope("beams_near"):
        down, up = (ring(down, -1), ring(up, 1))
        far_down, far_up = (ring(far_down, -2), ring(far_up, 2))
    keep, weight, stats = fir((0, -2, 2), (3 * share,), True, *args)
    low, high = relay_sums(keep, down, up, far_down, far_up)
    with jax.named_scope("beams_far"):
        low, high = (ring(low, -2), ring(high, 2))
    my_beams, packed = packed_gram(keep, down, up, low, high, weight)
    with jax.named_scope("gram_sum"):
        parts = lax.all_to_all(
            packed.reshape(groups, packed.shape[0] // groups, TILE), "elem", 0, 0
        )
    spread, own = spread_share(parts, stats, my_beams, blocks)
    with jax.named_scope("beams_gather"):
        below, above = (ring(own, 1), ring(own, -1))
        below2, above2 = (ring(own, 2), ring(own, -2))
    with jax.named_scope("blocks_out"):
        received = lax.all_to_all(spread, "tm", 0, 0, tiled=True)
    estimate, low, high = decayed(received, below, below2, above, above2)
    with jax.named_scope("beams_gather"):
        low, high = (ring(low, -2), ring(high, 2))
    with jax.named_scope("blocks_back"):
        returned = lax.all_to_all(estimate, "tm", 0, 0, tiled=True)
    with jax.named_scope("gram_gather"):
        packed_estimate = lax.all_to_all(
            replicated(returned, groups, low, high), "elem", 0, 0
        )
    return whitened_rows(
        group, packed_estimate, own, below, below2, above, above2, low, high
    )


def solution(mesh):
    placed = (P("tm", "elem"), P(None, "elem", None), P("tm"))
    return jax.shard_map(
        local, mesh=mesh, in_specs=placed, out_specs=P("elem", "tm"), check_vma=False
    )
```

```python
import jax
import jax.numpy as jnp
from jax import lax
from jax.experimental import pallas as pl
from jax.experimental.pallas import tpu as pltpu
from jax.sharding import PartitionSpec as P

loading_level = 0.1
HI = lax.Precision.HIGHEST
TILE = 128
VMEM = pl.BlockSpec(memory_space=pltpu.VMEM)
SMEM = pl.BlockSpec(memory_space=pltpu.SMEM)


def shifted(array, axis, by):
    size = lax.axis_size(axis)
    pairs = [(i, i + by) for i in range(size) if 0 <= i + by < size]
    return lax.ppermute(array, axis, pairs)


LEAD = 16


def widen_body(x_ref, w_ref, xe_ref):
    xe_ref[...] = x_ref[...].astype(jnp.float32)


def widened(samples, taps_weight):
    return pl.pallas_call(
        widen_body,
        out_shape=jax.ShapeDtypeStruct(samples.shape, jnp.float32),
        in_specs=[VMEM, VMEM],
        out_specs=VMEM,
        compiler_params=pltpu.CompilerParams(vmem_limit_bytes=24 << 20),
        cost_estimate=pl.CostEstimate(flops=0, bytes_accessed=12 << 20, transcendentals=0),
        name="widened",
    )(samples, taps_weight)


def fir_body(offsets, weights, group_ref, halo_ref, x_ref, w_ref, *refs):
    if weights:
        retain_ref, refs = (refs[0], refs[1:])
    outs, (xe_ref, part_ref) = (refs[:-2], refs[-2:])
    taps, width, beams = w_ref.shape
    rows = x_ref.shape[0]
    groups = 8
    share = rows // groups
    group = group_ref[0]
    if weights:
        weights_of(group, groups, retain_ref, outs[-2], outs[-1])
        outs = outs[:-2]
    xe_ref[:LEAD, :] = halo_ref[...].astype(jnp.float32)
    xe_ref[LEAD:, :] = x_ref[...]
    tall = share + LEAD
    for i, by in enumerate(offsets):
        chunk = lax.rem(group + (by + groups), groups)
        part_ref[i * tall : (i + 1) * tall, :] = xe_ref[
            pl.ds(pl.multiple_of(chunk * share, 8), tall), :
        ]
    window = jnp.concatenate(
        [
            jnp.concatenate(
                [
                    part_ref[i * tall + LEAD - k : (i + 1) * tall - k, :]
                    for i in range(len(offsets))
                ],
                0,
            ).astype(jnp.bfloat16)
            for k in range(taps)
        ],
        1,
    )
    product = jnp.dot(
        window, w_ref[...].reshape(taps * width, beams), preferred_element_type=jnp.float32
    )
    at = 0
    for o_ref in outs:
        o_ref[...] = product[at : at + o_ref.shape[0]]
        at += o_ref.shape[0]


def weights_of(group, groups, retain_ref, weight_ref, stats_ref):
    rows = retain_ref.shape[0]
    share = rows // groups
    logs = jnp.log(retain_ref[...].reshape(1, rows))
    lane = lax.broadcasted_iota(jnp.int32, (share, rows), 1)
    row = lax.broadcasted_iota(jnp.int32, (share, rows), 0)
    spread = jnp.broadcast_to(logs, (share, rows))

    def weight_at(first):
        later = jnp.where(lane > row + first, spread, 0.0)
        return jnp.exp(jnp.sum(later, axis=1, keepdims=True))

    mass = jnp.zeros((1, 1), jnp.float32)
    for g in range(groups):
        mass = mass + jnp.sum(weight_at(g * share), axis=0, keepdims=True)
    weight_ref[...] = jnp.broadcast_to(weight_at(group * share), weight_ref.shape)
    log_total = jnp.sum(logs, axis=1, keepdims=True)
    at = lax.broadcasted_iota(jnp.int32, stats_ref.shape, 1)
    stats_ref[...] = jnp.where(
        at == HALF,
        jnp.broadcast_to(log_total, stats_ref.shape),
        jnp.broadcast_to(mass, stats_ref.shape),
    )


def fir(offsets, heights, weights, group, halo, wide, taps_weight, retain):
    rows, width = wide.shape
    taps, _, beams = taps_weight.shape
    share = rows // 8
    tall = share + LEAD
    shapes = [jax.ShapeDtypeStruct((h, beams), jnp.float32) for h in heights]
    if weights:
        shapes.append(jax.ShapeDtypeStruct((share, TILE), jnp.float32))
        shapes.append(jax.ShapeDtypeStruct((1, TILE), jnp.float32))
    return pl.pallas_call(
        lambda *refs: fir_body(offsets, weights, *refs),
        out_shape=shapes,
        in_specs=[SMEM, VMEM, VMEM, VMEM] + [VMEM] * weights,
        out_specs=[VMEM] * len(shapes),
        scratch_shapes=[
            pltpu.VMEM((rows + LEAD, width), jnp.float32),
            pltpu.VMEM((tall * len(offsets), width), jnp.float32),
        ],
        compiler_params=pltpu.CompilerParams(vmem_limit_bytes=24 << 20),
        cost_estimate=pl.CostEstimate(
            flops=2 * share * len(offsets) * taps * width * beams,
            bytes_accessed=6 << 20,
            transcendentals=0,
        ),
        name="fir_rest" if weights else "fir_sent",
    )(group, halo, wide, taps_weight, *([retain] if weights else []))


def ring(array, by):
    size = lax.axis_size("elem")
    return lax.ppermute(array, "elem", [(i, (i + by) % size) for i in range(size)])


def relay_body(keep_ref, down_ref, up_ref, far_down_ref, far_up_ref, low_ref, high_ref):
    share = low_ref.shape[0]
    half = share // 2
    low = keep_ref[share : 2 * share, :] + down_ref[share:, :]
    low_ref[:half, :] = low[:half] + far_down_ref[...]
    low_ref[half:, :] = low[half:]
    high = keep_ref[2 * share :, :] + up_ref[share:, :]
    high_ref[:half, :] = high[:half]
    high_ref[half:, :] = high[half:] + far_up_ref[...]


def relay_sums(keep, down, up, far_down, far_up):
    shape = jax.ShapeDtypeStruct((keep.shape[0] // 3, keep.shape[1]), jnp.float32)
    return pl.pallas_call(
        relay_body,
        out_shape=(shape, shape),
        in_specs=[VMEM] * 5,
        out_specs=(VMEM, VMEM),
        compiler_params=pltpu.CompilerParams(vmem_limit_bytes=5 << 20),
        name="relay_sums",
    )(keep, down, up, far_down, far_up)


def gram_body(keep_ref, down_ref, up_ref, low_ref, high_ref, weight_ref, b_ref, o_ref):
    share, beams = b_ref.shape
    b_ref[...] = (
        (keep_ref[:share, :] + down_ref[:share, :])
        + (up_ref[:share, :] + low_ref[...])
        + high_ref[...]
    )
    weighted = b_ref[...] * jnp.concatenate([weight_ref[...]] * (beams // TILE), 1)
    n = beams // TILE
    places = packing(n)
    lane = lax.broadcasted_iota(jnp.int32, (HALF, TILE), 1)
    corner = None
    for r in range(n):
        part = lax.dot_general(
            weighted[:, r * TILE : (r + 1) * TILE],
            b_ref[:, r * TILE :],
            (((0,), (0,)), ((), ())),
            precision=HI,
            preferred_element_type=jnp.float32,
        )
        for c in range(r + 1, n):
            at = places[r, c]
            o_ref[at : at + TILE, :] = part[:, (c - r) * TILE : (c - r + 1) * TILE]
        at, low = places[r, r]
        o_ref[at : at + HALF, :] = part[:HALF, :TILE]
        if r % 2 == 0:
            corner = pltpu.roll(part[HALF:, :TILE], HALF, 1)
        else:
            o_ref[low : low + HALF, :] = jnp.where(lane < HALF, corner, part[HALF:, :TILE])


HALF = TILE // 2


def packing(n):
    places, at = ({}, 0)
    for r in range(n):
        for c in range(r + 1, n):
            places[r, c] = at
            at += TILE
    for r in range(n):
        places[r, r] = (at + r * HALF, at + n * HALF + r // 2 * HALF)
    return places


def packed_rows(n):
    return (n * (n - 1) // 2) * TILE + n * HALF + n // 2 * HALF


def packed_gram(keep, down, up, low, high, weight):
    share, beams = low.shape
    n = beams // TILE
    return pl.pallas_call(
        gram_body,
        out_shape=(
            jax.ShapeDtypeStruct((share, beams), jnp.float32),
            jax.ShapeDtypeStruct((packed_rows(n), TILE), jnp.float32),
        ),
        in_specs=[VMEM] * 6,
        out_specs=(VMEM, VMEM),
        compiler_params=pltpu.CompilerParams(vmem_limit_bytes=6 << 20),
        name="packed_gram",
    )(keep, down, up, low, high, weight)


def share_body(stats_ref, p_ref, b_ref, o_ref, c_ref):
    c_ref[...] = b_ref[...]
    groups, rows, _ = p_ref.shape
    ways = o_ref.shape[0]
    total = p_ref[0]
    for g in range(1, groups):
        total = total + p_ref[g]
    tiles = rows // ways
    for s in range(tiles):
        o_ref[:, s, :] = total[s * ways : (s + 1) * ways, :]
    rest = total[tiles * ways :, :]
    lane = lax.broadcasted_iota(jnp.int32, (ways, TILE), 1)
    rest = jnp.concatenate([rest, pltpu.roll(rest, HALF, 1)], 0)
    o_ref[:, tiles, :] = jnp.where(lane < HALF, rest, stats_ref[...])


def spread_share(parts, stats, my_beams, ways):
    groups, rows, _ = parts.shape
    return pl.pallas_call(
        share_body,
        out_shape=(
            jax.ShapeDtypeStruct((ways, rows // ways + 1, TILE), jnp.float32),
            jax.ShapeDtypeStruct(my_beams.shape, jnp.float32),
        ),
        in_specs=[VMEM] * 3,
        out_specs=(VMEM, VMEM),
        compiler_params=pltpu.CompilerParams(vmem_limit_bytes=4 << 20),
        name="spread_share",
    )(stats, parts, my_beams)


def decay_body(r_ref, from_below, from_below2, from_above, from_above2, o_ref, low_ref, high_ref):
    share = from_below.shape[0]
    half = share // 2
    low_ref[:share, :] = from_above[...]
    low_ref[share:, :] = from_above2[:half, :]
    high_ref[:share, :] = from_below[...]
    high_ref[share:, :] = from_below2[half:, :]
    n, tiles, _ = r_ref.shape
    stats = r_ref[:, tiles - 1, :]
    logs = stats[:, HALF : HALF + 1]
    row = lax.broadcasted_iota(jnp.int32, (n, n), 0)
    col = lax.broadcasted_iota(jnp.int32, (n, n), 1)
    upto = jnp.where(col <= row, 1.0, 0.0)
    later = jnp.where(row > col, jnp.broadcast_to(logs, (n, n)), 0.0)
    span = jnp.dot(upto, later, precision=HI, preferred_element_type=jnp.float32)
    factor = jnp.where(col <= row, jnp.exp(jnp.where(col <= row, span, 0.0)), 0.0)
    count = jnp.dot(factor, stats, precision=HI, preferred_element_type=jnp.float32)[
        :, HALF + 1 : HALF + 2
    ]
    gram = jnp.dot(
        factor,
        jnp.concatenate([r_ref[:, s, :] for s in range(tiles)], 1),
        precision=HI,
        preferred_element_type=jnp.float32,
    )
    gram = gram / count
    for s in range(tiles):
        o_ref[:, s, :] = gram[:, s * TILE : (s + 1) * TILE]


def decayed(received, *near):
    n, tiles, _ = received.shape
    share, beams = near[0].shape
    packed = jax.ShapeDtypeStruct((share + share // 2, beams), jnp.float32)
    return pl.pallas_call(
        decay_body,
        out_shape=(jax.ShapeDtypeStruct((n, tiles, TILE), jnp.float32), packed, packed),
        in_specs=[VMEM] * 5,
        out_specs=(VMEM,) * 3,
        compiler_params=pltpu.CompilerParams(vmem_limit_bytes=5 << 20),
        name="decayed_sums",
    )(received, *near)


def replicate_body(r_ref, low_ref, high_ref, o_ref):
    ways, tiles, _ = r_ref.shape
    half = ways // 2
    tiles -= 1
    last = r_ref[:, tiles, :]
    lane = lax.broadcasted_iota(jnp.int32, (half, TILE), 1)
    last = jnp.where(lane < HALF, last[:half, :], pltpu.roll(last[half:, :], HALF, 1))
    for g in range(o_ref.shape[0]):
        for s in range(tiles):
            o_ref[g, s * ways : (s + 1) * ways, :] = r_ref[:, s, :]
        o_ref[g, tiles * ways :, :] = last


def replicated(returned, groups, low, high):
    ways, tiles, _ = returned.shape
    return pl.pallas_call(
        replicate_body,
        out_shape=jax.ShapeDtypeStruct((groups, ways * tiles - ways // 2, TILE), jnp.float32),
        in_specs=[VMEM] * 3,
        out_specs=VMEM,
        compiler_params=pltpu.CompilerParams(vmem_limit_bytes=4 << 20),
        name="replicated",
    )(returned, low, high)


def spread_row(x, r):
    return jnp.broadcast_to(x[r : r + 1, :], x.shape)


def spread_lane(x, at):
    return jnp.broadcast_to(x[:, at : at + 1], x.shape)


def factor_tile(rows):
    lane = lax.broadcasted_iota(jnp.int32, (8, TILE), 1)
    sub = lax.broadcasted_iota(jnp.int32, (8, TILE), 0)
    rows, out, done, n = (list(rows), [], [], len(rows))
    cols = [spread_lane(rows[0], c) for c in range(8)]
    for k in range(n):
        base = 8 * k
        last = k + 1 == n
        after = [] if last else [spread_lane(rows[k], base + 8 + c) for c in range(8)]
        inside = (lane >= base) & (lane < base + 8)
        g = jnp.where(inside, jnp.where(lane - base == sub, 1.0, 0.0), rows[k])
        w = g
        pivots = jnp.ones((8, TILE), jnp.float32)
        inverses = pivots
        for c in range(8):
            pivot = spread_row(cols[c], c)
            inverse = 1.0 / pivot
            other = jnp.where(sub == c, 0.0, cols[c])
            below = jnp.where(sub > c, cols[c], 0.0)
            for s in range(c + 1, 8):
                cols[s] = cols[s] - (other * spread_row(cols[s], c)) * inverse
            scaled = other * inverse
            g = g - scaled * spread_row(g, c)
            w = w - (below * inverse) * spread_row(w, c)
            after = [v - scaled * spread_row(v, c) for v in after]
            pivots = jnp.where(sub == c, pivot, pivots)
            inverses = jnp.where(sub == c, inverse, inverses)
        z = g * inverses
        y = w * lax.rsqrt(pivots)
        out.append(jnp.where(lane < base + 8, y, 0.0))
        if last:
            break
        z_rows = [spread_row(z, c) for c in range(8)]
        panel = (k // 8 + 1) * 8
        far = k + 1 == panel
        done.append((y, jnp.where((lane < base + 8) | (lane >= 8 * panel), y, 0.0)))
        if far:
            block = jnp.concatenate([d[0] for d in done[-8:]], 0)
            right = jnp.concatenate([d[1] for d in done[-8:]], 0)
            rest = jnp.concatenate(rows[panel:], 0)
            change = lax.dot_general(
                block[:, 8 * panel :],
                right,
                (((0,), (0,)), ((), ())),
                precision=HI,
                preferred_element_type=jnp.float32,
            )
            cut = (lax.broadcasted_iota(jnp.int32, change.shape, 1) // 64) == k // 8
            rest = jnp.where(cut, 0.0, rest) - change
            for i in range(panel, n):
                rows[i] = rest[8 * (i - panel) : 8 * (i - panel) + 8, :]
            cols = [spread_lane(rows[k + 1], base + 8 + c) for c in range(8)]
        for i in range(k + 1, panel):
            factors = [spread_lane(rows[i], base + c) for c in range(8)]
            if i == k + 1:
                new = []
                for s in range(8):
                    v = after[s] * inverses
                    m = [factors[c] * spread_row(v, c) for c in range(8)]
                    new.append(spread_lane(rows[i], base + 8 + s) - sum_of(m))
                cols = new
            m = [factors[c] * z_rows[c] for c in range(8)]
            rows[i] = jnp.where(inside, 0.0, rows[i]) - sum_of(m)
    return out


def sum_of(m):
    return ((m[0] + m[1]) + (m[2] + m[3])) + ((m[4] + m[5]) + (m[6] + m[7]))


def factor_body(group_ref, p_ref, *refs):
    *beam_refs, o_ref, s_ref, d_ref, l_ref, b_ref = refs
    groups, high, _ = p_ref.shape
    n = s_ref.shape[0]
    count = n // TILE
    unit = 16
    lane = lax.broadcasted_iota(jnp.int32, (unit, TILE), 1)
    row = lax.broadcasted_iota(jnp.int32, (unit, TILE), 0)

    def loaded(r, c, at, piece):
        if r == c:
            piece = piece + jnp.where(row + at == lane, loading_level, 0.0)
        s_ref[r * TILE + at : r * TILE + at + unit, c * TILE : (c + 1) * TILE] = piece

    def pieces(first, tall):
        for at in range(0, tall, unit):
            g, at_row = divmod(first + at, high)
            yield at, p_ref[g, at_row : at_row + unit, :]

    for (r, c), first in packing(count).items():
        if r != c:
            for at, piece in pieces(first, TILE):
                loaded(r, c, at, piece)
        else:
            for at, piece in pieces(first[0], HALF):
                loaded(r, r, at, piece)
            for at, piece in pieces(first[1], HALF):
                if r % 2 == 0:
                    piece = pltpu.roll(piece, HALF, 1)
                loaded(r, r, HALF + at, jnp.where(lane < HALF, 0.0, piece))
    for r in range(count):
        for c in range(r):
            s_ref[r * TILE : (r + 1) * TILE, c * TILE : (c + 1) * TILE] = jnp.zeros(
                (TILE, TILE), jnp.float32
            )
    tile_of = lax.broadcasted_iota(jnp.int32, (TILE, n), 1) // TILE

    def times_transposed(a, b):
        return lax.dot_general(
            a, b, (((0,), (0,)), ((), ())), precision=HI, preferred_element_type=jnp.float32
        )

    tile = s_ref[:TILE, :TILE]
    for k in range(count):
        first = k * TILE
        after = first + TILE
        rows = factor_tile([tile[i : i + 8, :] for i in range(0, TILE, 8)])
        x = jnp.concatenate(rows, 0)
        l_ref[first:after, first:after] = x
        pieces = {k: x}
        for t in [*range(k + 1, count), *range(k)]:
            pieces[t] = jnp.dot(
                x,
                s_ref[first:after, t * TILE : (t + 1) * TILE],
                precision=HI,
                preferred_element_type=jnp.float32,
            )
            if t == k + 1:
                tile = s_ref[after : after + TILE, after : after + TILE] - times_transposed(
                    pieces[t], pieces[t]
                )
            if t < k:
                l_ref[first:after, t * TILE : (t + 1) * TILE] = pieces[t]
        for t in range(k + 1, count):
            l_ref[first:after, t * TILE : (t + 1) * TILE] = jnp.zeros((TILE, TILE), jnp.float32)
        for i in range(k + 1, count):
            for t in range(count):
                if k < t < i or i == t == k + 1:
                    continue
                change = times_transposed(pieces[i], pieces[t])
                span = (slice(i * TILE, (i + 1) * TILE), slice(t * TILE, (t + 1) * TILE))
                s_ref[span] = -change if t == k else s_ref[span] - change

    place_beams(group_ref[0], groups, beam_refs, b_ref)
    mine = o_ref.shape[0]
    left_high, left_low = split(l_ref[pl.ds(pl.multiple_of(group_ref[0] * mine, 8), mine), :])
    right_high, right_low = split(b_ref[...])
    o_ref[...] = (
        product_nt(left_high, right_low) + product_nt(left_low, right_high)
    ) + product_nt(left_high, right_high)


def split(x):
    high = x.astype(jnp.bfloat16)
    return high, (x - high.astype(jnp.float32)).astype(jnp.bfloat16)


def product_nt(a, b):
    return lax.dot_general(a, b, (((1,), (1,)), ((), ())), preferred_element_type=jnp.float32)


def place_beams(group, groups, beam_refs, b_ref):
    own, below, below2, above, above2, low, high = beam_refs
    share = own.shape[0]
    half = share // 2

    def put(by, at, values):
        owner = lax.rem(group + (by + groups), groups)
        first = pl.multiple_of(owner * share + at, 8)
        b_ref[pl.ds(first, values.shape[0]), :] = values

    put(0, 0, own[...])
    put(1, 0, above[...])
    put(2, 0, above2[...])
    put(3, 0, low[:share, :])
    put(4, 0, low[share:, :])
    put(4, half, high[share:, :])
    put(-3, 0, high[:share, :])
    put(-2, 0, below2[...])
    put(-1, 0, below[...])


def whitened_rows(group, packed, *beams):
    share, n = beams[0].shape
    groups = packed.shape[0]
    return pl.pallas_call(
        factor_body,
        out_shape=jax.ShapeDtypeStruct((n // groups, groups * share), jnp.float32),
        in_specs=[SMEM] + [VMEM] * 8,
        out_specs=VMEM,
        scratch_shapes=[
            pltpu.VMEM((n, n), jnp.float32),
            pltpu.VMEM((TILE, TILE), jnp.float32),
            pltpu.VMEM((n, n), jnp.float32),
            pltpu.VMEM((groups * share, n), jnp.float32),
        ],
        compiler_params=pltpu.CompilerParams(vmem_limit_bytes=14 << 20),
        cost_estimate=pl.CostEstimate(flops=12 * n**3, bytes_accessed=1 << 20, transcendentals=n),
        name="whitened_rows",
    )(group, packed, *beams)


def local(samples, taps_weight, retain):
    row_count = samples.shape[0]
    groups, blocks = (lax.axis_size("elem"), lax.axis_size("tm"))
    group = lax.axis_index("elem").reshape(1).astype(jnp.int32)
    share = row_count // groups
    half = share // 2
    with jax.named_scope("halo"):
        halo = shifted(samples[row_count - LEAD :], "tm", 1)
    args = (group, halo, widened(samples, taps_weight), taps_weight, retain)
    down, up, far_down, far_up = fir(
        (-1, -3, 1, 3, 4), (2 * share, 2 * share, half, half), False, *args
    )
    with jax.named_scope("beams_near"):
        down, up = (ring(down, -1), ring(up, 1))
        far_down, far_up = (ring(far_down, -2), ring(far_up, 2))
    keep, weight, stats = fir((0, -2, 2), (3 * share,), True, *args)
    low, high = relay_sums(keep, down, up, far_down, far_up)
    with jax.named_scope("beams_far"):
        low, high = (ring(low, -2), ring(high, 2))
    my_beams, packed = packed_gram(keep, down, up, low, high, weight)
    with jax.named_scope("gram_sum"):
        parts = lax.all_to_all(
            packed.reshape(groups, packed.shape[0] // groups, TILE), "elem", 0, 0
        )
    spread, own = spread_share(parts, stats, my_beams, blocks)
    with jax.named_scope("beams_gather"):
        below, above = (ring(own, 1), ring(own, -1))
        below2, above2 = (ring(own, 2), ring(own, -2))
    with jax.named_scope("blocks_out"):
        received = lax.all_to_all(spread, "tm", 0, 0, tiled=True)
    estimate, low, high = decayed(received, below, below2, above, above2)
    with jax.named_scope("beams_gather"):
        low, high = (ring(low, -2), ring(high, 2))
    with jax.named_scope("blocks_back"):
        returned = lax.all_to_all(estimate, "tm", 0, 0, tiled=True)
    with jax.named_scope("gram_gather"):
        packed_estimate = lax.all_to_all(
            replicated(returned, groups, low, high), "elem", 0, 0
        )
    return whitened_rows(
        group, packed_estimate, own, below, below2, above, above2, low, high
    )


def solution(mesh):
    placed = (P("tm", "elem"), P(None, "elem", None), P("tm"))
    return jax.shard_map(
        local, mesh=mesh, in_specs=placed, out_specs=P("elem", "tm"), check_vma=False
    )
```

```python
import jax
import jax.numpy as jnp
from jax import lax
from jax.experimental import pallas as pl
from jax.experimental.pallas import tpu as pltpu
from jax.sharding import PartitionSpec as P

loading_level = 0.1
HI = lax.Precision.HIGHEST
TILE = 128
VMEM = pl.BlockSpec(memory_space=pltpu.VMEM)
SMEM = pl.BlockSpec(memory_space=pltpu.SMEM)


def shifted(array, axis, by):
    size = lax.axis_size(axis)
    pairs = [(i, i + by) for i in range(size) if 0 <= i + by < size]
    return lax.ppermute(array, axis, pairs)


LEAD = 16
SPLIT = 4


def fir_body(offsets, weights, group_ref, halo_ref, x_hbm, w_hbm, *refs):
    if weights:
        retain_ref, refs = (refs[0], refs[1:])
    held = 2 if weights else 6
    outs, (xe_ref, part_ref, *own) = (refs[:-held], refs[-held:])
    taps, width, beams = w_hbm.shape
    rows = x_hbm.shape[0]
    groups = 8
    share = rows // groups
    each = taps // SPLIT
    copies = []
    if weights:
        xb_ref, wv_ref = (x_hbm, w_hbm)
    else:
        xb_ref, wv_ref, x_sem, w_sem = own
        copy_x = pltpu.make_async_copy(x_hbm, xb_ref, x_sem)
        copy_x.start()
        for q in range(SPLIT):
            span = pl.ds(q * each, each)
            copies.append(pltpu.make_async_copy(w_hbm.at[span], wv_ref.at[span], w_sem.at[q]))
            copies[-1].start()
    group = group_ref[0]
    if weights:
        weights_of(group, groups, retain_ref, outs[-2], outs[-1])
        outs = outs[:-2]
    xe_ref[:LEAD, :] = halo_ref[...].astype(jnp.float32)
    if not weights:
        copy_x.wait()
    xe_ref[LEAD:, :] = xb_ref[...].astype(jnp.float32)
    tall = share + LEAD
    for i, by in enumerate(offsets):
        chunk = lax.rem(group + (by + groups), groups)
        part_ref[i * tall : (i + 1) * tall, :] = xe_ref[
            pl.ds(pl.multiple_of(chunk * share, 8), tall), :
        ]
    total = None
    for q in range(SPLIT):
        if not weights:
            copies[q].wait()
        window = jnp.concatenate(
            [
                jnp.concatenate(
                    [
                        part_ref[i * tall + LEAD - k : (i + 1) * tall - k, :]
                        for i in range(len(offsets))
                    ],
                    0,
                ).astype(jnp.bfloat16)
                for k in range(q * each, (q + 1) * each)
            ],
            1,
        )
        product = jnp.dot(
            window,
            wv_ref[q * each : (q + 1) * each].reshape(each * width, beams),
            preferred_element_type=jnp.float32,
        )
        at = 0
        for o_ref in outs:
            tall_o = o_ref.shape[0]
            piece = product[at : at + tall_o]
            o_ref[...] = piece if q == 0 else o_ref[...] + piece
            at += tall_o


def weights_of(group, groups, retain_ref, weight_ref, stats_ref):
    rows = retain_ref.shape[0]
    share = rows // groups
    logs = jnp.log(retain_ref[...].reshape(1, rows))
    lane = lax.broadcasted_iota(jnp.int32, (share, rows), 1)
    row = lax.broadcasted_iota(jnp.int32, (share, rows), 0)
    spread = jnp.broadcast_to(logs, (share, rows))

    def weight_at(first):
        later = jnp.where(lane > row + first, spread, 0.0)
        return jnp.exp(jnp.sum(later, axis=1, keepdims=True))

    mass = jnp.zeros((1, 1), jnp.float32)
    for g in range(groups):
        mass = mass + jnp.sum(weight_at(g * share), axis=0, keepdims=True)
    weight_ref[...] = jnp.broadcast_to(weight_at(group * share), weight_ref.shape)
    log_total = jnp.sum(logs, axis=1, keepdims=True)
    at = lax.broadcasted_iota(jnp.int32, stats_ref.shape, 1)
    stats_ref[...] = jnp.where(
        at == HALF,
        jnp.broadcast_to(log_total, stats_ref.shape),
        jnp.broadcast_to(mass, stats_ref.shape),
    )


def fir(offsets, heights, weights, group, halo, samples, taps_weight, retain):
    rows, width = samples.shape
    taps, _, beams = taps_weight.shape
    share = rows // 8
    tall = share + LEAD
    shapes = [jax.ShapeDtypeStruct((h, beams), jnp.float32) for h in heights]
    if weights:
        shapes.append(jax.ShapeDtypeStruct((share, TILE), jnp.float32))
        shapes.append(jax.ShapeDtypeStruct((1, TILE), jnp.float32))
    large = VMEM if weights else pl.BlockSpec(memory_space=pltpu.HBM)
    scratch = [
        pltpu.VMEM((rows + LEAD, width), jnp.float32),
        pltpu.VMEM((tall * len(offsets), width), jnp.float32),
    ]
    if not weights:
        scratch += [
            pltpu.VMEM((rows, width), samples.dtype),
            pltpu.VMEM(taps_weight.shape, taps_weight.dtype),
            pltpu.SemaphoreType.DMA,
            pltpu.SemaphoreType.DMA((SPLIT,)),
        ]
    return pl.pallas_call(
        lambda *refs: fir_body(offsets, weights, *refs),
        out_shape=shapes,
        in_specs=[SMEM, VMEM, large, large] + [VMEM] * weights,
        out_specs=[VMEM] * len(shapes),
        scratch_shapes=scratch,
        compiler_params=pltpu.CompilerParams(vmem_limit_bytes=(16 if weights else 60) << 20),
        cost_estimate=pl.CostEstimate(
            flops=2 * share * len(offsets) * taps * width * beams,
            bytes_accessed=6 << 20,
            transcendentals=0,
        ),
        name="fir_rest" if weights else "fir_sent",
    )(group, halo, samples, taps_weight, *([retain] if weights else []))


def ring(array, by):
    size = lax.axis_size("elem")
    return lax.ppermute(array, "elem", [(i, (i + by) % size) for i in range(size)])


def relay_body(keep_ref, down_ref, up_ref, far_down_ref, far_up_ref, low_ref, high_ref):
    share = low_ref.shape[0]
    half = share // 2
    low = keep_ref[share : 2 * share, :] + down_ref[share:, :]
    low_ref[:half, :] = low[:half] + far_down_ref[...]
    low_ref[half:, :] = low[half:]
    high = keep_ref[2 * share :, :] + up_ref[share:, :]
    high_ref[:half, :] = high[:half]
    high_ref[half:, :] = high[half:] + far_up_ref[...]


def relay_sums(keep, down, up, far_down, far_up):
    shape = jax.ShapeDtypeStruct((keep.shape[0] // 3, keep.shape[1]), jnp.float32)
    return pl.pallas_call(
        relay_body,
        out_shape=(shape, shape),
        in_specs=[VMEM] * 5,
        out_specs=(VMEM, VMEM),
        compiler_params=pltpu.CompilerParams(vmem_limit_bytes=5 << 20),
        name="relay_sums",
    )(keep, down, up, far_down, far_up)


def gram_body(keep_ref, down_ref, up_ref, low_ref, high_ref, weight_ref, b_ref, o_ref):
    share, beams = b_ref.shape
    b_ref[...] = (
        (keep_ref[:share, :] + down_ref[:share, :])
        + (up_ref[:share, :] + low_ref[...])
        + high_ref[...]
    )
    weighted = b_ref[...] * jnp.concatenate([weight_ref[...]] * (beams // TILE), 1)
    n = beams // TILE
    places = packing(n)
    lane = lax.broadcasted_iota(jnp.int32, (HALF, TILE), 1)
    corner = None
    for r in range(n):
        part = lax.dot_general(
            weighted[:, r * TILE : (r + 1) * TILE],
            b_ref[:, r * TILE :],
            (((0,), (0,)), ((), ())),
            precision=HI,
            preferred_element_type=jnp.float32,
        )
        for c in range(r + 1, n):
            at = places[r, c]
            o_ref[at : at + TILE, :] = part[:, (c - r) * TILE : (c - r + 1) * TILE]
        at, low = places[r, r]
        o_ref[at : at + HALF, :] = part[:HALF, :TILE]
        if r % 2 == 0:
            corner = pltpu.roll(part[HALF:, :TILE], HALF, 1)
        else:
            o_ref[low : low + HALF, :] = jnp.where(lane < HALF, corner, part[HALF:, :TILE])


HALF = TILE // 2


def packing(n):
    places, at = ({}, 0)
    for r in range(n):
        for c in range(r + 1, n):
            places[r, c] = at
            at += TILE
    for r in range(n):
        places[r, r] = (at + r * HALF, at + n * HALF + r // 2 * HALF)
    return places


def packed_rows(n):
    return (n * (n - 1) // 2) * TILE + n * HALF + n // 2 * HALF


def packed_gram(keep, down, up, low, high, weight):
    share, beams = low.shape
    n = beams // TILE
    return pl.pallas_call(
        gram_body,
        out_shape=(
            jax.ShapeDtypeStruct((share, beams), jnp.float32),
            jax.ShapeDtypeStruct((packed_rows(n), TILE), jnp.float32),
        ),
        in_specs=[VMEM] * 6,
        out_specs=(VMEM, VMEM),
        compiler_params=pltpu.CompilerParams(vmem_limit_bytes=6 << 20),
        name="packed_gram",
    )(keep, down, up, low, high, weight)


def share_body(stats_ref, p_ref, b_ref, o_ref, c_ref):
    c_ref[...] = b_ref[...]
    groups, rows, _ = p_ref.shape
    ways = o_ref.shape[0]
    total = p_ref[0]
    for g in range(1, groups):
        total = total + p_ref[g]
    tiles = rows // ways
    for s in range(tiles):
        o_ref[:, s, :] = total[s * ways : (s + 1) * ways, :]
    rest = total[tiles * ways :, :]
    lane = lax.broadcasted_iota(jnp.int32, (ways, TILE), 1)
    rest = jnp.concatenate([rest, pltpu.roll(rest, HALF, 1)], 0)
    o_ref[:, tiles, :] = jnp.where(lane < HALF, rest, stats_ref[...])


def spread_share(parts, stats, my_beams, ways):
    groups, rows, _ = parts.shape
    return pl.pallas_call(
        share_body,
        out_shape=(
            jax.ShapeDtypeStruct((ways, rows // ways + 1, TILE), jnp.float32),
            jax.ShapeDtypeStruct(my_beams.shape, jnp.float32),
        ),
        in_specs=[VMEM] * 3,
        out_specs=(VMEM, VMEM),
        compiler_params=pltpu.CompilerParams(vmem_limit_bytes=4 << 20),
        name="spread_share",
    )(stats, parts, my_beams)


def decay_body(r_ref, from_below, from_below2, from_above, from_above2, o_ref, low_ref, high_ref):
    share = from_below.shape[0]
    half = share // 2
    low_ref[:share, :] = from_above[...]
    low_ref[share:, :] = from_above2[:half, :]
    high_ref[:share, :] = from_below[...]
    high_ref[share:, :] = from_below2[half:, :]
    n, tiles, _ = r_ref.shape
    stats = r_ref[:, tiles - 1, :]
    logs = stats[:, HALF : HALF + 1]
    row = lax.broadcasted_iota(jnp.int32, (n, n), 0)
    col = lax.broadcasted_iota(jnp.int32, (n, n), 1)
    upto = jnp.where(col <= row, 1.0, 0.0)
    later = jnp.where(row > col, jnp.broadcast_to(logs, (n, n)), 0.0)
    span = jnp.dot(upto, later, precision=HI, preferred_element_type=jnp.float32)
    factor = jnp.where(col <= row, jnp.exp(jnp.where(col <= row, span, 0.0)), 0.0)
    count = jnp.dot(factor, stats, precision=HI, preferred_element_type=jnp.float32)[
        :, HALF + 1 : HALF + 2
    ]
    gram = jnp.dot(
        factor,
        jnp.concatenate([r_ref[:, s, :] for s in range(tiles)], 1),
        precision=HI,
        preferred_element_type=jnp.float32,
    )
    gram = gram / count
    for s in range(tiles):
        o_ref[:, s, :] = gram[:, s * TILE : (s + 1) * TILE]


def decayed(received, *near):
    n, tiles, _ = received.shape
    share, beams = near[0].shape
    packed = jax.ShapeDtypeStruct((share + share // 2, beams), jnp.float32)
    return pl.pallas_call(
        decay_body,
        out_shape=(jax.ShapeDtypeStruct((n, tiles, TILE), jnp.float32), packed, packed),
        in_specs=[VMEM] * 5,
        out_specs=(VMEM,) * 3,
        compiler_params=pltpu.CompilerParams(vmem_limit_bytes=5 << 20),
        name="decayed_sums",
    )(received, *near)


def replicate_body(r_ref, low_ref, high_ref, o_ref):
    ways, tiles, _ = r_ref.shape
    half = ways // 2
    tiles -= 1
    last = r_ref[:, tiles, :]
    lane = lax.broadcasted_iota(jnp.int32, (half, TILE), 1)
    last = jnp.where(lane < HALF, last[:half, :], pltpu.roll(last[half:, :], HALF, 1))
    for g in range(o_ref.shape[0]):
        for s in range(tiles):
            o_ref[g, s * ways : (s + 1) * ways, :] = r_ref[:, s, :]
        o_ref[g, tiles * ways :, :] = last


def replicated(returned, groups, low, high):
    ways, tiles, _ = returned.shape
    return pl.pallas_call(
        replicate_body,
        out_shape=jax.ShapeDtypeStruct((groups, ways * tiles - ways // 2, TILE), jnp.float32),
        in_specs=[VMEM] * 3,
        out_specs=VMEM,
        compiler_params=pltpu.CompilerParams(vmem_limit_bytes=4 << 20),
        name="replicated",
    )(returned, low, high)


def spread_row(x, r):
    return jnp.broadcast_to(x[r : r + 1, :], x.shape)


def spread_lane(x, at):
    return jnp.broadcast_to(x[:, at : at + 1], x.shape)


def factor_tile(rows):
    lane = lax.broadcasted_iota(jnp.int32, (8, TILE), 1)
    sub = lax.broadcasted_iota(jnp.int32, (8, TILE), 0)
    rows, out, done, n = (list(rows), [], [], len(rows))
    cols = [spread_lane(rows[0], c) for c in range(8)]
    for k in range(n):
        base = 8 * k
        last = k + 1 == n
        after = [] if last else [spread_lane(rows[k], base + 8 + c) for c in range(8)]
        inside = (lane >= base) & (lane < base + 8)
        g = jnp.where(inside, jnp.where(lane - base == sub, 1.0, 0.0), rows[k])
        w = g
        pivots = jnp.ones((8, TILE), jnp.float32)
        inverses = pivots
        for c in range(8):
            pivot = spread_row(cols[c], c)
            inverse = 1.0 / pivot
            other = jnp.where(sub == c, 0.0, cols[c])
            below = jnp.where(sub > c, cols[c], 0.0)
            for s in range(c + 1, 8):
                cols[s] = cols[s] - (other * spread_row(cols[s], c)) * inverse
            scaled = other * inverse
            g = g - scaled * spread_row(g, c)
            w = w - (below * inverse) * spread_row(w, c)
            after = [v - scaled * spread_row(v, c) for v in after]
            pivots = jnp.where(sub == c, pivot, pivots)
            inverses = jnp.where(sub == c, inverse, inverses)
        z = g * inverses
        y = w * lax.rsqrt(pivots)
        out.append(jnp.where(lane < base + 8, y, 0.0))
        if last:
            break
        z_rows = [spread_row(z, c) for c in range(8)]
        panel = (k // 8 + 1) * 8
        far = k + 1 == panel
        done.append((y, jnp.where((lane < base + 8) | (lane >= 8 * panel), y, 0.0)))
        if far:
            block = jnp.concatenate([d[0] for d in done[-8:]], 0)
            right = jnp.concatenate([d[1] for d in done[-8:]], 0)
            rest = jnp.concatenate(rows[panel:], 0)
            change = lax.dot_general(
                block[:, 8 * panel :],
                right,
                (((0,), (0,)), ((), ())),
                precision=HI,
                preferred_element_type=jnp.float32,
            )
            cut = (lax.broadcasted_iota(jnp.int32, change.shape, 1) // 64) == k // 8
            rest = jnp.where(cut, 0.0, rest) - change
            for i in range(panel, n):
                rows[i] = rest[8 * (i - panel) : 8 * (i - panel) + 8, :]
            cols = [spread_lane(rows[k + 1], base + 8 + c) for c in range(8)]
        for i in range(k + 1, panel):
            factors = [spread_lane(rows[i], base + c) for c in range(8)]
            if i == k + 1:
                new = []
                for s in range(8):
                    v = after[s] * inverses
                    m = [factors[c] * spread_row(v, c) for c in range(8)]
                    new.append(spread_lane(rows[i], base + 8 + s) - sum_of(m))
                cols = new
            m = [factors[c] * z_rows[c] for c in range(8)]
            rows[i] = jnp.where(inside, 0.0, rows[i]) - sum_of(m)
    return out


def sum_of(m):
    return ((m[0] + m[1]) + (m[2] + m[3])) + ((m[4] + m[5]) + (m[6] + m[7]))


def factor_body(group_ref, p_ref, *refs):
    *beam_refs, o_ref, s_ref, d_ref, l_ref, b_ref = refs
    groups, high, _ = p_ref.shape
    n = s_ref.shape[0]
    count = n // TILE
    unit = 16
    lane = lax.broadcasted_iota(jnp.int32, (unit, TILE), 1)
    row = lax.broadcasted_iota(jnp.int32, (unit, TILE), 0)

    def loaded(r, c, at, piece):
        if r == c:
            piece = piece + jnp.where(row + at == lane, loading_level, 0.0)
        s_ref[r * TILE + at : r * TILE + at + unit, c * TILE : (c + 1) * TILE] = piece

    def pieces(first, tall):
        for at in range(0, tall, unit):
            g, at_row = divmod(first + at, high)
            yield at, p_ref[g, at_row : at_row + unit, :]

    for (r, c), first in packing(count).items():
        if r != c:
            for at, piece in pieces(first, TILE):
                loaded(r, c, at, piece)
        else:
            for at, piece in pieces(first[0], HALF):
                loaded(r, r, at, piece)
            for at, piece in pieces(first[1], HALF):
                if r % 2 == 0:
                    piece = pltpu.roll(piece, HALF, 1)
                loaded(r, r, HALF + at, jnp.where(lane < HALF, 0.0, piece))
    for r in range(count):
        for c in range(r):
            s_ref[r * TILE : (r + 1) * TILE, c * TILE : (c + 1) * TILE] = jnp.zeros(
                (TILE, TILE), jnp.float32
            )
    tile_of = lax.broadcasted_iota(jnp.int32, (TILE, n), 1) // TILE

    def times_transposed(a, b):
        return lax.dot_general(
            a, b, (((0,), (0,)), ((), ())), precision=HI, preferred_element_type=jnp.float32
        )

    tile = s_ref[:TILE, :TILE]
    for k in range(count):
        first = k * TILE
        after = first + TILE
        rows = factor_tile([tile[i : i + 8, :] for i in range(0, TILE, 8)])
        x = jnp.concatenate(rows, 0)
        l_ref[first:after, first:after] = x
        pieces = {k: x}
        for t in [*range(k + 1, count), *range(k)]:
            pieces[t] = jnp.dot(
                x,
                s_ref[first:after, t * TILE : (t + 1) * TILE],
                precision=HI,
                preferred_element_type=jnp.float32,
            )
            if t == k + 1:
                tile = s_ref[after : after + TILE, after : after + TILE] - times_transposed(
                    pieces[t], pieces[t]
                )
            if t < k:
                l_ref[first:after, t * TILE : (t + 1) * TILE] = pieces[t]
        for t in range(k + 1, count):
            l_ref[first:after, t * TILE : (t + 1) * TILE] = jnp.zeros((TILE, TILE), jnp.float32)
        for i in range(k + 1, count):
            for t in range(count):
                if k < t < i or i == t == k + 1:
                    continue
                change = times_transposed(pieces[i], pieces[t])
                span = (slice(i * TILE, (i + 1) * TILE), slice(t * TILE, (t + 1) * TILE))
                s_ref[span] = -change if t == k else s_ref[span] - change

    place_beams(group_ref[0], groups, beam_refs, b_ref)
    mine = o_ref.shape[0]
    left_high, left_low = split(l_ref[pl.ds(pl.multiple_of(group_ref[0] * mine, 8), mine), :])
    right_high, right_low = split(b_ref[...])
    o_ref[...] = (
        product_nt(left_high, right_low) + product_nt(left_low, right_high)
    ) + product_nt(left_high, right_high)


def split(x):
    high = x.astype(jnp.bfloat16)
    return high, (x - high.astype(jnp.float32)).astype(jnp.bfloat16)


def product_nt(a, b):
    return lax.dot_general(a, b, (((1,), (1,)), ((), ())), preferred_element_type=jnp.float32)


def place_beams(group, groups, beam_refs, b_ref):
    own, below, below2, above, above2, low, high = beam_refs
    share = own.shape[0]
    half = share // 2

    def put(by, at, values):
        owner = lax.rem(group + (by + groups), groups)
        first = pl.multiple_of(owner * share + at, 8)
        b_ref[pl.ds(first, values.shape[0]), :] = values

    put(0, 0, own[...])
    put(1, 0, above[...])
    put(2, 0, above2[...])
    put(3, 0, low[:share, :])
    put(4, 0, low[share:, :])
    put(4, half, high[share:, :])
    put(-3, 0, high[:share, :])
    put(-2, 0, below2[...])
    put(-1, 0, below[...])


def whitened_rows(group, packed, *beams):
    share, n = beams[0].shape
    groups = packed.shape[0]
    return pl.pallas_call(
        factor_body,
        out_shape=jax.ShapeDtypeStruct((n // groups, groups * share), jnp.float32),
        in_specs=[SMEM] + [VMEM] * 8,
        out_specs=VMEM,
        scratch_shapes=[
            pltpu.VMEM((n, n), jnp.float32),
            pltpu.VMEM((TILE, TILE), jnp.float32),
            pltpu.VMEM((n, n), jnp.float32),
            pltpu.VMEM((groups * share, n), jnp.float32),
        ],
        compiler_params=pltpu.CompilerParams(vmem_limit_bytes=14 << 20),
        cost_estimate=pl.CostEstimate(flops=12 * n**3, bytes_accessed=1 << 20, transcendentals=n),
        name="whitened_rows",
    )(group, packed, *beams)


def local(samples, taps_weight, retain):
    row_count = samples.shape[0]
    groups, blocks = (lax.axis_size("elem"), lax.axis_size("tm"))
    group = lax.axis_index("elem").reshape(1).astype(jnp.int32)
    share = row_count // groups
    half = share // 2
    with jax.named_scope("halo"):
        halo = shifted(samples[row_count - LEAD :], "tm", 1)
    args = (group, halo, samples, taps_weight, retain)
    down, up, far_down, far_up = fir(
        (-1, -3, 1, 3, 4), (2 * share, 2 * share, half, half), False, *args
    )
    with jax.named_scope("beams_near"):
        down, up = (ring(down, -1), ring(up, 1))
        far_down, far_up = (ring(far_down, -2), ring(far_up, 2))
    keep, weight, stats = fir((0, -2, 2), (3 * share,), True, *args)
    low, high = relay_sums(keep, down, up, far_down, far_up)
    with jax.named_scope("beams_far"):
        low, high = (ring(low, -2), ring(high, 2))
    my_beams, packed = packed_gram(keep, down, up, low, high, weight)
    with jax.named_scope("gram_sum"):
        parts = lax.all_to_all(
            packed.reshape(groups, packed.shape[0] // groups, TILE), "elem", 0, 0
        )
    spread, own = spread_share(parts, stats, my_beams, blocks)
    with jax.named_scope("beams_gather"):
        below, above = (ring(own, 1), ring(own, -1))
        below2, above2 = (ring(own, 2), ring(own, -2))
    with jax.named_scope("blocks_out"):
        received = lax.all_to_all(spread, "tm", 0, 0, tiled=True)
    estimate, low, high = decayed(received, below, below2, above, above2)
    with jax.named_scope("beams_gather"):
        low, high = (ring(low, -2), ring(high, 2))
    with jax.named_scope("blocks_back"):
        returned = lax.all_to_all(estimate, "tm", 0, 0, tiled=True)
    with jax.named_scope("gram_gather"):
        packed_estimate = lax.all_to_all(
            replicated(returned, groups, low, high), "elem", 0, 0
        )
    return whitened_rows(
        group, packed_estimate, own, below, below2, above, above2, low, high
    )


def solution(mesh):
    placed = (P("tm", "elem"), P(None, "elem", None), P("tm"))
    return jax.shard_map(
        local, mesh=mesh, in_specs=placed, out_specs=P("elem", "tm"), check_vma=False
    )
```

```python
import jax
import jax.numpy as jnp
from jax import lax
from jax.experimental import pallas as pl
from jax.experimental.pallas import tpu as pltpu
from jax.sharding import PartitionSpec as P

loading_level = 0.1
HI = lax.Precision.HIGHEST
TILE = 128
VMEM = pl.BlockSpec(memory_space=pltpu.VMEM)
SMEM = pl.BlockSpec(memory_space=pltpu.SMEM)


def shifted(array, axis, by):
    size = lax.axis_size(axis)
    pairs = [(i, i + by) for i in range(size) if 0 <= i + by < size]
    return lax.ppermute(array, axis, pairs)


LEAD = 16


def widen_body(x_ref, w_ref, xe_ref):
    xe_ref[...] = x_ref[...].astype(jnp.float32)


def widened(samples, taps_weight):
    return pl.pallas_call(
        widen_body,
        out_shape=jax.ShapeDtypeStruct(samples.shape, jnp.float32),
        in_specs=[VMEM, VMEM],
        out_specs=VMEM,
        compiler_params=pltpu.CompilerParams(vmem_limit_bytes=24 << 20),
        cost_estimate=pl.CostEstimate(flops=0, bytes_accessed=12 << 20, transcendentals=0),
        name="widened",
    )(samples, taps_weight)


def fir_body(offsets, weights, group_ref, halo_ref, x_ref, w_ref, *refs):
    if weights:
        retain_ref, refs = (refs[0], refs[1:])
    outs, (xe_ref, part_ref) = (refs[:-2], refs[-2:])
    taps, width, beams = w_ref.shape
    rows = x_ref.shape[0]
    groups = 8
    share = rows // groups
    group = group_ref[0]
    if weights:
        weights_of(group, groups, retain_ref, outs[-2], outs[-1])
        outs = outs[:-2]
    xe_ref[:LEAD, :] = halo_ref[...].astype(jnp.float32)
    xe_ref[LEAD:, :] = x_ref[...]
    tall = share + LEAD
    for i, by in enumerate(offsets):
        chunk = lax.rem(group + (by + groups), groups)
        part_ref[i * tall : (i + 1) * tall, :] = xe_ref[
            pl.ds(pl.multiple_of(chunk * share, 8), tall), :
        ]
    window = jnp.concatenate(
        [
            jnp.concatenate(
                [
                    part_ref[i * tall + LEAD - k : (i + 1) * tall - k, :]
                    for i in range(len(offsets))
                ],
                0,
            ).astype(jnp.bfloat16)
            for k in range(taps)
        ],
        1,
    )
    product = jnp.dot(
        window, w_ref[...].reshape(taps * width, beams), preferred_element_type=jnp.float32
    )
    at = 0
    for o_ref in outs:
        o_ref[...] = product[at : at + o_ref.shape[0]]
        at += o_ref.shape[0]


def weights_of(group, groups, retain_ref, weight_ref, stats_ref):
    rows = retain_ref.shape[0]
    share = rows // groups
    logs = jnp.log(retain_ref[...].reshape(1, rows))
    lane = lax.broadcasted_iota(jnp.int32, (share, rows), 1)
    row = lax.broadcasted_iota(jnp.int32, (share, rows), 0)
    spread = jnp.broadcast_to(logs, (share, rows))

    def weight_at(first):
        later = jnp.where(lane > row + first, spread, 0.0)
        return jnp.exp(jnp.sum(later, axis=1, keepdims=True))

    mass = jnp.zeros((1, 1), jnp.float32)
    for g in range(groups):
        mass = mass + jnp.sum(weight_at(g * share), axis=0, keepdims=True)
    weight_ref[...] = jnp.broadcast_to(weight_at(group * share), weight_ref.shape)
    log_total = jnp.sum(logs, axis=1, keepdims=True)
    at = lax.broadcasted_iota(jnp.int32, stats_ref.shape, 1)
    stats_ref[...] = jnp.where(
        at == HALF,
        jnp.broadcast_to(log_total, stats_ref.shape),
        jnp.broadcast_to(mass, stats_ref.shape),
    )


def fir(offsets, heights, weights, group, halo, wide, taps_weight, retain):
    rows, width = wide.shape
    taps, _, beams = taps_weight.shape
    share = rows // 8
    tall = share + LEAD
    place = jax.ShapeDtypeStruct if weights else pltpu.HBM
    shapes = [place((h, beams), jnp.float32) for h in heights]
    if weights:
        shapes.append(jax.ShapeDtypeStruct((share, TILE), jnp.float32))
        shapes.append(jax.ShapeDtypeStruct((1, TILE), jnp.float32))
    return pl.pallas_call(
        lambda *refs: fir_body(offsets, weights, *refs),
        out_shape=shapes,
        in_specs=[SMEM, VMEM, VMEM, VMEM] + [VMEM] * weights,
        out_specs=[VMEM] * len(shapes),
        scratch_shapes=[
            pltpu.VMEM((rows + LEAD, width), jnp.float32),
            pltpu.VMEM((tall * len(offsets), width), jnp.float32),
        ],
        compiler_params=pltpu.CompilerParams(vmem_limit_bytes=24 << 20),
        cost_estimate=pl.CostEstimate(
            flops=2 * share * len(offsets) * taps * width * beams,
            bytes_accessed=6 << 20,
            transcendentals=0,
        ),
        name="fir_rest" if weights else "fir_sent",
    )(group, halo, wide, taps_weight, *([retain] if weights else []))


def ring(array, by):
    size = lax.axis_size("elem")
    return lax.ppermute(array, "elem", [(i, (i + by) % size) for i in range(size)])


def relay_body(keep_ref, down_ref, up_ref, far_down_ref, far_up_ref, low_ref, high_ref):
    share = low_ref.shape[0]
    half = share // 2
    low = keep_ref[share : 2 * share, :] + down_ref[share:, :]
    low_ref[:half, :] = low[:half] + far_down_ref[...]
    low_ref[half:, :] = low[half:]
    high = keep_ref[2 * share :, :] + up_ref[share:, :]
    high_ref[:half, :] = high[:half]
    high_ref[half:, :] = high[half:] + far_up_ref[...]


def relay_sums(keep, down, up, far_down, far_up):
    shape = pltpu.HBM((keep.shape[0] // 3, keep.shape[1]), jnp.float32)
    return pl.pallas_call(
        relay_body,
        out_shape=(shape, shape),
        in_specs=[VMEM] * 5,
        out_specs=(VMEM, VMEM),
        compiler_params=pltpu.CompilerParams(vmem_limit_bytes=5 << 20),
        name="relay_sums",
    )(keep, down, up, far_down, far_up)


def gram_body(keep_ref, down_ref, up_ref, low_ref, high_ref, weight_ref, b_ref, o_ref):
    share, beams = b_ref.shape
    b_ref[...] = (
        (keep_ref[:share, :] + down_ref[:share, :])
        + (up_ref[:share, :] + low_ref[...])
        + high_ref[...]
    )
    weighted = b_ref[...] * jnp.concatenate([weight_ref[...]] * (beams // TILE), 1)
    n = beams // TILE
    places = packing(n)
    lane = lax.broadcasted_iota(jnp.int32, (HALF, TILE), 1)
    corner = None
    for r in range(n):
        part = lax.dot_general(
            weighted[:, r * TILE : (r + 1) * TILE],
            b_ref[:, r * TILE :],
            (((0,), (0,)), ((), ())),
            precision=HI,
            preferred_element_type=jnp.float32,
        )
        for c in range(r + 1, n):
            at = places[r, c]
            o_ref[at : at + TILE, :] = part[:, (c - r) * TILE : (c - r + 1) * TILE]
        at, low = places[r, r]
        o_ref[at : at + HALF, :] = part[:HALF, :TILE]
        if r % 2 == 0:
            corner = pltpu.roll(part[HALF:, :TILE], HALF, 1)
        else:
            o_ref[low : low + HALF, :] = jnp.where(lane < HALF, corner, part[HALF:, :TILE])


HALF = TILE // 2


def packing(n):
    places, at = ({}, 0)
    for r in range(n):
        for c in range(r + 1, n):
            places[r, c] = at
            at += TILE
    for r in range(n):
        places[r, r] = (at + r * HALF, at + n * HALF + r // 2 * HALF)
    return places


def packed_rows(n):
    return (n * (n - 1) // 2) * TILE + n * HALF + n // 2 * HALF


def packed_gram(keep, down, up, low, high, weight):
    share, beams = low.shape
    n = beams // TILE
    return pl.pallas_call(
        gram_body,
        out_shape=(
            jax.ShapeDtypeStruct((share, beams), jnp.float32),
            pltpu.HBM((packed_rows(n), TILE), jnp.float32),
        ),
        in_specs=[VMEM] * 6,
        out_specs=(VMEM, VMEM),
        compiler_params=pltpu.CompilerParams(vmem_limit_bytes=6 << 20),
        name="packed_gram",
    )(keep, down, up, low, high, weight)


def share_body(stats_ref, p_ref, b_ref, o_ref, c_ref):
    c_ref[...] = b_ref[...]
    groups, rows, _ = p_ref.shape
    ways = o_ref.shape[0]
    total = p_ref[0]
    for g in range(1, groups):
        total = total + p_ref[g]
    tiles = rows // ways
    for s in range(tiles):
        o_ref[:, s, :] = total[s * ways : (s + 1) * ways, :]
    rest = total[tiles * ways :, :]
    lane = lax.broadcasted_iota(jnp.int32, (ways, TILE), 1)
    rest = jnp.concatenate([rest, pltpu.roll(rest, HALF, 1)], 0)
    o_ref[:, tiles, :] = jnp.where(lane < HALF, rest, stats_ref[...])


def spread_share(parts, stats, my_beams, ways):
    groups, rows, _ = parts.shape
    return pl.pallas_call(
        share_body,
        out_shape=(
            jax.ShapeDtypeStruct((ways, rows // ways + 1, TILE), jnp.float32),
            jax.ShapeDtypeStruct(my_beams.shape, jnp.float32),
        ),
        in_specs=[VMEM] * 3,
        out_specs=(VMEM, VMEM),
        compiler_params=pltpu.CompilerParams(vmem_limit_bytes=4 << 20),
        name="spread_share",
    )(stats, parts, my_beams)


def decay_body(r_ref, from_below, from_below2, from_above, from_above2, o_ref, low_ref, high_ref):
    share = from_below.shape[0]
    half = share // 2
    low_ref[:share, :] = from_above[...]
    low_ref[share:, :] = from_above2[:half, :]
    high_ref[:share, :] = from_below[...]
    high_ref[share:, :] = from_below2[half:, :]
    n, tiles, _ = r_ref.shape
    stats = r_ref[:, tiles - 1, :]
    logs = stats[:, HALF : HALF + 1]
    row = lax.broadcasted_iota(jnp.int32, (n, n), 0)
    col = lax.broadcasted_iota(jnp.int32, (n, n), 1)
    upto = jnp.where(col <= row, 1.0, 0.0)
    later = jnp.where(row > col, jnp.broadcast_to(logs, (n, n)), 0.0)
    span = jnp.dot(upto, later, precision=HI, preferred_element_type=jnp.float32)
    factor = jnp.where(col <= row, jnp.exp(jnp.where(col <= row, span, 0.0)), 0.0)
    count = jnp.dot(factor, stats, precision=HI, preferred_element_type=jnp.float32)[
        :, HALF + 1 : HALF + 2
    ]
    gram = jnp.dot(
        factor,
        jnp.concatenate([r_ref[:, s, :] for s in range(tiles)], 1),
        precision=HI,
        preferred_element_type=jnp.float32,
    )
    gram = gram / count
    for s in range(tiles):
        o_ref[:, s, :] = gram[:, s * TILE : (s + 1) * TILE]


def decayed(received, *near):
    n, tiles, _ = received.shape
    share, beams = near[0].shape
    packed = jax.ShapeDtypeStruct((share + share // 2, beams), jnp.float32)
    return pl.pallas_call(
        decay_body,
        out_shape=(jax.ShapeDtypeStruct((n, tiles, TILE), jnp.float32), packed, packed),
        in_specs=[VMEM] * 5,
        out_specs=(VMEM,) * 3,
        compiler_params=pltpu.CompilerParams(vmem_limit_bytes=5 << 20),
        name="decayed_sums",
    )(received, *near)


def replicate_body(r_ref, low_ref, high_ref, o_ref):
    ways, tiles, _ = r_ref.shape
    half = ways // 2
    tiles -= 1
    last = r_ref[:, tiles, :]
    lane = lax.broadcasted_iota(jnp.int32, (half, TILE), 1)
    last = jnp.where(lane < HALF, last[:half, :], pltpu.roll(last[half:, :], HALF, 1))
    for g in range(o_ref.shape[0]):
        for s in range(tiles):
            o_ref[g, s * ways : (s + 1) * ways, :] = r_ref[:, s, :]
        o_ref[g, tiles * ways :, :] = last


def replicated(returned, groups, low, high):
    ways, tiles, _ = returned.shape
    return pl.pallas_call(
        replicate_body,
        out_shape=pltpu.HBM((groups, ways * tiles - ways // 2, TILE), jnp.float32),
        in_specs=[VMEM] * 3,
        out_specs=VMEM,
        compiler_params=pltpu.CompilerParams(vmem_limit_bytes=4 << 20),
        name="replicated",
    )(returned, low, high)


def spread_row(x, r):
    return jnp.broadcast_to(x[r : r + 1, :], x.shape)


def spread_lane(x, at):
    return jnp.broadcast_to(x[:, at : at + 1], x.shape)


def factor_tile(rows):
    lane = lax.broadcasted_iota(jnp.int32, (8, TILE), 1)
    sub = lax.broadcasted_iota(jnp.int32, (8, TILE), 0)
    rows, out, done, n = (list(rows), [], [], len(rows))
    cols = [spread_lane(rows[0], c) for c in range(8)]
    for k in range(n):
        base = 8 * k
        last = k + 1 == n
        after = [] if last else [spread_lane(rows[k], base + 8 + c) for c in range(8)]
        inside = (lane >= base) & (lane < base + 8)
        g = jnp.where(inside, jnp.where(lane - base == sub, 1.0, 0.0), rows[k])
        w = g
        pivots = jnp.ones((8, TILE), jnp.float32)
        inverses = pivots
        for c in range(8):
            pivot = spread_row(cols[c], c)
            inverse = 1.0 / pivot
            other = jnp.where(sub == c, 0.0, cols[c])
            below = jnp.where(sub > c, cols[c], 0.0)
            for s in range(c + 1, 8):
                cols[s] = cols[s] - (other * spread_row(cols[s], c)) * inverse
            scaled = other * inverse
            g = g - scaled * spread_row(g, c)
            w = w - (below * inverse) * spread_row(w, c)
            after = [v - scaled * spread_row(v, c) for v in after]
            pivots = jnp.where(sub == c, pivot, pivots)
            inverses = jnp.where(sub == c, inverse, inverses)
        z = g * inverses
        y = w * lax.rsqrt(pivots)
        out.append(jnp.where(lane < base + 8, y, 0.0))
        if last:
            break
        z_rows = [spread_row(z, c) for c in range(8)]
        panel = (k // 8 + 1) * 8
        far = k + 1 == panel
        done.append((y, jnp.where((lane < base + 8) | (lane >= 8 * panel), y, 0.0)))
        if far:
            block = jnp.concatenate([d[0] for d in done[-8:]], 0)
            right = jnp.concatenate([d[1] for d in done[-8:]], 0)
            rest = jnp.concatenate(rows[panel:], 0)
            change = lax.dot_general(
                block[:, 8 * panel :],
                right,
                (((0,), (0,)), ((), ())),
                precision=HI,
                preferred_element_type=jnp.float32,
            )
            cut = (lax.broadcasted_iota(jnp.int32, change.shape, 1) // 64) == k // 8
            rest = jnp.where(cut, 0.0, rest) - change
            for i in range(panel, n):
                rows[i] = rest[8 * (i - panel) : 8 * (i - panel) + 8, :]
            cols = [spread_lane(rows[k + 1], base + 8 + c) for c in range(8)]
        for i in range(k + 1, panel):
            factors = [spread_lane(rows[i], base + c) for c in range(8)]
            if i == k + 1:
                new = []
                for s in range(8):
                    v = after[s] * inverses
                    m = [factors[c] * spread_row(v, c) for c in range(8)]
                    new.append(spread_lane(rows[i], base + 8 + s) - sum_of(m))
                cols = new
            m = [factors[c] * z_rows[c] for c in range(8)]
            rows[i] = jnp.where(inside, 0.0, rows[i]) - sum_of(m)
    return out


def sum_of(m):
    return ((m[0] + m[1]) + (m[2] + m[3])) + ((m[4] + m[5]) + (m[6] + m[7]))


def factor_body(group_ref, p_ref, *refs):
    *beam_refs, o_ref, s_ref, d_ref, l_ref, b_ref = refs
    groups, high, _ = p_ref.shape
    n = s_ref.shape[0]
    count = n // TILE
    unit = 16
    lane = lax.broadcasted_iota(jnp.int32, (unit, TILE), 1)
    row = lax.broadcasted_iota(jnp.int32, (unit, TILE), 0)

    def loaded(r, c, at, piece):
        if r == c:
            piece = piece + jnp.where(row + at == lane, loading_level, 0.0)
        s_ref[r * TILE + at : r * TILE + at + unit, c * TILE : (c + 1) * TILE] = piece

    def pieces(first, tall):
        for at in range(0, tall, unit):
            g, at_row = divmod(first + at, high)
            yield at, p_ref[g, at_row : at_row + unit, :]

    for (r, c), first in packing(count).items():
        if r != c:
            for at, piece in pieces(first, TILE):
                loaded(r, c, at, piece)
        else:
            for at, piece in pieces(first[0], HALF):
                loaded(r, r, at, piece)
            for at, piece in pieces(first[1], HALF):
                if r % 2 == 0:
                    piece = pltpu.roll(piece, HALF, 1)
                loaded(r, r, HALF + at, jnp.where(lane < HALF, 0.0, piece))
    for r in range(count):
        for c in range(r):
            s_ref[r * TILE : (r + 1) * TILE, c * TILE : (c + 1) * TILE] = jnp.zeros(
                (TILE, TILE), jnp.float32
            )
    tile_of = lax.broadcasted_iota(jnp.int32, (TILE, n), 1) // TILE

    def times_transposed(a, b):
        return lax.dot_general(
            a, b, (((0,), (0,)), ((), ())), precision=HI, preferred_element_type=jnp.float32
        )

    tile = s_ref[:TILE, :TILE]
    for k in range(count):
        first = k * TILE
        after = first + TILE
        rows = factor_tile([tile[i : i + 8, :] for i in range(0, TILE, 8)])
        x = jnp.concatenate(rows, 0)
        l_ref[first:after, first:after] = x
        pieces = {k: x}
        for t in [*range(k + 1, count), *range(k)]:
            pieces[t] = jnp.dot(
                x,
                s_ref[first:after, t * TILE : (t + 1) * TILE],
                precision=HI,
                preferred_element_type=jnp.float32,
            )
            if t == k + 1:
                tile = s_ref[after : after + TILE, after : after + TILE] - times_transposed(
                    pieces[t], pieces[t]
                )
            if t < k:
                l_ref[first:after, t * TILE : (t + 1) * TILE] = pieces[t]
        for t in range(k + 1, count):
            l_ref[first:after, t * TILE : (t + 1) * TILE] = jnp.zeros((TILE, TILE), jnp.float32)
        for i in range(k + 1, count):
            for t in range(count):
                if k < t < i or i == t == k + 1:
                    continue
                change = times_transposed(pieces[i], pieces[t])
                span = (slice(i * TILE, (i + 1) * TILE), slice(t * TILE, (t + 1) * TILE))
                s_ref[span] = -change if t == k else s_ref[span] - change

    place_beams(group_ref[0], groups, beam_refs, b_ref)
    mine = o_ref.shape[0]
    left_high, left_low = split(l_ref[pl.ds(pl.multiple_of(group_ref[0] * mine, 8), mine), :])
    right_high, right_low = split(b_ref[...])
    o_ref[...] = (
        product_nt(left_high, right_low) + product_nt(left_low, right_high)
    ) + product_nt(left_high, right_high)


def split(x):
    high = x.astype(jnp.bfloat16)
    return high, (x - high.astype(jnp.float32)).astype(jnp.bfloat16)


def product_nt(a, b):
    return lax.dot_general(a, b, (((1,), (1,)), ((), ())), preferred_element_type=jnp.float32)


def place_beams(group, groups, beam_refs, b_ref):
    own, below, below2, above, above2, low, high = beam_refs
    share = own.shape[0]
    half = share // 2

    def put(by, at, values):
        owner = lax.rem(group + (by + groups), groups)
        first = pl.multiple_of(owner * share + at, 8)
        b_ref[pl.ds(first, values.shape[0]), :] = values

    put(0, 0, own[...])
    put(1, 0, above[...])
    put(2, 0, above2[...])
    put(3, 0, low[:share, :])
    put(4, 0, low[share:, :])
    put(4, half, high[share:, :])
    put(-3, 0, high[:share, :])
    put(-2, 0, below2[...])
    put(-1, 0, below[...])


def whitened_rows(group, packed, *beams):
    share, n = beams[0].shape
    groups = packed.shape[0]
    return pl.pallas_call(
        factor_body,
        out_shape=jax.ShapeDtypeStruct((n // groups, groups * share), jnp.float32),
        in_specs=[SMEM] + [VMEM] * 8,
        out_specs=VMEM,
        scratch_shapes=[
            pltpu.VMEM((n, n), jnp.float32),
            pltpu.VMEM((TILE, TILE), jnp.float32),
            pltpu.VMEM((n, n), jnp.float32),
            pltpu.VMEM((groups * share, n), jnp.float32),
        ],
        compiler_params=pltpu.CompilerParams(vmem_limit_bytes=14 << 20),
        cost_estimate=pl.CostEstimate(flops=12 * n**3, bytes_accessed=1 << 20, transcendentals=n),
        name="whitened_rows",
    )(group, packed, *beams)


def local(samples, taps_weight, retain):
    row_count = samples.shape[0]
    groups, blocks = (lax.axis_size("elem"), lax.axis_size("tm"))
    group = lax.axis_index("elem").reshape(1).astype(jnp.int32)
    share = row_count // groups
    half = share // 2
    with jax.named_scope("halo"):
        halo = shifted(samples[row_count - LEAD :], "tm", 1)
    args = (group, halo, widened(samples, taps_weight), taps_weight, retain)
    down, up, far_down, far_up = fir(
        (-1, -3, 1, 3, 4), (2 * share, 2 * share, half, half), False, *args
    )
    with jax.named_scope("beams_near"):
        down, up = (ring(down, -1), ring(up, 1))
        far_down, far_up = (ring(far_down, -2), ring(far_up, 2))
    keep, weight, stats = fir((0, -2, 2), (3 * share,), True, *args)
    low, high = relay_sums(keep, down, up, far_down, far_up)
    with jax.named_scope("beams_far"):
        low, high = (ring(low, -2), ring(high, 2))
    my_beams, packed = packed_gram(keep, down, up, low, high, weight)
    with jax.named_scope("gram_sum"):
        parts = lax.all_to_all(
            packed.reshape(groups, packed.shape[0] // groups, TILE), "elem", 0, 0
        )
    spread, own = spread_share(parts, stats, my_beams, blocks)
    with jax.named_scope("beams_gather"):
        below, above = (ring(own, 1), ring(own, -1))
        below2, above2 = (ring(own, 2), ring(own, -2))
    with jax.named_scope("blocks_out"):
        received = lax.all_to_all(spread, "tm", 0, 0, tiled=True)
    estimate, low, high = decayed(received, below, below2, above, above2)
    with jax.named_scope("beams_gather"):
        low, high = (ring(low, -2), ring(high, 2))
    with jax.named_scope("blocks_back"):
        returned = lax.all_to_all(estimate, "tm", 0, 0, tiled=True)
    with jax.named_scope("gram_gather"):
        packed_estimate = lax.all_to_all(
            replicated(returned, groups, low, high), "elem", 0, 0
        )
    return whitened_rows(
        group, packed_estimate, own, below, below2, above, above2, low, high
    )


def solution(mesh):
    placed = (P("tm", "elem"), P(None, "elem", None), P("tm"))
    return jax.shard_map(
        local, mesh=mesh, in_specs=placed, out_specs=P("elem", "tm"), check_vma=False
    )
```

```python
import jax
import jax.numpy as jnp
from jax import lax
from jax.experimental import pallas as pl
from jax.experimental.pallas import tpu as pltpu
from jax.sharding import PartitionSpec as P

loading_level = 0.1
HI = lax.Precision.HIGHEST
TILE = 128
VMEM = pl.BlockSpec(memory_space=pltpu.VMEM)
SMEM = pl.BlockSpec(memory_space=pltpu.SMEM)


def shifted(array, axis, by):
    size = lax.axis_size(axis)
    pairs = [(i, i + by) for i in range(size) if 0 <= i + by < size]
    return lax.ppermute(array, axis, pairs)


LEAD = 16
SPLIT = 2


def fir_body(offsets, weights, group_ref, halo_ref, x_hbm, w_hbm, *refs):
    if weights:
        retain_ref, refs = (refs[0], refs[1:])
    held = 2 if weights else 6
    outs, (xe_ref, part_ref, *own) = (refs[:-held], refs[-held:])
    taps, width, beams = w_hbm.shape
    rows = x_hbm.shape[0]
    groups = 8
    share = rows // groups
    each = taps // SPLIT
    copies = []
    if weights:
        xb_ref, wv_ref = (x_hbm, w_hbm)
    else:
        xb_ref, wv_ref, x_sem, w_sem = own
        copy_x = pltpu.make_async_copy(x_hbm, xb_ref, x_sem)
        copy_x.start()
        for q in range(SPLIT):
            span = pl.ds(q * each, each)
            copies.append(pltpu.make_async_copy(w_hbm.at[span], wv_ref.at[span], w_sem.at[q]))
            copies[-1].start()
    group = group_ref[0]
    if weights:
        weights_of(group, groups, retain_ref, outs[-2], outs[-1])
        outs = outs[:-2]
    xe_ref[:LEAD, :] = halo_ref[...].astype(jnp.float32)
    if not weights:
        copy_x.wait()
    xe_ref[LEAD:, :] = xb_ref[...].astype(jnp.float32)
    tall = share + LEAD
    for i, by in enumerate(offsets):
        chunk = lax.rem(group + (by + groups), groups)
        part_ref[i * tall : (i + 1) * tall, :] = xe_ref[
            pl.ds(pl.multiple_of(chunk * share, 8), tall), :
        ]
    total = None
    for q in range(SPLIT):
        if not weights:
            copies[q].wait()
        window = jnp.concatenate(
            [
                jnp.concatenate(
                    [
                        part_ref[i * tall + LEAD - k : (i + 1) * tall - k, :]
                        for i in range(len(offsets))
                    ],
                    0,
                ).astype(jnp.bfloat16)
                for k in range(q * each, (q + 1) * each)
            ],
            1,
        )
        product = jnp.dot(
            window,
            wv_ref[q * each : (q + 1) * each].reshape(each * width, beams),
            preferred_element_type=jnp.float32,
        )
        at = 0
        for o_ref in outs:
            tall_o = o_ref.shape[0]
            piece = product[at : at + tall_o]
            o_ref[...] = piece if q == 0 else o_ref[...] + piece
            at += tall_o


def weights_of(group, groups, retain_ref, weight_ref, stats_ref):
    rows = retain_ref.shape[0]
    share = rows // groups
    logs = jnp.log(retain_ref[...].reshape(1, rows))
    lane = lax.broadcasted_iota(jnp.int32, (share, rows), 1)
    row = lax.broadcasted_iota(jnp.int32, (share, rows), 0)
    spread = jnp.broadcast_to(logs, (share, rows))

    def weight_at(first):
        later = jnp.where(lane > row + first, spread, 0.0)
        return jnp.exp(jnp.sum(later, axis=1, keepdims=True))

    mass = jnp.zeros((1, 1), jnp.float32)
    for g in range(groups):
        mass = mass + jnp.sum(weight_at(g * share), axis=0, keepdims=True)
    weight_ref[...] = jnp.broadcast_to(weight_at(group * share), weight_ref.shape)
    log_total = jnp.sum(logs, axis=1, keepdims=True)
    at = lax.broadcasted_iota(jnp.int32, stats_ref.shape, 1)
    stats_ref[...] = jnp.where(
        at == HALF,
        jnp.broadcast_to(log_total, stats_ref.shape),
        jnp.broadcast_to(mass, stats_ref.shape),
    )


def fir(offsets, heights, weights, group, halo, samples, taps_weight, retain):
    rows, width = samples.shape
    taps, _, beams = taps_weight.shape
    share = rows // 8
    tall = share + LEAD
    place = jax.ShapeDtypeStruct if weights else pltpu.HBM
    shapes = [place((h, beams), jnp.float32) for h in heights]
    if weights:
        shapes.append(jax.ShapeDtypeStruct((share, TILE), jnp.float32))
        shapes.append(jax.ShapeDtypeStruct((1, TILE), jnp.float32))
    large = VMEM if weights else pl.BlockSpec(memory_space=pltpu.HBM)
    scratch = [
        pltpu.VMEM((rows + LEAD, width), jnp.float32),
        pltpu.VMEM((tall * len(offsets), width), jnp.float32),
    ]
    if not weights:
        scratch += [
            pltpu.VMEM((rows, width), samples.dtype),
            pltpu.VMEM(taps_weight.shape, taps_weight.dtype),
            pltpu.SemaphoreType.DMA,
            pltpu.SemaphoreType.DMA((SPLIT,)),
        ]
    if not weights:
        samples, taps_weight = (
            pltpu.with_memory_space_constraint(a, pltpu.HBM) for a in (samples, taps_weight)
        )
    return pl.pallas_call(
        lambda *refs: fir_body(offsets, weights, *refs),
        out_shape=shapes,
        in_specs=[SMEM, VMEM, large, large] + [VMEM] * weights,
        out_specs=[VMEM] * len(shapes),
        scratch_shapes=scratch,
        compiler_params=pltpu.CompilerParams(vmem_limit_bytes=(16 if weights else 40) << 20),
        cost_estimate=pl.CostEstimate(
            flops=2 * share * len(offsets) * taps * width * beams,
            bytes_accessed=6 << 20,
            transcendentals=0,
        ),
        name="fir_rest" if weights else "fir_sent",
    )(group, halo, samples, taps_weight, *([retain] if weights else []))


def ring(array, by):
    size = lax.axis_size("elem")
    return lax.ppermute(array, "elem", [(i, (i + by) % size) for i in range(size)])


def relay_body(keep_ref, down_ref, up_ref, far_down_ref, far_up_ref, low_ref, high_ref):
    share = low_ref.shape[0]
    half = share // 2
    low = keep_ref[share : 2 * share, :] + down_ref[share:, :]
    low_ref[:half, :] = low[:half] + far_down_ref[...]
    low_ref[half:, :] = low[half:]
    high = keep_ref[2 * share :, :] + up_ref[share:, :]
    high_ref[:half, :] = high[:half]
    high_ref[half:, :] = high[half:] + far_up_ref[...]


def relay_sums(keep, down, up, far_down, far_up):
    shape = jax.ShapeDtypeStruct((keep.shape[0] // 3, keep.shape[1]), jnp.float32)
    return pl.pallas_call(
        relay_body,
        out_shape=(shape, shape),
        in_specs=[VMEM] * 5,
        out_specs=(VMEM, VMEM),
        compiler_params=pltpu.CompilerParams(vmem_limit_bytes=5 << 20),
        name="relay_sums",
    )(keep, down, up, far_down, far_up)


def gram_body(keep_ref, down_ref, up_ref, low_ref, high_ref, weight_ref, b_ref, o_ref):
    share, beams = b_ref.shape
    b_ref[...] = (
        (keep_ref[:share, :] + down_ref[:share, :])
        + (up_ref[:share, :] + low_ref[...])
        + high_ref[...]
    )
    weighted = b_ref[...] * jnp.concatenate([weight_ref[...]] * (beams // TILE), 1)
    n = beams // TILE
    places = packing(n)
    lane = lax.broadcasted_iota(jnp.int32, (HALF, TILE), 1)
    corner = None
    for r in range(n):
        part = lax.dot_general(
            weighted[:, r * TILE : (r + 1) * TILE],
            b_ref[:, r * TILE :],
            (((0,), (0,)), ((), ())),
            precision=HI,
            preferred_element_type=jnp.float32,
        )
        for c in range(r + 1, n):
            at = places[r, c]
            o_ref[at : at + TILE, :] = part[:, (c - r) * TILE : (c - r + 1) * TILE]
        at, low = places[r, r]
        o_ref[at : at + HALF, :] = part[:HALF, :TILE]
        if r % 2 == 0:
            corner = pltpu.roll(part[HALF:, :TILE], HALF, 1)
        else:
            o_ref[low : low + HALF, :] = jnp.where(lane < HALF, corner, part[HALF:, :TILE])


HALF = TILE // 2


def packing(n):
    places, at = ({}, 0)
    for r in range(n):
        for c in range(r + 1, n):
            places[r, c] = at
            at += TILE
    for r in range(n):
        places[r, r] = (at + r * HALF, at + n * HALF + r // 2 * HALF)
    return places


def packed_rows(n):
    return (n * (n - 1) // 2) * TILE + n * HALF + n // 2 * HALF


def packed_gram(keep, down, up, low, high, weight):
    share, beams = low.shape
    n = beams // TILE
    return pl.pallas_call(
        gram_body,
        out_shape=(
            jax.ShapeDtypeStruct((share, beams), jnp.float32),
            jax.ShapeDtypeStruct((packed_rows(n), TILE), jnp.float32),
        ),
        in_specs=[VMEM] * 6,
        out_specs=(VMEM, VMEM),
        compiler_params=pltpu.CompilerParams(vmem_limit_bytes=6 << 20),
        name="packed_gram",
    )(keep, down, up, low, high, weight)


def share_body(stats_ref, p_ref, b_ref, o_ref, c_ref):
    c_ref[...] = b_ref[...]
    groups, rows, _ = p_ref.shape
    ways = o_ref.shape[0]
    total = p_ref[0]
    for g in range(1, groups):
        total = total + p_ref[g]
    tiles = rows // ways
    for s in range(tiles):
        o_ref[:, s, :] = total[s * ways : (s + 1) * ways, :]
    rest = total[tiles * ways :, :]
    lane = lax.broadcasted_iota(jnp.int32, (ways, TILE), 1)
    rest = jnp.concatenate([rest, pltpu.roll(rest, HALF, 1)], 0)
    o_ref[:, tiles, :] = jnp.where(lane < HALF, rest, stats_ref[...])


def spread_share(parts, stats, my_beams, ways):
    groups, rows, _ = parts.shape
    return pl.pallas_call(
        share_body,
        out_shape=(
            jax.ShapeDtypeStruct((ways, rows // ways + 1, TILE), jnp.float32),
            jax.ShapeDtypeStruct(my_beams.shape, jnp.float32),
        ),
        in_specs=[VMEM] * 3,
        out_specs=(VMEM, VMEM),
        compiler_params=pltpu.CompilerParams(vmem_limit_bytes=4 << 20),
        name="spread_share",
    )(stats, parts, my_beams)


def decay_body(r_ref, from_below, from_below2, from_above, from_above2, o_ref, low_ref, high_ref):
    share = from_below.shape[0]
    half = share // 2
    low_ref[:share, :] = from_above[...]
    low_ref[share:, :] = from_above2[:half, :]
    high_ref[:share, :] = from_below[...]
    high_ref[share:, :] = from_below2[half:, :]
    n, tiles, _ = r_ref.shape
    stats = r_ref[:, tiles - 1, :]
    logs = stats[:, HALF : HALF + 1]
    row = lax.broadcasted_iota(jnp.int32, (n, n), 0)
    col = lax.broadcasted_iota(jnp.int32, (n, n), 1)
    upto = jnp.where(col <= row, 1.0, 0.0)
    later = jnp.where(row > col, jnp.broadcast_to(logs, (n, n)), 0.0)
    span = jnp.dot(upto, later, precision=HI, preferred_element_type=jnp.float32)
    factor = jnp.where(col <= row, jnp.exp(jnp.where(col <= row, span, 0.0)), 0.0)
    count = jnp.dot(factor, stats, precision=HI, preferred_element_type=jnp.float32)[
        :, HALF + 1 : HALF + 2
    ]
    gram = jnp.dot(
        factor,
        jnp.concatenate([r_ref[:, s, :] for s in range(tiles)], 1),
        precision=HI,
        preferred_element_type=jnp.float32,
    )
    gram = gram / count
    for s in range(tiles):
        o_ref[:, s, :] = gram[:, s * TILE : (s + 1) * TILE]


def decayed(received, *near):
    n, tiles, _ = received.shape
    share, beams = near[0].shape
    packed = jax.ShapeDtypeStruct((share + share // 2, beams), jnp.float32)
    return pl.pallas_call(
        decay_body,
        out_shape=(jax.ShapeDtypeStruct((n, tiles, TILE), jnp.float32), packed, packed),
        in_specs=[VMEM] * 5,
        out_specs=(VMEM,) * 3,
        compiler_params=pltpu.CompilerParams(vmem_limit_bytes=5 << 20),
        name="decayed_sums",
    )(received, *near)


def replicate_body(r_ref, low_ref, high_ref, o_ref):
    ways, tiles, _ = r_ref.shape
    half = ways // 2
    tiles -= 1
    last = r_ref[:, tiles, :]
    lane = lax.broadcasted_iota(jnp.int32, (half, TILE), 1)
    last = jnp.where(lane < HALF, last[:half, :], pltpu.roll(last[half:, :], HALF, 1))
    for g in range(o_ref.shape[0]):
        for s in range(tiles):
            o_ref[g, s * ways : (s + 1) * ways, :] = r_ref[:, s, :]
        o_ref[g, tiles * ways :, :] = last


def replicated(returned, groups, low, high):
    ways, tiles, _ = returned.shape
    return pl.pallas_call(
        replicate_body,
        out_shape=jax.ShapeDtypeStruct((groups, ways * tiles - ways // 2, TILE), jnp.float32),
        in_specs=[VMEM] * 3,
        out_specs=VMEM,
        compiler_params=pltpu.CompilerParams(vmem_limit_bytes=4 << 20),
        name="replicated",
    )(returned, low, high)


def spread_row(x, r):
    return jnp.broadcast_to(x[r : r + 1, :], x.shape)


def spread_lane(x, at):
    return jnp.broadcast_to(x[:, at : at + 1], x.shape)


def factor_tile(rows):
    lane = lax.broadcasted_iota(jnp.int32, (8, TILE), 1)
    sub = lax.broadcasted_iota(jnp.int32, (8, TILE), 0)
    rows, out, done, n = (list(rows), [], [], len(rows))
    cols = [spread_lane(rows[0], c) for c in range(8)]
    for k in range(n):
        base = 8 * k
        last = k + 1 == n
        after = [] if last else [spread_lane(rows[k], base + 8 + c) for c in range(8)]
        inside = (lane >= base) & (lane < base + 8)
        g = jnp.where(inside, jnp.where(lane - base == sub, 1.0, 0.0), rows[k])
        w = g
        pivots = jnp.ones((8, TILE), jnp.float32)
        inverses = pivots
        for c in range(8):
            pivot = spread_row(cols[c], c)
            inverse = 1.0 / pivot
            other = jnp.where(sub == c, 0.0, cols[c])
            below = jnp.where(sub > c, cols[c], 0.0)
            for s in range(c + 1, 8):
                cols[s] = cols[s] - (other * spread_row(cols[s], c)) * inverse
            scaled = other * inverse
            g = g - scaled * spread_row(g, c)
            w = w - (below * inverse) * spread_row(w, c)
            after = [v - scaled * spread_row(v, c) for v in after]
            pivots = jnp.where(sub == c, pivot, pivots)
            inverses = jnp.where(sub == c, inverse, inverses)
        z = g * inverses
        y = w * lax.rsqrt(pivots)
        out.append(jnp.where(lane < base + 8, y, 0.0))
        if last:
            break
        z_rows = [spread_row(z, c) for c in range(8)]
        panel = (k // 8 + 1) * 8
        far = k + 1 == panel
        done.append((y, jnp.where((lane < base + 8) | (lane >= 8 * panel), y, 0.0)))
        if far:
            block = jnp.concatenate([d[0] for d in done[-8:]], 0)
            right = jnp.concatenate([d[1] for d in done[-8:]], 0)
            rest = jnp.concatenate(rows[panel:], 0)
            change = lax.dot_general(
                block[:, 8 * panel :],
                right,
                (((0,), (0,)), ((), ())),
                precision=HI,
                preferred_element_type=jnp.float32,
            )
            cut = (lax.broadcasted_iota(jnp.int32, change.shape, 1) // 64) == k // 8
            rest = jnp.where(cut, 0.0, rest) - change
            for i in range(panel, n):
                rows[i] = rest[8 * (i - panel) : 8 * (i - panel) + 8, :]
            cols = [spread_lane(rows[k + 1], base + 8 + c) for c in range(8)]
        for i in range(k + 1, panel):
            factors = [spread_lane(rows[i], base + c) for c in range(8)]
            if i == k + 1:
                new = []
                for s in range(8):
                    v = after[s] * inverses
                    m = [factors[c] * spread_row(v, c) for c in range(8)]
                    new.append(spread_lane(rows[i], base + 8 + s) - sum_of(m))
                cols = new
            m = [factors[c] * z_rows[c] for c in range(8)]
            rows[i] = jnp.where(inside, 0.0, rows[i]) - sum_of(m)
    return out


def sum_of(m):
    return ((m[0] + m[1]) + (m[2] + m[3])) + ((m[4] + m[5]) + (m[6] + m[7]))


def factor_body(group_ref, p_ref, *refs):
    *beam_refs, o_ref, s_ref, d_ref, l_ref, b_ref = refs
    groups, high, _ = p_ref.shape
    n = s_ref.shape[0]
    count = n // TILE
    unit = 16
    lane = lax.broadcasted_iota(jnp.int32, (unit, TILE), 1)
    row = lax.broadcasted_iota(jnp.int32, (unit, TILE), 0)

    def loaded(r, c, at, piece):
        if r == c:
            piece = piece + jnp.where(row + at == lane, loading_level, 0.0)
        s_ref[r * TILE + at : r * TILE + at + unit, c * TILE : (c + 1) * TILE] = piece

    def pieces(first, tall):
        for at in range(0, tall, unit):
            g, at_row = divmod(first + at, high)
            yield at, p_ref[g, at_row : at_row + unit, :]

    for (r, c), first in packing(count).items():
        if r != c:
            for at, piece in pieces(first, TILE):
                loaded(r, c, at, piece)
        else:
            for at, piece in pieces(first[0], HALF):
                loaded(r, r, at, piece)
            for at, piece in pieces(first[1], HALF):
                if r % 2 == 0:
                    piece = pltpu.roll(piece, HALF, 1)
                loaded(r, r, HALF + at, jnp.where(lane < HALF, 0.0, piece))
    for r in range(count):
        for c in range(r):
            s_ref[r * TILE : (r + 1) * TILE, c * TILE : (c + 1) * TILE] = jnp.zeros(
                (TILE, TILE), jnp.float32
            )
    tile_of = lax.broadcasted_iota(jnp.int32, (TILE, n), 1) // TILE

    def times_transposed(a, b):
        return lax.dot_general(
            a, b, (((0,), (0,)), ((), ())), precision=HI, preferred_element_type=jnp.float32
        )

    tile = s_ref[:TILE, :TILE]
    for k in range(count):
        first = k * TILE
        after = first + TILE
        rows = factor_tile([tile[i : i + 8, :] for i in range(0, TILE, 8)])
        x = jnp.concatenate(rows, 0)
        l_ref[first:after, first:after] = x
        pieces = {k: x}
        for t in [*range(k + 1, count), *range(k)]:
            pieces[t] = jnp.dot(
                x,
                s_ref[first:after, t * TILE : (t + 1) * TILE],
                precision=HI,
                preferred_element_type=jnp.float32,
            )
            if t == k + 1:
                tile = s_ref[after : after + TILE, after : after + TILE] - times_transposed(
                    pieces[t], pieces[t]
                )
            if t < k:
                l_ref[first:after, t * TILE : (t + 1) * TILE] = pieces[t]
        for t in range(k + 1, count):
            l_ref[first:after, t * TILE : (t + 1) * TILE] = jnp.zeros((TILE, TILE), jnp.float32)
        for i in range(k + 1, count):
            for t in range(count):
                if k < t < i or i == t == k + 1:
                    continue
                change = times_transposed(pieces[i], pieces[t])
                span = (slice(i * TILE, (i + 1) * TILE), slice(t * TILE, (t + 1) * TILE))
                s_ref[span] = -change if t == k else s_ref[span] - change

    place_beams(group_ref[0], groups, beam_refs, b_ref)
    mine = o_ref.shape[0]
    left_high, left_low = split(l_ref[pl.ds(pl.multiple_of(group_ref[0] * mine, 8), mine), :])
    right_high, right_low = split(b_ref[...])
    o_ref[...] = (
        product_nt(left_high, right_low) + product_nt(left_low, right_high)
    ) + product_nt(left_high, right_high)


def split(x):
    high = x.astype(jnp.bfloat16)
    return high, (x - high.astype(jnp.float32)).astype(jnp.bfloat16)


def product_nt(a, b):
    return lax.dot_general(a, b, (((1,), (1,)), ((), ())), preferred_element_type=jnp.float32)


def place_beams(group, groups, beam_refs, b_ref):
    own, below, below2, above, above2, low, high = beam_refs
    share = own.shape[0]
    half = share // 2

    def put(by, at, values):
        owner = lax.rem(group + (by + groups), groups)
        first = pl.multiple_of(owner * share + at, 8)
        b_ref[pl.ds(first, values.shape[0]), :] = values

    put(0, 0, own[...])
    put(1, 0, above[...])
    put(2, 0, above2[...])
    put(3, 0, low[:share, :])
    put(4, 0, low[share:, :])
    put(4, half, high[share:, :])
    put(-3, 0, high[:share, :])
    put(-2, 0, below2[...])
    put(-1, 0, below[...])


def whitened_rows(group, packed, *beams):
    share, n = beams[0].shape
    groups = packed.shape[0]
    return pl.pallas_call(
        factor_body,
        out_shape=jax.ShapeDtypeStruct((n // groups, groups * share), jnp.float32),
        in_specs=[SMEM] + [VMEM] * 8,
        out_specs=VMEM,
        scratch_shapes=[
            pltpu.VMEM((n, n), jnp.float32),
            pltpu.VMEM((TILE, TILE), jnp.float32),
            pltpu.VMEM((n, n), jnp.float32),
            pltpu.VMEM((groups * share, n), jnp.float32),
        ],
        compiler_params=pltpu.CompilerParams(vmem_limit_bytes=14 << 20),
        cost_estimate=pl.CostEstimate(flops=12 * n**3, bytes_accessed=1 << 20, transcendentals=n),
        name="whitened_rows",
    )(group, packed, *beams)


def local(samples, taps_weight, retain):
    row_count = samples.shape[0]
    groups, blocks = (lax.axis_size("elem"), lax.axis_size("tm"))
    group = lax.axis_index("elem").reshape(1).astype(jnp.int32)
    share = row_count // groups
    half = share // 2
    with jax.named_scope("halo"):
        halo = shifted(samples[row_count - LEAD :], "tm", 1)
    args = (group, halo, samples, taps_weight, retain)
    down, up, far_down, far_up = fir(
        (-1, -3, 1, 3, 4), (2 * share, 2 * share, half, half), False, *args
    )
    with jax.named_scope("beams_near"):
        down, up = (ring(down, -1), ring(up, 1))
        far_down, far_up = (ring(far_down, -2), ring(far_up, 2))
    keep, weight, stats = fir((0, -2, 2), (3 * share,), True, *args)
    low, high = relay_sums(keep, down, up, far_down, far_up)
    with jax.named_scope("beams_far"):
        low, high = (ring(low, -2), ring(high, 2))
    my_beams, packed = packed_gram(keep, down, up, low, high, weight)
    with jax.named_scope("gram_sum"):
        parts = lax.all_to_all(
            packed.reshape(groups, packed.shape[0] // groups, TILE), "elem", 0, 0
        )
    spread, own = spread_share(parts, stats, my_beams, blocks)
    with jax.named_scope("beams_gather"):
        below, above = (ring(own, 1), ring(own, -1))
        below2, above2 = (ring(own, 2), ring(own, -2))
    with jax.named_scope("blocks_out"):
        received = lax.all_to_all(spread, "tm", 0, 0, tiled=True)
    estimate, low, high = decayed(received, below, below2, above, above2)
    with jax.named_scope("beams_gather"):
        low, high = (ring(low, -2), ring(high, 2))
    with jax.named_scope("blocks_back"):
        returned = lax.all_to_all(estimate, "tm", 0, 0, tiled=True)
    with jax.named_scope("gram_gather"):
        packed_estimate = lax.all_to_all(
            replicated(returned, groups, low, high), "elem", 0, 0
        )
    return whitened_rows(
        group, packed_estimate, own, below, below2, above, above2, low, high
    )


def solution(mesh):
    placed = (P("tm", "elem"), P(None, "elem", None), P("tm"))
    return jax.shard_map(
        local, mesh=mesh, in_specs=placed, out_specs=P("elem", "tm"), check_vma=False
    )
```

```python
import jax
import jax.numpy as jnp
from jax import lax
from jax.experimental import pallas as pl
from jax.experimental.pallas import tpu as pltpu
from jax.sharding import PartitionSpec as P

loading_level = 0.1
HI = lax.Precision.HIGHEST
TILE = 128
VMEM = pl.BlockSpec(memory_space=pltpu.VMEM)
SMEM = pl.BlockSpec(memory_space=pltpu.SMEM)


def shifted(array, axis, by):
    size = lax.axis_size(axis)
    pairs = [(i, i + by) for i in range(size) if 0 <= i + by < size]
    return lax.ppermute(array, axis, pairs)


LEAD = 16
SPLIT = 2


def fir_body(offsets, weights, group_ref, halo_ref, x_hbm, w_hbm, *refs):
    if weights:
        retain_ref, refs = (refs[0], refs[1:])
    held = 2 if weights else 6
    outs, (xe_ref, part_ref, *own) = (refs[:-held], refs[-held:])
    taps, width, beams = w_hbm.shape
    rows = x_hbm.shape[0]
    groups = 8
    share = rows // groups
    each = taps // SPLIT
    copies = []
    if weights:
        xb_ref, wv_ref = (x_hbm, w_hbm)
    else:
        xb_ref, wv_ref, x_sem, w_sem = own
        copy_x = pltpu.make_async_copy(x_hbm, xb_ref, x_sem)
        copy_x.start()
        for q in range(SPLIT):
            span = pl.ds(q * each, each)
            copies.append(pltpu.make_async_copy(w_hbm.at[span], wv_ref.at[span], w_sem.at[q]))
            copies[-1].start()
    group = group_ref[0]
    if weights:
        weights_of(group, groups, retain_ref, outs[-2], outs[-1])
        outs = outs[:-2]
    xe_ref[:LEAD, :] = halo_ref[...].astype(jnp.float32)
    if not weights:
        copy_x.wait()
    xe_ref[LEAD:, :] = xb_ref[...].astype(jnp.float32)
    tall = share + LEAD
    for i, by in enumerate(offsets):
        chunk = lax.rem(group + (by + groups), groups)
        part_ref[i * tall : (i + 1) * tall, :] = xe_ref[
            pl.ds(pl.multiple_of(chunk * share, 8), tall), :
        ]
    total = None
    for q in range(SPLIT):
        if not weights:
            copies[q].wait()
        window = jnp.concatenate(
            [
                jnp.concatenate(
                    [
                        part_ref[i * tall + LEAD - k : (i + 1) * tall - k, :]
                        for i in range(len(offsets))
                    ],
                    0,
                ).astype(jnp.bfloat16)
                for k in range(q * each, (q + 1) * each)
            ],
            1,
        )
        product = jnp.dot(
            window,
            wv_ref[q * each : (q + 1) * each].reshape(each * width, beams),
            preferred_element_type=jnp.float32,
        )
        at = 0
        for o_ref in outs:
            tall_o = o_ref.shape[0]
            piece = product[at : at + tall_o]
            o_ref[...] = piece if q == 0 else o_ref[...] + piece
            at += tall_o


def weights_of(group, groups, retain_ref, weight_ref, stats_ref):
    rows = retain_ref.shape[0]
    share = rows // groups
    logs = jnp.log(retain_ref[...].reshape(1, rows))
    lane = lax.broadcasted_iota(jnp.int32, (share, rows), 1)
    row = lax.broadcasted_iota(jnp.int32, (share, rows), 0)
    spread = jnp.broadcast_to(logs, (share, rows))

    def weight_at(first):
        later = jnp.where(lane > row + first, spread, 0.0)
        return jnp.exp(jnp.sum(later, axis=1, keepdims=True))

    mass = jnp.zeros((1, 1), jnp.float32)
    for g in range(groups):
        mass = mass + jnp.sum(weight_at(g * share), axis=0, keepdims=True)
    weight_ref[...] = jnp.broadcast_to(weight_at(group * share), weight_ref.shape)
    log_total = jnp.sum(logs, axis=1, keepdims=True)
    at = lax.broadcasted_iota(jnp.int32, stats_ref.shape, 1)
    stats_ref[...] = jnp.where(
        at == HALF,
        jnp.broadcast_to(log_total, stats_ref.shape),
        jnp.broadcast_to(mass, stats_ref.shape),
    )


def fir(offsets, heights, weights, group, halo, samples, taps_weight, retain):
    rows, width = samples.shape
    taps, _, beams = taps_weight.shape
    share = rows // 8
    tall = share + LEAD
    shapes = [jax.ShapeDtypeStruct((h, beams), jnp.float32) for h in heights]
    if weights:
        shapes.append(jax.ShapeDtypeStruct((share, TILE), jnp.float32))
        shapes.append(jax.ShapeDtypeStruct((1, TILE), jnp.float32))
    large = VMEM if weights else pl.BlockSpec(memory_space=pltpu.HBM)
    scratch = [
        pltpu.VMEM((rows + LEAD, width), jnp.float32),
        pltpu.VMEM((tall * len(offsets), width), jnp.float32),
    ]
    if not weights:
        scratch += [
            pltpu.VMEM((rows, width), samples.dtype),
            pltpu.VMEM(taps_weight.shape, taps_weight.dtype),
            pltpu.SemaphoreType.DMA,
            pltpu.SemaphoreType.DMA((SPLIT,)),
        ]
    if not weights:
        samples, taps_weight = (
            pltpu.with_memory_space_constraint(a, pltpu.HBM) for a in (samples, taps_weight)
        )
    return pl.pallas_call(
        lambda *refs: fir_body(offsets, weights, *refs),
        out_shape=shapes,
        in_specs=[SMEM, VMEM, large, large] + [VMEM] * weights,
        out_specs=[VMEM] * len(shapes),
        scratch_shapes=scratch,
        compiler_params=pltpu.CompilerParams(vmem_limit_bytes=(16 if weights else 40) << 20),
        cost_estimate=pl.CostEstimate(
            flops=2 * share * len(offsets) * taps * width * beams,
            bytes_accessed=6 << 20,
            transcendentals=0,
        ),
        name="fir_rest" if weights else "fir_sent",
    )(group, halo, samples, taps_weight, *([retain] if weights else []))


def ring(array, by):
    size = lax.axis_size("elem")
    return lax.ppermute(array, "elem", [(i, (i + by) % size) for i in range(size)])


def relay_body(keep_ref, down_ref, up_ref, far_down_ref, far_up_ref, low_ref, high_ref):
    share = low_ref.shape[0]
    half = share // 2
    low = keep_ref[share : 2 * share, :] + down_ref[share:, :]
    low_ref[:half, :] = low[:half] + far_down_ref[...]
    low_ref[half:, :] = low[half:]
    high = keep_ref[2 * share :, :] + up_ref[share:, :]
    high_ref[:half, :] = high[:half]
    high_ref[half:, :] = high[half:] + far_up_ref[...]


def relay_sums(keep, down, up, far_down, far_up):
    shape = jax.ShapeDtypeStruct((keep.shape[0] // 3, keep.shape[1]), jnp.float32)
    return pl.pallas_call(
        relay_body,
        out_shape=(shape, shape),
        in_specs=[VMEM] * 5,
        out_specs=(VMEM, VMEM),
        compiler_params=pltpu.CompilerParams(vmem_limit_bytes=5 << 20),
        name="relay_sums",
    )(keep, down, up, far_down, far_up)


def gram_body(keep_ref, down_ref, up_ref, low_ref, high_ref, weight_ref, b_ref, o_ref):
    share, beams = b_ref.shape
    b_ref[...] = (
        (keep_ref[:share, :] + down_ref[:share, :])
        + (up_ref[:share, :] + low_ref[...])
        + high_ref[...]
    )
    weighted = b_ref[...] * jnp.concatenate([weight_ref[...]] * (beams // TILE), 1)
    n = beams // TILE
    places = packing(n)
    lane = lax.broadcasted_iota(jnp.int32, (HALF, TILE), 1)
    corner = None
    for r in range(n):
        part = lax.dot_general(
            weighted[:, r * TILE : (r + 1) * TILE],
            b_ref[:, r * TILE :],
            (((0,), (0,)), ((), ())),
            precision=HI,
            preferred_element_type=jnp.float32,
        )
        for c in range(r + 1, n):
            at = places[r, c]
            o_ref[at : at + TILE, :] = part[:, (c - r) * TILE : (c - r + 1) * TILE]
        at, low = places[r, r]
        o_ref[at : at + HALF, :] = part[:HALF, :TILE]
        if r % 2 == 0:
            corner = pltpu.roll(part[HALF:, :TILE], HALF, 1)
        else:
            o_ref[low : low + HALF, :] = jnp.where(lane < HALF, corner, part[HALF:, :TILE])


HALF = TILE // 2


def packing(n):
    places, at = ({}, 0)
    for r in range(n):
        for c in range(r + 1, n):
            places[r, c] = at
            at += TILE
    for r in range(n):
        places[r, r] = (at + r * HALF, at + n * HALF + r // 2 * HALF)
    return places


def packed_rows(n):
    return (n * (n - 1) // 2) * TILE + n * HALF + n // 2 * HALF


def packed_gram(keep, down, up, low, high, weight):
    share, beams = low.shape
    n = beams // TILE
    return pl.pallas_call(
        gram_body,
        out_shape=(
            jax.ShapeDtypeStruct((share, beams), jnp.float32),
            jax.ShapeDtypeStruct((packed_rows(n), TILE), jnp.float32),
        ),
        in_specs=[VMEM] * 6,
        out_specs=(VMEM, VMEM),
        compiler_params=pltpu.CompilerParams(vmem_limit_bytes=6 << 20),
        name="packed_gram",
    )(keep, down, up, low, high, weight)


def share_body(stats_ref, p_ref, b_ref, o_ref, c_ref):
    c_ref[...] = b_ref[...]
    groups, rows, _ = p_ref.shape
    ways = o_ref.shape[0]
    total = p_ref[0]
    for g in range(1, groups):
        total = total + p_ref[g]
    tiles = rows // ways
    for s in range(tiles):
        o_ref[:, s, :] = total[s * ways : (s + 1) * ways, :]
    rest = total[tiles * ways :, :]
    lane = lax.broadcasted_iota(jnp.int32, (ways, TILE), 1)
    rest = jnp.concatenate([rest, pltpu.roll(rest, HALF, 1)], 0)
    o_ref[:, tiles, :] = jnp.where(lane < HALF, rest, stats_ref[...])


def spread_share(parts, stats, my_beams, ways):
    groups, rows, _ = parts.shape
    return pl.pallas_call(
        share_body,
        out_shape=(
            jax.ShapeDtypeStruct((ways, rows // ways + 1, TILE), jnp.float32),
            jax.ShapeDtypeStruct(my_beams.shape, jnp.float32),
        ),
        in_specs=[VMEM] * 3,
        out_specs=(VMEM, VMEM),
        compiler_params=pltpu.CompilerParams(vmem_limit_bytes=4 << 20),
        name="spread_share",
    )(stats, parts, my_beams)


def decay_body(r_ref, from_below, from_below2, from_above, from_above2, o_ref, low_ref, high_ref):
    share = from_below.shape[0]
    half = share // 2
    low_ref[:share, :] = from_above[...]
    low_ref[share:, :] = from_above2[:half, :]
    high_ref[:share, :] = from_below[...]
    high_ref[share:, :] = from_below2[half:, :]
    n, tiles, _ = r_ref.shape
    stats = r_ref[:, tiles - 1, :]
    logs = stats[:, HALF : HALF + 1]
    row = lax.broadcasted_iota(jnp.int32, (n, n), 0)
    col = lax.broadcasted_iota(jnp.int32, (n, n), 1)
    upto = jnp.where(col <= row, 1.0, 0.0)
    later = jnp.where(row > col, jnp.broadcast_to(logs, (n, n)), 0.0)
    span = jnp.dot(upto, later, precision=HI, preferred_element_type=jnp.float32)
    factor = jnp.where(col <= row, jnp.exp(jnp.where(col <= row, span, 0.0)), 0.0)
    count = jnp.dot(factor, stats, precision=HI, preferred_element_type=jnp.float32)[
        :, HALF + 1 : HALF + 2
    ]
    gram = jnp.dot(
        factor,
        jnp.concatenate([r_ref[:, s, :] for s in range(tiles)], 1),
        precision=HI,
        preferred_element_type=jnp.float32,
    )
    gram = gram / count
    for s in range(tiles):
        o_ref[:, s, :] = gram[:, s * TILE : (s + 1) * TILE]


def decayed(received, *near):
    n, tiles, _ = received.shape
    share, beams = near[0].shape
    packed = jax.ShapeDtypeStruct((share + share // 2, beams), jnp.float32)
    return pl.pallas_call(
        decay_body,
        out_shape=(jax.ShapeDtypeStruct((n, tiles, TILE), jnp.float32), packed, packed),
        in_specs=[VMEM] * 5,
        out_specs=(VMEM,) * 3,
        compiler_params=pltpu.CompilerParams(vmem_limit_bytes=5 << 20),
        name="decayed_sums",
    )(received, *near)


def replicate_body(r_ref, low_ref, high_ref, o_ref):
    ways, tiles, _ = r_ref.shape
    half = ways // 2
    tiles -= 1
    last = r_ref[:, tiles, :]
    lane = lax.broadcasted_iota(jnp.int32, (half, TILE), 1)
    last = jnp.where(lane < HALF, last[:half, :], pltpu.roll(last[half:, :], HALF, 1))
    for g in range(o_ref.shape[0]):
        for s in range(tiles):
            o_ref[g, s * ways : (s + 1) * ways, :] = r_ref[:, s, :]
        o_ref[g, tiles * ways :, :] = last


def replicated(returned, groups, low, high):
    ways, tiles, _ = returned.shape
    return pl.pallas_call(
        replicate_body,
        out_shape=jax.ShapeDtypeStruct((groups, ways * tiles - ways // 2, TILE), jnp.float32),
        in_specs=[VMEM] * 3,
        out_specs=VMEM,
        compiler_params=pltpu.CompilerParams(vmem_limit_bytes=4 << 20),
        name="replicated",
    )(returned, low, high)


def spread_row(x, r):
    return jnp.broadcast_to(x[r : r + 1, :], x.shape)


def spread_lane(x, at):
    return jnp.broadcast_to(x[:, at : at + 1], x.shape)


def factor_tile(rows):
    lane = lax.broadcasted_iota(jnp.int32, (8, TILE), 1)
    sub = lax.broadcasted_iota(jnp.int32, (8, TILE), 0)
    rows, out, done, n = (list(rows), [], [], len(rows))
    cols = [spread_lane(rows[0], c) for c in range(8)]
    for k in range(n):
        base = 8 * k
        last = k + 1 == n
        after = [] if last else [spread_lane(rows[k], base + 8 + c) for c in range(8)]
        inside = (lane >= base) & (lane < base + 8)
        g = jnp.where(inside, jnp.where(lane - base == sub, 1.0, 0.0), rows[k])
        w = g
        pivots = jnp.ones((8, TILE), jnp.float32)
        inverses = pivots
        for c in range(8):
            pivot = spread_row(cols[c], c)
            inverse = 1.0 / pivot
            other = jnp.where(sub == c, 0.0, cols[c])
            below = jnp.where(sub > c, cols[c], 0.0)
            for s in range(c + 1, 8):
                cols[s] = cols[s] - (other * spread_row(cols[s], c)) * inverse
            scaled = other * inverse
            g = g - scaled * spread_row(g, c)
            w = w - (below * inverse) * spread_row(w, c)
            after = [v - scaled * spread_row(v, c) for v in after]
            pivots = jnp.where(sub == c, pivot, pivots)
            inverses = jnp.where(sub == c, inverse, inverses)
        z = g * inverses
        y = w * lax.rsqrt(pivots)
        out.append(jnp.where(lane < base + 8, y, 0.0))
        if last:
            break
        z_rows = [spread_row(z, c) for c in range(8)]
        panel = (k // 8 + 1) * 8
        far = k + 1 == panel
        done.append((y, jnp.where((lane < base + 8) | (lane >= 8 * panel), y, 0.0)))
        if far:
            block = jnp.concatenate([d[0] for d in done[-8:]], 0)
            right = jnp.concatenate([d[1] for d in done[-8:]], 0)
            rest = jnp.concatenate(rows[panel:], 0)
            change = lax.dot_general(
                block[:, 8 * panel :],
                right,
                (((0,), (0,)), ((), ())),
                precision=HI,
                preferred_element_type=jnp.float32,
            )
            cut = (lax.broadcasted_iota(jnp.int32, change.shape, 1) // 64) == k // 8
            rest = jnp.where(cut, 0.0, rest) - change
            for i in range(panel, n):
                rows[i] = rest[8 * (i - panel) : 8 * (i - panel) + 8, :]
            cols = [spread_lane(rows[k + 1], base + 8 + c) for c in range(8)]
        for i in range(k + 1, panel):
            factors = [spread_lane(rows[i], base + c) for c in range(8)]
            if i == k + 1:
                new = []
                for s in range(8):
                    v = after[s] * inverses
                    m = [factors[c] * spread_row(v, c) for c in range(8)]
                    new.append(spread_lane(rows[i], base + 8 + s) - sum_of(m))
                cols = new
            m = [factors[c] * z_rows[c] for c in range(8)]
            rows[i] = jnp.where(inside, 0.0, rows[i]) - sum_of(m)
    return out


def sum_of(m):
    return ((m[0] + m[1]) + (m[2] + m[3])) + ((m[4] + m[5]) + (m[6] + m[7]))


def factor_body(group_ref, p_ref, *refs):
    *beam_refs, o_ref, s_ref, d_ref, l_ref, b_ref = refs
    groups, high, _ = p_ref.shape
    n = s_ref.shape[0]
    count = n // TILE
    unit = 16
    lane = lax.broadcasted_iota(jnp.int32, (unit, TILE), 1)
    row = lax.broadcasted_iota(jnp.int32, (unit, TILE), 0)

    def loaded(r, c, at, piece):
        if r == c:
            piece = piece + jnp.where(row + at == lane, loading_level, 0.0)
        s_ref[r * TILE + at : r * TILE + at + unit, c * TILE : (c + 1) * TILE] = piece

    def pieces(first, tall):
        for at in range(0, tall, unit):
            g, at_row = divmod(first + at, high)
            yield at, p_ref[g, at_row : at_row + unit, :]

    for (r, c), first in packing(count).items():
        if r != c:
            for at, piece in pieces(first, TILE):
                loaded(r, c, at, piece)
        else:
            for at, piece in pieces(first[0], HALF):
                loaded(r, r, at, piece)
            for at, piece in pieces(first[1], HALF):
                if r % 2 == 0:
                    piece = pltpu.roll(piece, HALF, 1)
                loaded(r, r, HALF + at, jnp.where(lane < HALF, 0.0, piece))
    for r in range(count):
        for c in range(r):
            s_ref[r * TILE : (r + 1) * TILE, c * TILE : (c + 1) * TILE] = jnp.zeros(
                (TILE, TILE), jnp.float32
            )
    tile_of = lax.broadcasted_iota(jnp.int32, (TILE, n), 1) // TILE

    def times_transposed(a, b):
        return lax.dot_general(
            a, b, (((0,), (0,)), ((), ())), precision=HI, preferred_element_type=jnp.float32
        )

    tile = s_ref[:TILE, :TILE]
    for k in range(count):
        first = k * TILE
        after = first + TILE
        rows = factor_tile([tile[i : i + 8, :] for i in range(0, TILE, 8)])
        x = jnp.concatenate(rows, 0)
        l_ref[first:after, first:after] = x
        pieces = {k: x}
        for t in [*range(k + 1, count), *range(k)]:
            pieces[t] = jnp.dot(
                x,
                s_ref[first:after, t * TILE : (t + 1) * TILE],
                precision=HI,
                preferred_element_type=jnp.float32,
            )
            if t == k + 1:
                tile = s_ref[after : after + TILE, after : after + TILE] - times_transposed(
                    pieces[t], pieces[t]
                )
            if t < k:
                l_ref[first:after, t * TILE : (t + 1) * TILE] = pieces[t]
        for t in range(k + 1, count):
            l_ref[first:after, t * TILE : (t + 1) * TILE] = jnp.zeros((TILE, TILE), jnp.float32)
        for i in range(k + 1, count):
            for t in range(count):
                if k < t < i or i == t == k + 1:
                    continue
                change = times_transposed(pieces[i], pieces[t])
                span = (slice(i * TILE, (i + 1) * TILE), slice(t * TILE, (t + 1) * TILE))
                s_ref[span] = -change if t == k else s_ref[span] - change

    place_beams(group_ref[0], groups, beam_refs, b_ref)
    mine = o_ref.shape[0]
    left_high, left_low = split(l_ref[pl.ds(pl.multiple_of(group_ref[0] * mine, 8), mine), :])
    right_high, right_low = split(b_ref[...])
    o_ref[...] = (
        product_nt(left_high, right_low) + product_nt(left_low, right_high)
    ) + product_nt(left_high, right_high)


def split(x):
    high = x.astype(jnp.bfloat16)
    return high, (x - high.astype(jnp.float32)).astype(jnp.bfloat16)


def product_nt(a, b):
    return lax.dot_general(a, b, (((1,), (1,)), ((), ())), preferred_element_type=jnp.float32)


def place_beams(group, groups, beam_refs, b_ref):
    own, below, below2, above, above2, low, high = beam_refs
    share = own.shape[0]
    half = share // 2

    def put(by, at, values):
        owner = lax.rem(group + (by + groups), groups)
        first = pl.multiple_of(owner * share + at, 8)
        b_ref[pl.ds(first, values.shape[0]), :] = values

    put(0, 0, own[...])
    put(1, 0, above[...])
    put(2, 0, above2[...])
    put(3, 0, low[:share, :])
    put(4, 0, low[share:, :])
    put(4, half, high[share:, :])
    put(-3, 0, high[:share, :])
    put(-2, 0, below2[...])
    put(-1, 0, below[...])


def whitened_rows(group, packed, *beams):
    share, n = beams[0].shape
    groups = packed.shape[0]
    return pl.pallas_call(
        factor_body,
        out_shape=jax.ShapeDtypeStruct((n // groups, groups * share), jnp.float32),
        in_specs=[SMEM] + [VMEM] * 8,
        out_specs=VMEM,
        scratch_shapes=[
            pltpu.VMEM((n, n), jnp.float32),
            pltpu.VMEM((TILE, TILE), jnp.float32),
            pltpu.VMEM((n, n), jnp.float32),
            pltpu.VMEM((groups * share, n), jnp.float32),
        ],
        compiler_params=pltpu.CompilerParams(vmem_limit_bytes=14 << 20),
        cost_estimate=pl.CostEstimate(flops=12 * n**3, bytes_accessed=1 << 20, transcendentals=n),
        name="whitened_rows",
    )(group, packed, *beams)


def local(samples, taps_weight, retain):
    row_count = samples.shape[0]
    groups, blocks = (lax.axis_size("elem"), lax.axis_size("tm"))
    group = lax.axis_index("elem").reshape(1).astype(jnp.int32)
    share = row_count // groups
    half = share // 2
    with jax.named_scope("halo"):
        halo = shifted(samples[row_count - LEAD :], "tm", 1)
    args = (group, halo, samples, taps_weight, retain)
    down, up, far_down, far_up = fir(
        (-1, -3, 1, 3, 4), (2 * share, 2 * share, half, half), False, *args
    )
    with jax.named_scope("beams_near"):
        down, up = (ring(down, -1), ring(up, 1))
        far_down, far_up = (ring(far_down, -2), ring(far_up, 2))
    keep, weight, stats = fir((0, -2, 2), (3 * share,), True, *args)
    low, high = relay_sums(keep, down, up, far_down, far_up)
    with jax.named_scope("beams_far"):
        low, high = (ring(low, -2), ring(high, 2))
    my_beams, packed = packed_gram(keep, down, up, low, high, weight)
    with jax.named_scope("gram_sum"):
        parts = lax.all_to_all(
            packed.reshape(groups, packed.shape[0] // groups, TILE), "elem", 0, 0
        )
    spread, own = spread_share(parts, stats, my_beams, blocks)
    with jax.named_scope("beams_gather"):
        below, above = (ring(own, 1), ring(own, -1))
        below2, above2 = (ring(own, 2), ring(own, -2))
    with jax.named_scope("blocks_out"):
        received = lax.all_to_all(spread, "tm", 0, 0, tiled=True)
    estimate, low, high = decayed(received, below, below2, above, above2)
    with jax.named_scope("beams_gather"):
        low, high = (ring(low, -2), ring(high, 2))
    with jax.named_scope("blocks_back"):
        returned = lax.all_to_all(estimate, "tm", 0, 0, tiled=True)
    with jax.named_scope("gram_gather"):
        packed_estimate = lax.all_to_all(
            replicated(returned, groups, low, high), "elem", 0, 0
        )
    return whitened_rows(
        group, packed_estimate, own, below, below2, above, above2, low, high
    )


def solution(mesh):
    placed = (P("tm", "elem"), P(None, "elem", None), P("tm"))
    return jax.shard_map(
        local, mesh=mesh, in_specs=placed, out_specs=P("elem", "tm"), check_vma=False
    )
```
